32 devices in a mesh: wide: 4 (over z), narrow: 8 (over y, x, core).
Axes of the slice: x: 2, y: 2, z: 4, core: 2. Of those that a mesh axis runs over, the one named last changes fastest.
Arguments:
- src_design: float32 [5, 4194304], P(None, ('wide', 'narrow')), may hold values from -6 to 6
- att_design: float32 [16, 4194304], P(None, ('wide', 'narrow')), may hold values from -3 to 3
- right_side: float32 [4194304], P(('wide', 'narrow')), may hold values from -6 to 6
- block_source: int32 [65536], P(('wide', 'narrow')), may hold values from 0 to 65535, as said below
- block_segment: int32 [65536], P(('wide', 'narrow')), may hold values from 0 to 8191, as said below
- block_count: int32 [65536], P(('wide', 'narrow')), may hold values from 8 to 64
Outputs:
- sol_src: float32 [5, 65536], P(None, ('wide', 'narrow'))
- sol_att: float32 [16, 8192], P(None, 'narrow')
- dir_src: float32 [5, 65536], P(None, ('wide', 'narrow'))
- dir_att: float32 [16, 8192], P(None, 'narrow')
The draws below stay inside these ranges and needn't reach their ends.
Inputs may be any that keep to these rules, and one draw needn't show every extreme that they name: `block_source`: A block held by the device at index w of wide names a source in [w * 2048 * 8, (w + 1) * 2048 * 8); of the 2048 blocks of one device, exactly 2048 / 8 name sources in [(w * 8 + m) * 2048, (w * 8 + m + 1) * 2048) for each m in 0 to 8 - 1; the lowest and highest source of the partition are named on every device. `block_segment`: A block held by the device at index n of narrow names a segment in [n * 1024, (n + 1) * 1024); the lowest and highest of that range are named on every device.
All inputs are finite; a program needn't handle non-finite values.
Results may differ from the reference program's by a relative error of at most 0.00018.
Values sent between devices are 32-bit elements; how exact they have to be, the bound alone decides.
No kernel may reach another device: no remote copies, remote signals or barrier semaphores. Data moves between devices by JAX's collectives and lax.ppermute only.
A program may use at most 192 MiB of HBM per device.

```python
import jax
import jax.numpy as jnp
from jax import lax

OBS_BLK = 64
SRC_PAR = 5
ATT_PAR = 16
ITERS = 2
BLK_DEV = 2048
SRC_DEV = 2048
SEG_DEV = 1024
NBLK = 65536
NOBS = 4194304
NSRC = 65536
NSEG = 8192
N_NARROW = 8
DEVICES = 32


def draw_block_source(key, part):
    position = jnp.arange(NBLK, dtype=jnp.int32)
    device = position // BLK_DEV
    spot = (position % BLK_DEV).reshape(DEVICES, BLK_DEV)
    slot_cap = BLK_DEV // N_NARROW
    scores = jax.random.randint(jax.random.fold_in(key, 3), (DEVICES, BLK_DEV), 0, 32768, dtype=jnp.int32) * BLK_DEV + spot
    ranks = jnp.argsort(jnp.argsort(scores, axis=1, stable=True), axis=1, stable=True).astype(jnp.int32).reshape(NBLK)
    owner = ranks // slot_cap
    local_ids = jax.random.randint(key, (NBLK,), 0, SRC_DEV, dtype=jnp.int32)
    local_ids = jnp.where(ranks == 0, 0, jnp.where(ranks == BLK_DEV - 1, SRC_DEV - 1, local_ids))
    group_size = SRC_DEV * N_NARROW
    return (device // N_NARROW * group_size + owner * SRC_DEV + local_ids).astype(jnp.int32)


def draw_block_segment(key, part):
    position = jnp.arange(NBLK, dtype=jnp.int32)
    device = position // BLK_DEV
    spot = position % BLK_DEV
    local_ids = jax.random.randint(jax.random.fold_in(key, 7), (NBLK,), 0, SEG_DEV, dtype=jnp.int32)
    local_ids = jnp.where(spot == 0, SEG_DEV - 1, jnp.where(spot == 1, 0, local_ids))
    return (device % N_NARROW * SEG_DEV + local_ids).astype(jnp.int32)


def with_ends(values, key, least, largest):
    extent = values.shape
    index_at = [jax.random.randint(jax.random.fold_in(key, axis), (), 0, extent[axis]) for axis in range(len(extent))]
    values = values.at[tuple(index_at)].set(least)
    longest = extent.index(max(extent))
    index_at[longest] = (index_at[longest] + 1) % extent[longest]
    return values.at[tuple(index_at)].set(largest)


def block_scale(own_key, dims, shards, least, largest):
    factor_of = 1.0
    for dim, shards_of in shards:
        draws = jax.random.uniform(jax.random.fold_in(jax.random.fold_in(own_key, 6), dim), (shards_of,), jnp.float32, least / len(shards), largest / len(shards))
        factor_of = factor_of * jnp.repeat(jnp.exp(draws), dims[dim] // shards_of).reshape((-1,) + (1,) * (len(dims) - 1 - dim))
    return factor_of


def gaussian(own_key, dims, deviation, limit, cuts=(), kind=jnp.bfloat16):
    drawn = jax.random.normal(own_key, dims, jnp.float32) * deviation
    if len(cuts) > 0:
        drawn = block_scale(own_key, dims, cuts, -0.22, 0.18) * drawn
    return jnp.clip(drawn, min=-limit, max=limit).astype(kind)


def setup_inputs(seed: int = 0) -> dict:
    key_list = jax.random.split(jax.random.key(seed), 7)
    src_design = gaussian(key_list[0], (SRC_PAR, NOBS), 1.0, 6.0, ((1, 32),), jnp.float32)
    att_design = gaussian(key_list[1], (ATT_PAR, NOBS), 0.5, 3.0, ((1, 32),), jnp.float32)
    right_side = gaussian(key_list[2], (NOBS,), 1.0, 6.0, ((0, 32),), jnp.float32)
    block_source = draw_block_source(jax.random.fold_in(key_list[6], 71), 0)
    block_segment = draw_block_segment(jax.random.fold_in(key_list[6], 71), 0)
    block_count = with_ends(jax.random.randint(key_list[5], (NBLK,), 8, 65), jax.random.fold_in(key_list[5], 1), 8, 64).astype(jnp.int32)
    return dict(src_design=src_design, att_design=att_design, right_side=right_side, block_source=block_source, block_segment=block_segment, block_count=block_count)


def apply_forward(src_vec, att_vec, src_blocks, att_blocks, src_index, seg_index, live_rows):
    src_vals = jnp.take(src_vec, src_index, axis=1)
    att_vals = jnp.take(att_vec, seg_index, axis=1)
    image = lax.optimization_barrier(jnp.sum(src_blocks * src_vals[:, :, None], axis=0))
    image = image + lax.optimization_barrier(jnp.sum(att_blocks * att_vals[:, :, None], axis=0))
    return image * live_rows

def apply_transposed(obs_vec, src_blocks, att_blocks, src_index, seg_index, src_count, seg_count):
    src_part = lax.optimization_barrier(jnp.sum(src_blocks * obs_vec[None], axis=2))
    att_part = lax.optimization_barrier(jnp.sum(att_blocks * obs_vec[None], axis=2))
    src_total = jnp.zeros((src_blocks.shape[0], src_count), src_part.dtype).at[:, src_index].add(src_part)
    att_total = jnp.zeros((att_blocks.shape[0], seg_count), att_part.dtype).at[:, seg_index].add(att_part)
    return (src_total, att_total)

def reference(src_design, att_design, right_side, block_source, block_segment, block_count):
    block_total = block_source.shape[0]
    src_blocks = src_design.reshape(SRC_PAR, block_total, OBS_BLK)
    att_blocks = att_design.reshape(ATT_PAR, block_total, OBS_BLK)
    live_rows = (jnp.arange(OBS_BLK, dtype=jnp.int32)[None, :] < block_count[:, None]).astype(src_design.dtype)
    obs_vec = right_side.reshape(block_total, OBS_BLK) * live_rows
    beta_norm = jnp.sqrt(jnp.sum(obs_vec * obs_vec))
    obs_vec = obs_vec / beta_norm
    src_vec, att_vec = apply_transposed(obs_vec, src_blocks, att_blocks, block_source, block_segment, NSRC, NSEG)
    alpha_norm = jnp.sqrt(jnp.sum(src_vec * src_vec) + jnp.sum(att_vec * att_vec))
    src_vec = src_vec / alpha_norm
    att_vec = att_vec / alpha_norm
    dir_src, dir_att = (src_vec, att_vec)
    sol_src = jnp.zeros_like(src_vec)
    sol_att = jnp.zeros_like(att_vec)
    phi_bar = beta_norm
    rho_bar = alpha_norm
    for step in range(ITERS):
        obs_vec = apply_forward(src_vec, att_vec, src_blocks, att_blocks, block_source, block_segment, live_rows) - alpha_norm * obs_vec
        beta_norm = jnp.sqrt(jnp.sum(obs_vec * obs_vec))
        obs_vec = obs_vec / beta_norm
        back_src, back_att = apply_transposed(obs_vec, src_blocks, att_blocks, block_source, block_segment, NSRC, NSEG)
        src_vec = back_src - beta_norm * src_vec
        att_vec = back_att - beta_norm * att_vec
        alpha_norm = jnp.sqrt(jnp.sum(src_vec * src_vec) + jnp.sum(att_vec * att_vec))
        src_vec = src_vec / alpha_norm
        att_vec = att_vec / alpha_norm
        rho_val = jnp.sqrt(rho_bar * rho_bar + beta_norm * beta_norm)
        cosine = rho_bar / rho_val
        sine_part = beta_norm / rho_val
        theta_val = sine_part * alpha_norm
        rho_bar = -cosine * alpha_norm
        phi_val = cosine * phi_bar
        phi_bar = sine_part * phi_bar
        sol_src = sol_src + phi_val / rho_val * dir_src
        sol_att = sol_att + phi_val / rho_val * dir_att
        dir_src = src_vec - theta_val / rho_val * dir_src
        dir_att = att_vec - theta_val / rho_val * dir_att
    return (sol_src, sol_att, dir_src, dir_att)
```

```python
import functools

import jax
import jax.numpy as jnp
from jax import lax
from jax.experimental import pallas as pl
from jax.experimental.pallas import tpu as pltpu
from jax.sharding import PartitionSpec as P

SRC_DEV = 2048
SEG_DEV = 1024
LANE = 128
HIGH = 256
F32 = jnp.float32
BF16 = jnp.bfloat16
I32 = jnp.int32
MIB = 1 << 20


def lanes_of(values, index):
    return jnp.take_along_axis(values, index, axis=1, mode="promise_in_bounds")


def row_iota(rows, columns=LANE):
    return lax.broadcasted_iota(I32, (rows, columns), 0)


def lane_iota(rows, columns=LANE):
    return lax.broadcasted_iota(I32, (rows, columns), 1)


def to_tiles(rows):
    count = rows.shape[0]
    lane = lane_iota(count)
    first = lanes_of(rows, (2 * lane) % LANE)
    second = lanes_of(rows, (2 * lane + 1) % LANE)
    head = lane < LANE // 2
    even = jnp.where(head, first, pltpu.roll(first, count - 1, 0))
    odd = jnp.where(head, pltpu.roll(second, 1, 0), second)
    return jnp.where(row_iota(count) % 2 == 0, even, odd)


def split_three(values):
    top = values.astype(BF16).astype(F32)
    rest = values - top
    middle = rest.astype(BF16).astype(F32)
    return top, middle, rest - middle


def dot_lanes(left, right):
    return lax.dot_general(left, right, (((1,), (1,)), ((), ())), preferred_element_type=F32)


def spread_rows(store, picked, row, column, levels):
    rows = picked.shape[0]
    for part, piece in enumerate(split_three(picked)):
        for level in range(levels):
            at = (part * levels + level) * rows
            kept = jnp.where(row == level, piece, 0.0)
            store[pl.ds(at, rows), pl.ds(column, LANE)] = kept.astype(BF16)


def index_kernel(narrow, source_ref, segment_ref, pos_ref, seg_ref, order_ref, ids_ref, left, right):
    tiles = source_ref.shape[0]
    cap = tiles * LANE // narrow
    local = to_tiles(source_ref[...]) & (SRC_DEV * narrow - 1)
    seg_ref[...] = to_tiles(segment_ref[...]) & (SEG_DEV - 1)
    owner = local // SRC_DEV
    inner = local & (SRC_DEV - 1)
    marks = jnp.concatenate([jnp.where(owner == m, 1.0, 0.0) for m in range(narrow)], axis=0)
    marks = marks.astype(BF16)
    total = narrow * tiles
    before = jnp.where(row_iota(LANE) < lane_iota(LANE), 1.0, 0.0).astype(BF16)
    in_row = jnp.dot(marks, before, preferred_element_type=F32)
    at_row, at_lane = row_iota(total, total), lane_iota(total, total)
    earlier = (at_row // tiles == at_lane // tiles) & (at_lane < at_row)
    ahead = jnp.dot(jnp.where(earlier, 1.0, 0.0).astype(BF16), marks, preferred_element_type=F32)
    ahead = jnp.dot(ahead.astype(BF16), jnp.ones((LANE, LANE), BF16), preferred_element_type=F32)
    rank = (in_row + ahead).astype(I32)
    pos = jnp.zeros((tiles, LANE), I32)
    for m in range(narrow):
        pos = jnp.where(owner == m, m * cap + rank[m * tiles : (m + 1) * tiles], pos)
    pos_ref[...] = pos
    levels = tiles * LANE // HIGH
    high_at = row_iota(HIGH)
    lane = lane_iota(1).astype(F32)
    for t in range(tiles):
        here = pos[t : t + 1]
        level = row_iota(levels) == here // HIGH
        mine = inner[t : t + 1]
        pieces = (
            jnp.full((1, LANE), float(t), F32),
            lane,
            (mine // LANE).astype(F32),
            (mine % LANE).astype(F32),
        )
        for part, piece in enumerate(pieces):
            left[part * levels : (part + 1) * levels, t * LANE : (t + 1) * LANE] = jnp.where(
                level, piece, 0.0
            ).astype(BF16)
        right[:, t * LANE : (t + 1) * LANE] = jnp.where(high_at == here % HIGH, 1.0, 0.0).astype(
            BF16
        )
    found = dot_lanes(left[...], right[...])
    tile_at, lane_at = found[:levels], found[levels : 2 * levels]
    order = (tile_at * LANE + lane_at).astype(I32)
    ids = found[2 * levels : 3 * levels] * LANE + found[3 * levels :]
    for level in range(levels):
        for half in range(HIGH // LANE):
            row = level * (HIGH // LANE) + half
            cut = slice(half * LANE, (half + 1) * LANE)
            order_ref[row : row + 1, :] = order[level : level + 1, cut]
            ids_ref[row : row + 1, :] = ids[level : level + 1, cut]


def scatter_att(blocks, seg_ref, out_ref, left, right):
    tiles = seg_ref.shape[0]
    levels = SEG_DEV // HIGH
    high_at = row_iota(HIGH)

    def fill(t, carry):
        here = seg_ref[pl.ds(t, 1), :]
        column = pl.multiple_of(t * LANE, LANE)
        spread_rows(left, blocks[t, 0:16, :], here // HIGH, column, levels)
        right[:, pl.ds(column, LANE)] = jnp.where(high_at == here % HIGH, 1.0, 0.0).astype(BF16)
        return carry

    lax.fori_loop(0, tiles, fill, 0)
    sums = dot_lanes(left[...], right[...])
    size = 16 * levels
    sums = sums[:size] + (sums[size : 2 * size] + sums[2 * size :])
    for level in range(levels):
        out_ref[:, level * HIGH : (level + 1) * HIGH] = sums[level * 16 : (level + 1) * 16]


def pick(tables, count, index):
    low = index & (LANE - 1)
    high = index // LANE
    rows = tables(0).shape[0]
    low = jnp.broadcast_to(low, (rows, LANE))
    out = lanes_of(tables(0), low)
    for c in range(1, count):
        out = jnp.where(high == c, lanes_of(tables(c), low), out)
    return out


def send_sorted(narrow, blocks, order_ref, extra, out_ref):
    tiles = order_ref.shape[0]
    cap = tiles * LANE // narrow
    per = cap // LANE
    keep = row_iota(8) < 5
    for t in range(tiles):
        values = pick(lambda c: blocks[c, 16:24, :], tiles, order_ref[t : t + 1, :])
        values = jnp.where(keep, values, extra(t))
        out_ref[t // per, :, (t % per) * LANE : (t % per + 1) * LANE] = values


def entry(ref, per, t):
    return ref[t // per, :, (t % per) * LANE : (t % per + 1) * LANE]


def start_kernel(att_ref, src_ref, rhs_ref, count_ref, table_ref, first_ref, square_ref, counts):
    step = pl.program_id(0)

    @pl.when(step == 0)
    def _():
        counts[...] = to_tiles(count_ref[...])
        square_ref[...] = jnp.zeros_like(square_ref)

    wide_rhs = rhs_ref[...].T
    place = row_iota(64)
    live, obs = [], []
    for half in range(2):
        alive = place < counts[pl.ds(step * 2 + half, 1), :]
        live.append(alive)
        part = jnp.where(alive, wide_rhs[half * 64 : half * 64 + 64], 0.0)
        obs.append(part)
        square = part * part
        total = square[0:8]
        for at in range(8, 64, 8):
            total = total + square[at : at + 8]
        square_ref[...] += total
    att_rows = 16
    for i in range(att_rows + src_ref.shape[1]):
        if i < att_rows:
            values = att_ref[i // 8, :, i % 8, :]
        else:
            values = src_ref[:, i - att_rows, :]
        turned = values.T
        for half in range(2):
            part = jnp.where(live[half], turned[half * 64 : half * 64 + 64], 0.0)
            table_ref[half, i] = part
            first_ref[half, i : i + 1, :] = jnp.sum(part * obs[half], axis=0, keepdims=True)
    for half in range(2):
        first_ref[half, 21:24, :] = jnp.zeros((3, LANE), F32)


def first_send_kernel(
    narrow, blocks, seg_ref, order_ref, ids_ref, square_ref, att_ref, send_ref, left, right
):
    scatter_att(blocks, seg_ref, att_ref, left, right)
    lane = lane_iota(16)
    att_ref[:, SEG_DEV:] = jnp.where(lane == 0, jnp.sum(square_ref[...]), 0.0)
    row = row_iota(8)
    send_sorted(
        narrow,
        blocks,
        order_ref,
        lambda t: jnp.where(row == 5, ids_ref[t : t + 1, :], 0.0),
        send_ref,
    )


def owner_kernel(
    narrow, first, recv_ref, half_ref, other_ref, given_ref, src_ref, back_ref, att_ref, out_ref,
    left, right,
):
    tiles, cap = given_ref.shape[0], recv_ref.shape[2]
    per = cap // LANE
    levels = SRC_DEV // HIGH
    high_at = row_iota(HIGH)
    keep = row_iota(8) < 5
    att_ref[...] = half_ref[...] + other_ref[...]
    if first:
        for t in range(tiles):
            out_ref[t : t + 1, :] = entry(recv_ref, per, t)[5:6].astype(I32)
        index_ref = out_ref
    else:
        index_ref = given_ref
        known = recv_ref[0, :, 0:LANE]
        for n in range(1, narrow):
            known = known + recv_ref[n, :, 0:LANE]
        out_ref[...] = known
    for t in range(tiles):
        here = index_ref[t : t + 1, :]
        values = jnp.where(keep, entry(recv_ref, per, t), 0.0)
        spread_rows(left, values, here // HIGH, t * LANE, levels)
        right[:, t * LANE : (t + 1) * LANE] = jnp.where(high_at == here % HIGH, 1.0, 0.0).astype(
            BF16
        )
    sums = dot_lanes(left[...], right[...])
    size = 8 * levels
    sums = sums[:size] + (sums[size : 2 * size] + sums[2 * size :])
    for level in range(levels):
        src_ref[:, level * HIGH : (level + 1) * HIGH] = sums[level * 8 : (level + 1) * 8]
    if back_ref is None:
        return
    square = jnp.sum(src_ref[...] * src_ref[...]) if first else 0.0
    mark = jnp.where((row_iota(8) == 6) & (lane_iota(8) == 0), square, 0.0)
    for t in range(tiles):
        values = pick(
            lambda c: src_ref[:, c * LANE : (c + 1) * LANE],
            SRC_DEV // LANE,
            index_ref[t : t + 1, :],
        )
        values = jnp.where(keep, values, mark)
        back_ref[t // per, :, (t % per) * LANE : (t % per + 1) * LANE] = values


def lane_value(row, at):
    return jnp.sum(jnp.where(lane_iota(1) == at, row, 0.0), axis=1, keepdims=True)


def product_kernel(
    narrow, first, recv_ref, half_ref, other_ref, known_ref, pos_ref, seg_ref, order_ref, table_ref,
    full_ref, att_ref, send_ref, scale_ref, vec, blocks, left, right, held, sems,
):
    tiles, rows = pos_ref.shape[0], held.shape[1]
    cap = recv_ref.shape[2]
    per = cap // LANE

    def copy(t):
        return pltpu.make_async_copy(table_ref.at[t], held.at[t], sems.at[t])

    def begin(t, carry):
        copy(t).start()
        return carry

    lax.fori_loop(0, tiles, begin, 0)
    full = half_ref[...] + other_ref[...]
    full_ref[...] = full[:, :SEG_DEV]
    notes = full[0:1, SEG_DEV:]
    if first:
        scale = jnp.ones((1, 1), F32)
        square_src = recv_ref[0, 6:7, 0:LANE]
        for n in range(1, narrow):
            square_src = square_src + recv_ref[n, 6:7, 0:LANE]
        square_src = lane_value(square_src, 0)
        square_att = jnp.sum(full[:, :SEG_DEV] * full[:, :SEG_DEV], keepdims=True)
        rhs_square = lane_value(notes, 0)
        att_note = jnp.where(lane_iota(16) == 1, square_src, 0.0)
        send_note = jnp.where(
            row_iota(8) == 6,
            jnp.where(lane_iota(8) == 0, rhs_square, jnp.where(lane_iota(8) == 1, square_att, 0.0)),
            0.0,
        )
    else:
        known = known_ref[6:7, :]
        square = lane_value(notes, 1) + lane_value(known, 1)
        scale = lane_value(known, 0) / square
        att_note = jnp.zeros((16, LANE), F32)
        send_note = jnp.zeros((8, LANE), F32)
    scale_ref[...] = jnp.broadcast_to(scale, (8, LANE))

    def gather(t, carry):
        where_src = pos_ref[pl.ds(t, 1), :]
        where_att = seg_ref[pl.ds(t, 1), :]
        for top in range(0, 16, 8):
            picked = pick(
                lambda c: full_ref[top : top + 8, c * LANE : (c + 1) * LANE],
                SEG_DEV // LANE,
                where_att,
            )
            vec[t, top : top + 8, :] = picked * scale
        vec[t, 16:24, :] = pick(lambda c: entry(recv_ref, per, c), tiles, where_src) * scale
        return carry

    lax.fori_loop(0, tiles, gather, 0)

    def multiply(t, carry):
        copy(t).wait()
        image = held[t, 0] * vec[t, 0:1, :]
        for i in range(1, rows):
            image = image + held[t, i] * vec[t, i : i + 1, :]
        for i in range(rows):
            blocks[t, i : i + 1, :] = jnp.sum(held[t, i] * image, axis=0, keepdims=True)
        blocks[t, rows:24, :] = jnp.zeros((24 - rows, LANE), F32)
        return carry

    lax.fori_loop(0, tiles, multiply, 0)
    scatter_att(blocks, seg_ref, att_ref, left, right)
    att_ref[:, SEG_DEV:] = att_note
    send_sorted(narrow, blocks, order_ref, lambda t: send_note, send_ref)


def dots_kernel(
    src0, src1, src2, att0, att1, att2a, att2b, square_ref, scale_ref, weight_ref, out_ref, att2
):
    att2[...] = (att2a[...] + att2b[...])[:, :SEG_DEV]
    scale = scale_ref[0:1, 0:1]
    weight = weight_ref[0:1, 0:1]
    src = (src0[...], src1[...] * scale, src2[...] * scale)
    att = (att0[...], att1[...] * scale, att2[...] * scale)
    out = jnp.where(lane_iota(1) == 0, jnp.sum(square_ref[...], keepdims=True), 0.0)
    for at, (one, two) in enumerate(((0, 0), (0, 1), (1, 1), (1, 2), (2, 2))):
        total = jnp.sum(src[one] * src[two], keepdims=True)
        total = total + weight * jnp.sum(att[one] * att[two], keepdims=True)
        out = jnp.where(lane_iota(1) == at + 1, total, out)
    out_ref[...] = jnp.broadcast_to(out, out_ref.shape)


def finish_kernel(
    dots_ref, scale_ref, src0, src1, src2, att0, att1, att2, sol_src, sol_att, dir_src, dir_att
):
    sums = jnp.sum(dots_ref[...], axis=0, keepdims=True)
    rhs_square, m0, m1, m2, m3, m4 = [lane_value(sums, at) for at in range(6)]
    scale = scale_ref[0:1, 0:1]
    mean = m1 / m0
    ww = m2 - mean * m1
    wz = m3 - 2.0 * mean * m2 + mean * mean * m1
    zz = m4 - 2.0 * mean * m3 + mean * mean * m2
    root0, root1 = jnp.sqrt(m0), jnp.sqrt(ww)
    beta1 = jnp.sqrt(rhs_square)
    alpha1 = root0 / beta1
    beta2 = jnp.sqrt(mean / scale - alpha1 * alpha1)
    cross = root1 / (scale * root0)
    alpha2 = cross / beta2
    quotient = wz / ww / scale
    beta3 = jnp.sqrt(quotient - alpha2 * alpha2)
    third = zz / ww / (scale * scale) - quotient * quotient - cross * cross
    alpha3 = jnp.sqrt(third) / beta3
    phi_bar, rho_bar = beta1, alpha1
    steps, turns = [], []
    for beta, alpha in ((beta2, alpha2), (beta3, alpha3)):
        rho = jnp.sqrt(rho_bar * rho_bar + beta * beta)
        cosine, sine = rho_bar / rho, beta / rho
        theta = sine * alpha
        rho_bar = -cosine * alpha
        steps.append(cosine * phi_bar / rho)
        turns.append(theta / rho)
        phi_bar = sine * phi_bar
    sides = (
        (src0, src1, src2, sol_src, dir_src),
        (att0, att1, att2, sol_att, dir_att),
    )
    for zero, one, two, sol, direction in sides:
        rows = sol.shape[0]
        base, once, twice = zero[0:rows], one[0:rows] * scale, two[0:rows] * scale
        v1 = base / root0
        v2 = (once - mean * base) / root1
        v3 = ((twice - mean * once) / (scale * root1) - quotient * v2 - cross * v1) / (
            beta3 * alpha3
        )
        turned = v2 - turns[0] * v1
        sol[...] = steps[0] * v1 + steps[1] * turned
        direction[...] = v3 - turns[1] * turned


def sds(shape, dtype=F32):
    return jax.ShapeDtypeStruct(shape, dtype)


def call(kernel, outs, scratch=(), limit=24, **more):
    return pl.pallas_call(
        kernel,
        out_shape=outs,
        scratch_shapes=list(scratch),
        compiler_params=pltpu.CompilerParams(vmem_limit_bytes=limit * MIB),
        **more,
    )


def on_device(src_design, att_design, right_side, block_source, block_segment, block_count):
    narrow, wide = lax.axis_size("narrow"), lax.axis_size("wide")
    devices = narrow * wide
    blocks = block_source.shape[0]
    tiles = blocks // LANE
    cap = blocks // narrow
    src_rows, att_rows = src_design.shape[0], att_design.shape[0]
    rows = src_rows + att_rows
    columns = right_side.shape[0] // LANE
    groups = columns // LANE
    obs = right_side.shape[0] // blocks

    def across(values, step):
        return lax.ppermute(values, "wide", [(i, i ^ step) for i in range(wide)])

    def exchange(values):
        return lax.all_to_all(values, "narrow", 0, 0)

    tile_rows = lambda values: values.reshape(tiles, LANE)
    att_view = att_design.reshape(att_rows // 8, 8, columns, LANE).transpose(0, 2, 1, 3)
    src_view = src_design.reshape(src_rows, columns, LANE).transpose(1, 0, 2)

    table, first, square = call(
        start_kernel,
        (sds((tiles, rows, obs, LANE)), sds((tiles, 24, LANE)), sds((8, LANE))),
        [pltpu.VMEM((tiles, LANE), I32)],
        grid=(groups,),
        in_specs=[
            pl.BlockSpec((att_rows // 8, LANE, 8, LANE), lambda g: (0, g, 0, 0)),
            pl.BlockSpec((LANE, src_rows, LANE), lambda g: (g, 0, 0)),
            pl.BlockSpec((LANE, LANE), lambda g: (g, 0)),
            pl.BlockSpec((tiles, LANE), lambda g: (0, 0)),
        ],
        out_specs=(
            pl.BlockSpec((2, rows, obs, LANE), lambda g: (g, 0, 0, 0)),
            pl.BlockSpec((2, 24, LANE), lambda g: (g, 0, 0)),
            pl.BlockSpec((8, LANE), lambda g: (0, 0)),
        ),
    )(att_view, src_view, right_side.reshape(columns, LANE), tile_rows(block_count))

    right_store = pltpu.VMEM((HIGH, blocks), BF16)
    att_left = pltpu.VMEM((3 * 16 * SEG_DEV // HIGH, blocks), BF16)
    src_left = pltpu.VMEM((3 * 8 * SRC_DEV // HIGH, blocks), BF16)
    tile_int = sds((tiles, LANE), I32)
    pos, seg, order, ids = call(
        functools.partial(index_kernel, narrow),
        (tile_int, tile_int, tile_int, sds((tiles, LANE))),
        [pltpu.VMEM((4 * blocks // HIGH, blocks), BF16), right_store],
    )(tile_rows(block_source), tile_rows(block_segment))

    send_shape = sds((narrow, 8, cap))
    att_shape = sds((16, SEG_DEV + LANE))
    src_shape = sds((8, SRC_DEV))
    part, send = call(
        functools.partial(first_send_kernel, narrow),
        (att_shape, send_shape),
        [att_left, right_store],
    )(first, seg, order, ids, square)

    given = ids_known = None
    results = []
    scale = None
    for step in range(3):
        other = across(part, 1)
        arrived = exchange(send)
        first_time = step == 0
        last_time = step == 2
        outs = [src_shape]
        if not last_time:
            outs.append(send_shape)
        outs.append(att_shape)
        outs.append(tile_int if first_time else sds((8, LANE)))
        kernel = functools.partial(owner_kernel, narrow, first_time)
        if last_time:
            whole = lambda *refs, k=kernel: k(*refs[:5], None, *refs[5:])
        else:
            whole = kernel
        given_in = seg if first_time else given
        made = call(whole, tuple(outs), [src_left, right_store])(arrived, part, other, given_in)
        src_sum, half, note = made[0], made[-2], made[-1]
        if first_time:
            given = note
            note = jnp.zeros((8, LANE), F32)
        later = None
        total = half
        jump = 2
        while jump < wide:
            if later is not None:
                total = total + later
            later = across(total, jump)
            jump *= 2
        if later is None:
            later = jnp.zeros_like(total)
        if last_time:
            results.append((src_sum, total, later))
            break
        back = exchange(made[1])
        att_sum, part, send, scale = call(
            functools.partial(product_kernel, narrow, first_time),
            (sds((16, SEG_DEV)), att_shape, send_shape, sds((8, LANE))),
            [
                pltpu.VMEM((tiles, 24, LANE), F32),
                pltpu.VMEM((tiles, 24, LANE), F32),
                att_left,
                right_store,
                pltpu.VMEM((tiles, rows, obs, LANE), F32),
                pltpu.SemaphoreType.DMA((tiles,)),
            ],
            in_specs=[pl.BlockSpec(memory_space=pltpu.VMEM)] * 7
            + [pl.BlockSpec(memory_space=pl.ANY)],
        )(back, total, later, note, pos, seg, order, table)
        results.append((src_sum, att_sum))

    weight = jnp.where(lax.axis_index("wide") == 0, 1.0, 0.0).astype(F32) * jnp.ones((8, LANE), F32)
    (src0, att0), (src1, att1), (src2, att2a, att2b) = results
    dots, att2 = call(dots_kernel, (sds((devices, LANE)), sds((16, SEG_DEV))))(
        src0, src1, src2, att0, att1, att2a, att2b, square, scale, weight
    )
    dots = lax.all_to_all(dots, ("wide", "narrow"), 0, 0, tiled=True)
    sol_src, sol_att, dir_src, dir_att = call(
        finish_kernel,
        (
            sds((src_rows, SRC_DEV)),
            sds((att_rows, SEG_DEV)),
            sds((src_rows, SRC_DEV)),
            sds((att_rows, SEG_DEV)),
        ),
    )(dots, scale, src0, src1, src2, att0, att1, att2)
    return (sol_src, sol_att, dir_src, dir_att)


def solution(mesh):
    both = ("wide", "narrow")
    in_specs = (P(None, both), P(None, both), P(both), P(both), P(both), P(both))
    out_specs = (P(None, both), P(None, "narrow"), P(None, both), P(None, "narrow"))
    return jax.shard_map(
        on_device, mesh=mesh, in_specs=in_specs, out_specs=out_specs, check_vma=False
    )
```

```python
import functools

import jax
import jax.numpy as jnp
from jax import lax
from jax.experimental import pallas as pl
from jax.experimental.pallas import tpu as pltpu
from jax.sharding import PartitionSpec as P

SRC_DEV = 2048
SEG_DEV = 1024
LANE = 128
HIGH = 256
F32 = jnp.float32
BF16 = jnp.bfloat16
I32 = jnp.int32
MIB = 1 << 20


def lanes_of(values, index):
    return jnp.take_along_axis(values, index, axis=1, mode="promise_in_bounds")


def row_iota(rows, columns=LANE):
    return lax.broadcasted_iota(I32, (rows, columns), 0)


def lane_iota(rows, columns=LANE):
    return lax.broadcasted_iota(I32, (rows, columns), 1)


def to_tiles(rows):
    count = rows.shape[0]
    lane = lane_iota(count)
    first = lanes_of(rows, (2 * lane) % LANE)
    second = lanes_of(rows, (2 * lane + 1) % LANE)
    head = lane < LANE // 2
    even = jnp.where(head, first, pltpu.roll(first, count - 1, 0))
    odd = jnp.where(head, pltpu.roll(second, 1, 0), second)
    return jnp.where(row_iota(count) % 2 == 0, even, odd)


def split_three(values):
    top = values.astype(BF16).astype(F32)
    rest = values - top
    middle = rest.astype(BF16).astype(F32)
    return top, middle, rest - middle


def dot_lanes(left, right):
    return lax.dot_general(left, right, (((1,), (1,)), ((), ())), preferred_element_type=F32)


def spread_rows(store, picked, row, column, levels):
    rows = picked.shape[0]
    for part, piece in enumerate(split_three(picked)):
        for level in range(levels):
            at = (part * levels + level) * rows
            kept = jnp.where(row == level, piece, 0.0)
            store[pl.ds(at, rows), pl.ds(column, LANE)] = kept.astype(BF16)


def rank_blocks(narrow, source_ref, segment_ref, pos_ref, seg_ref, order_ref, ids_ref, left, right):
    tiles = source_ref.shape[0]
    cap = tiles * LANE // narrow
    local = to_tiles(source_ref[...]) & (SRC_DEV * narrow - 1)
    seg_ref[...] = to_tiles(segment_ref[...]) & (SEG_DEV - 1)
    owner = local // SRC_DEV
    inner = local & (SRC_DEV - 1)
    marks = jnp.concatenate([jnp.where(owner == m, 1.0, 0.0) for m in range(narrow)], axis=0)
    marks = marks.astype(BF16)
    total = narrow * tiles
    before = jnp.where(row_iota(LANE) < lane_iota(LANE), 1.0, 0.0).astype(BF16)
    in_row = jnp.dot(marks, before, preferred_element_type=F32)
    at_row, at_lane = row_iota(total, total), lane_iota(total, total)
    earlier = (at_row // tiles == at_lane // tiles) & (at_lane < at_row)
    ahead = jnp.dot(jnp.where(earlier, 1.0, 0.0).astype(BF16), marks, preferred_element_type=F32)
    ahead = jnp.dot(ahead.astype(BF16), jnp.ones((LANE, LANE), BF16), preferred_element_type=F32)
    rank = (in_row + ahead).astype(I32)
    pos = jnp.zeros((tiles, LANE), I32)
    for m in range(narrow):
        pos = jnp.where(owner == m, m * cap + rank[m * tiles : (m + 1) * tiles], pos)
    pos_ref[...] = pos
    levels = tiles * LANE // HIGH
    high_at = row_iota(HIGH)
    lane = lane_iota(1).astype(F32)
    for t in range(tiles):
        here = pos[t : t + 1]
        level = row_iota(levels) == here // HIGH
        mine = inner[t : t + 1]
        pieces = (
            jnp.full((1, LANE), float(t), F32),
            lane,
            (mine // LANE).astype(F32),
            (mine % LANE).astype(F32),
        )
        for part, piece in enumerate(pieces):
            left[part * levels : (part + 1) * levels, t * LANE : (t + 1) * LANE] = jnp.where(
                level, piece, 0.0
            ).astype(BF16)
        right[:, t * LANE : (t + 1) * LANE] = jnp.where(high_at == here % HIGH, 1.0, 0.0).astype(
            BF16
        )
    found = dot_lanes(left[0 : 4 * levels, :], right[...])
    tile_at, lane_at = found[:levels], found[levels : 2 * levels]
    order = (tile_at * LANE + lane_at).astype(I32)
    ids = found[2 * levels : 3 * levels] * LANE + found[3 * levels :]
    for level in range(levels):
        for half in range(HIGH // LANE):
            row = level * (HIGH // LANE) + half
            cut = slice(half * LANE, (half + 1) * LANE)
            order_ref[row : row + 1, :] = order[level : level + 1, cut]
            ids_ref[row : row + 1, :] = ids[level : level + 1, cut]


def scatter_att(blocks, seg_ref, out_ref, left, right):
    tiles = seg_ref.shape[0]
    levels = SEG_DEV // HIGH
    high_at = row_iota(HIGH)

    def fill(t, carry):
        here = seg_ref[pl.ds(t, 1), :]
        column = pl.multiple_of(t * LANE, LANE)
        spread_rows(left, blocks[t, 0:16, :], here // HIGH, column, levels)
        right[:, pl.ds(column, LANE)] = jnp.where(high_at == here % HIGH, 1.0, 0.0).astype(BF16)
        return carry

    lax.fori_loop(0, tiles, fill, 0)
    sums = dot_lanes(left[...], right[...])
    size = 16 * levels
    sums = sums[:size] + (sums[size : 2 * size] + sums[2 * size :])
    for level in range(levels):
        out_ref[:, level * HIGH : (level + 1) * HIGH] = sums[level * 16 : (level + 1) * 16]


def pick(tables, count, index):
    low = index & (LANE - 1)
    high = index // LANE
    rows = tables(0).shape[0]
    low = jnp.broadcast_to(low, (rows, LANE))
    out = lanes_of(tables(0), low)
    for c in range(1, count):
        out = jnp.where(high == c, lanes_of(tables(c), low), out)
    return out


def send_sorted(narrow, blocks, order_ref, extra, out_ref):
    tiles = order_ref.shape[0]
    cap = tiles * LANE // narrow
    per = cap // LANE
    keep = row_iota(8) < 5
    for t in range(tiles):
        values = pick(lambda c: blocks[c, 16:24, :], tiles, order_ref[t : t + 1, :])
        values = jnp.where(keep, values, extra(t))
        out_ref[t // per, :, (t % per) * LANE : (t % per + 1) * LANE] = values


def entry(ref, per, t):
    return ref[t // per, :, (t % per) * LANE : (t % per + 1) * LANE]


def start_kernel(
    narrow,
    att_hbm, src_hbm, rhs_hbm, source_hbm, segment_hbm, count_hbm,
    table_ref, square_ref, pos_ref, seg_ref, order_ref, att_ref, send_ref,
    att_in, src_in, rhs_in, source_in, segment_in, count_in, blocks, ids, left, right, sems, int_sems,
):
    groups = att_in.shape[0]
    att_rows, src_rows = att_in.shape[1] * att_in.shape[3], src_in.shape[2]
    obs = table_ref.shape[2]

    def ints():
        pairs = ((source_hbm, source_in), (segment_hbm, segment_in), (count_hbm, count_in))
        return [
            pltpu.make_async_copy(one, two, int_sems.at[at]) for at, (one, two) in enumerate(pairs)
        ]

    def loads(g):
        cut = pl.ds(g * LANE, LANE)
        return [
            pltpu.make_async_copy(att_hbm.at[:, cut], att_in.at[g], sems.at[0, g]),
            pltpu.make_async_copy(src_hbm.at[cut], src_in.at[g], sems.at[1, g]),
            pltpu.make_async_copy(rhs_hbm.at[cut], rhs_in.at[g], sems.at[2, g]),
        ]

    def begin(g, carry):
        for one in loads(g):
            one.start()
        return carry

    for one in ints():
        one.start()
    lax.fori_loop(0, groups, begin, 0)
    for one in ints():
        one.wait()
    count_in[...] = to_tiles(count_in[...])
    square_ref[...] = jnp.zeros_like(square_ref)
    rank_blocks(narrow, source_in, segment_in, pos_ref, seg_ref, order_ref, ids, left, right)
    place = row_iota(obs)

    def turn(g, carry):
        for one in loads(g):
            one.wait()
        wide_rhs = rhs_in[g].T
        live, rhs = [], []
        for half in range(2):
            alive = place < count_in[pl.ds(g * 2 + half, 1), :]
            live.append(alive)
            part = jnp.where(alive, wide_rhs[half * obs : half * obs + obs], 0.0)
            rhs.append(part)
            square = part * part
            total = square[0:8]
            for at in range(8, obs, 8):
                total = total + square[at : at + 8]
            square_ref[...] += total
        for i in range(att_rows + src_rows):
            if i < att_rows:
                values = att_in[g, i // 8, :, i % 8, :]
            else:
                values = src_in[g, :, i - att_rows, :]
            turned = values.T
            for half in range(2):
                part = jnp.where(live[half], turned[half * obs : half * obs + obs], 0.0)
                table_ref[g * 2 + half, i] = part
                blocks[g * 2 + half, i : i + 1, :] = jnp.sum(part * rhs[half], axis=0, keepdims=True)
        for half in range(2):
            rest = 24 - att_rows - src_rows
            blocks[g * 2 + half, 24 - rest : 24, :] = jnp.zeros((rest, LANE), F32)
        return carry

    lax.fori_loop(0, groups, turn, 0)
    scatter_att(blocks, seg_ref, att_ref, left, right)
    lane = lane_iota(16)
    att_ref[:, SEG_DEV:] = jnp.where(lane == 0, jnp.sum(square_ref[...]), 0.0)
    row = row_iota(8)
    send_sorted(
        narrow,
        blocks,
        order_ref,
        lambda t: jnp.where(row == 5, ids[t : t + 1, :], 0.0),
        send_ref,
    )


def owner_kernel(
    narrow, first, recv_ref, half_ref, other_ref, given_ref, src_ref, back_ref, att_ref, out_ref,
    left, right,
):
    tiles, cap = given_ref.shape[0], recv_ref.shape[2]
    per = cap // LANE
    levels = SRC_DEV // HIGH
    high_at = row_iota(HIGH)
    keep = row_iota(8) < 5
    att_ref[...] = half_ref[...] + other_ref[...]
    if first:
        for t in range(tiles):
            out_ref[t : t + 1, :] = entry(recv_ref, per, t)[5:6].astype(I32)
        index_ref = out_ref
    else:
        index_ref = given_ref
        known = recv_ref[0, :, 0:LANE]
        for n in range(1, narrow):
            known = known + recv_ref[n, :, 0:LANE]
        out_ref[...] = known
    for t in range(tiles):
        here = index_ref[t : t + 1, :]
        values = jnp.where(keep, entry(recv_ref, per, t), 0.0)
        spread_rows(left, values, here // HIGH, t * LANE, levels)
        right[:, t * LANE : (t + 1) * LANE] = jnp.where(high_at == here % HIGH, 1.0, 0.0).astype(
            BF16
        )
    sums = dot_lanes(left[...], right[...])
    size = 8 * levels
    sums = sums[:size] + (sums[size : 2 * size] + sums[2 * size :])
    for level in range(levels):
        src_ref[:, level * HIGH : (level + 1) * HIGH] = sums[level * 8 : (level + 1) * 8]
    if back_ref is None:
        return
    square = jnp.sum(src_ref[...] * src_ref[...]) if first else 0.0
    mark = jnp.where((row_iota(8) == 6) & (lane_iota(8) == 0), square, 0.0)
    for t in range(tiles):
        values = pick(
            lambda c: src_ref[:, c * LANE : (c + 1) * LANE],
            SRC_DEV // LANE,
            index_ref[t : t + 1, :],
        )
        values = jnp.where(keep, values, mark)
        back_ref[t // per, :, (t % per) * LANE : (t % per + 1) * LANE] = values


def lane_value(row, at):
    return jnp.sum(jnp.where(lane_iota(1) == at, row, 0.0), axis=1, keepdims=True)


def product_kernel(
    narrow, first, recv_ref, half_ref, other_ref, known_ref, pos_ref, seg_ref, order_ref, table_ref,
    full_ref, att_ref, send_ref, scale_ref, vec, blocks, left, right,
):
    tiles, rows = pos_ref.shape[0], table_ref.shape[1]
    cap = recv_ref.shape[2]
    per = cap // LANE

    full = half_ref[...] + other_ref[...]
    full_ref[...] = full[:, :SEG_DEV]
    notes = full[0:1, SEG_DEV:]
    if first:
        scale = jnp.ones((1, 1), F32)
        square_src = recv_ref[0, 6:7, 0:LANE]
        for n in range(1, narrow):
            square_src = square_src + recv_ref[n, 6:7, 0:LANE]
        square_src = lane_value(square_src, 0)
        square_att = jnp.sum(full[:, :SEG_DEV] * full[:, :SEG_DEV], keepdims=True)
        rhs_square = lane_value(notes, 0)
        att_note = jnp.where(lane_iota(16) == 1, square_src, 0.0)
        send_note = jnp.where(
            row_iota(8) == 6,
            jnp.where(lane_iota(8) == 0, rhs_square, jnp.where(lane_iota(8) == 1, square_att, 0.0)),
            0.0,
        )
    else:
        known = known_ref[6:7, :]
        square = lane_value(notes, 1) + lane_value(known, 1)
        scale = lane_value(known, 0) / square
        att_note = jnp.zeros((16, LANE), F32)
        send_note = jnp.zeros((8, LANE), F32)
    scale_ref[...] = jnp.broadcast_to(scale, (8, LANE))

    def gather(t, carry):
        where_src = pos_ref[pl.ds(t, 1), :]
        where_att = seg_ref[pl.ds(t, 1), :]
        for top in range(0, 16, 8):
            picked = pick(
                lambda c: full_ref[top : top + 8, c * LANE : (c + 1) * LANE],
                SEG_DEV // LANE,
                where_att,
            )
            vec[t, top : top + 8, :] = picked * scale
        vec[t, 16:24, :] = pick(lambda c: entry(recv_ref, per, c), tiles, where_src) * scale
        return carry

    lax.fori_loop(0, tiles, gather, 0)

    def multiply(t, carry):
        image = table_ref[t, 0] * vec[t, 0:1, :]
        for i in range(1, rows):
            image = image + table_ref[t, i] * vec[t, i : i + 1, :]
        for i in range(rows):
            blocks[t, i : i + 1, :] = jnp.sum(table_ref[t, i] * image, axis=0, keepdims=True)
        blocks[t, rows:24, :] = jnp.zeros((24 - rows, LANE), F32)
        return carry

    lax.fori_loop(0, tiles, multiply, 0)
    scatter_att(blocks, seg_ref, att_ref, left, right)
    att_ref[:, SEG_DEV:] = att_note
    send_sorted(narrow, blocks, order_ref, lambda t: send_note, send_ref)


def dots_kernel(
    src0, src1, src2, att0, att1, att2a, att2b, square_ref, scale_ref, weight_ref, out_ref, att2
):
    att2[...] = (att2a[...] + att2b[...])[:, :SEG_DEV]
    scale = scale_ref[0:1, 0:1]
    weight = weight_ref[0:1, 0:1]
    src = (src0[...], src1[...] * scale, src2[...] * scale)
    att = (att0[...], att1[...] * scale, att2[...] * scale)
    out = jnp.where(lane_iota(1) == 0, jnp.sum(square_ref[...], keepdims=True), 0.0)
    for at, (one, two) in enumerate(((0, 0), (0, 1), (1, 1), (1, 2), (2, 2))):
        total = jnp.sum(src[one] * src[two], keepdims=True)
        total = total + weight * jnp.sum(att[one] * att[two], keepdims=True)
        out = jnp.where(lane_iota(1) == at + 1, total, out)
    out_ref[...] = jnp.broadcast_to(out, out_ref.shape)


def finish_kernel(
    dots_ref, scale_ref, src0, src1, src2, att0, att1, att2, sol_src, sol_att, dir_src, dir_att
):
    sums = jnp.sum(dots_ref[...], axis=0, keepdims=True)
    rhs_square, m0, m1, m2, m3, m4 = [lane_value(sums, at) for at in range(6)]
    scale = scale_ref[0:1, 0:1]
    mean = m1 / m0
    ww = m2 - mean * m1
    wz = m3 - 2.0 * mean * m2 + mean * mean * m1
    zz = m4 - 2.0 * mean * m3 + mean * mean * m2
    root0, root1 = jnp.sqrt(m0), jnp.sqrt(ww)
    beta1 = jnp.sqrt(rhs_square)
    alpha1 = root0 / beta1
    beta2 = jnp.sqrt(mean / scale - alpha1 * alpha1)
    cross = root1 / (scale * root0)
    alpha2 = cross / beta2
    quotient = wz / ww / scale
    beta3 = jnp.sqrt(quotient - alpha2 * alpha2)
    third = zz / ww / (scale * scale) - quotient * quotient - cross * cross
    alpha3 = jnp.sqrt(third) / beta3
    phi_bar, rho_bar = beta1, alpha1
    steps, turns = [], []
    for beta, alpha in ((beta2, alpha2), (beta3, alpha3)):
        rho = jnp.sqrt(rho_bar * rho_bar + beta * beta)
        cosine, sine = rho_bar / rho, beta / rho
        theta = sine * alpha
        rho_bar = -cosine * alpha
        steps.append(cosine * phi_bar / rho)
        turns.append(theta / rho)
        phi_bar = sine * phi_bar
    sides = (
        (src0, src1, src2, sol_src, dir_src),
        (att0, att1, att2, sol_att, dir_att),
    )
    for zero, one, two, sol, direction in sides:
        rows = sol.shape[0]
        base, once, twice = zero[0:rows], one[0:rows] * scale, two[0:rows] * scale
        v1 = base / root0
        v2 = (once - mean * base) / root1
        v3 = ((twice - mean * once) / (scale * root1) - quotient * v2 - cross * v1) / (
            beta3 * alpha3
        )
        turned = v2 - turns[0] * v1
        sol[...] = steps[0] * v1 + steps[1] * turned
        direction[...] = v3 - turns[1] * turned


def sds(shape, dtype=F32):
    return jax.ShapeDtypeStruct(shape, dtype)


def in_hbm(values):
    return pltpu.with_memory_space_constraint(values, pltpu.HBM)


def call(kernel, outs, scratch=(), limit=24, **more):
    return pl.pallas_call(
        kernel,
        out_shape=outs,
        scratch_shapes=list(scratch),
        compiler_params=pltpu.CompilerParams(vmem_limit_bytes=limit * MIB),
        **more,
    )


def on_device(src_design, att_design, right_side, block_source, block_segment, block_count):
    narrow, wide = lax.axis_size("narrow"), lax.axis_size("wide")
    devices = narrow * wide
    blocks = block_source.shape[0]
    tiles = blocks // LANE
    cap = blocks // narrow
    src_rows, att_rows = src_design.shape[0], att_design.shape[0]
    rows = src_rows + att_rows
    columns = right_side.shape[0] // LANE
    groups = columns // LANE
    obs = right_side.shape[0] // blocks

    def across(values, step):
        return lax.ppermute(values, "wide", [(i, i ^ step) for i in range(wide)])

    def exchange(values):
        return lax.all_to_all(values, "narrow", 0, 0)

    tile_rows = lambda values: values.reshape(tiles, LANE)
    att_view = att_design.reshape(att_rows // 8, 8, columns, LANE).transpose(0, 2, 1, 3)
    src_view = src_design.reshape(src_rows, columns, LANE).transpose(1, 0, 2)

    right_store = pltpu.VMEM((HIGH, blocks), BF16)
    att_left = pltpu.VMEM((3 * 16 * SEG_DEV // HIGH, blocks), BF16)
    src_left = pltpu.VMEM((3 * 8 * SRC_DEV // HIGH, blocks), BF16)
    tile_int = sds((tiles, LANE), I32)
    send_shape = sds((narrow, 8, cap))
    att_shape = sds((16, SEG_DEV + LANE))
    src_shape = sds((8, SRC_DEV))
    table, square, pos, seg, order, part, send = call(
        functools.partial(start_kernel, narrow),
        (
            sds((tiles, rows, obs, LANE)),
            sds((8, LANE)),
            tile_int,
            tile_int,
            tile_int,
            att_shape,
            send_shape,
        ),
        [
            pltpu.VMEM((groups, att_rows // 8, LANE, 8, LANE), F32),
            pltpu.VMEM((groups, LANE, src_rows, LANE), F32),
            pltpu.VMEM((groups, LANE, LANE), F32),
            pltpu.VMEM((tiles, LANE), I32),
            pltpu.VMEM((tiles, LANE), I32),
            pltpu.VMEM((tiles, LANE), I32),
            pltpu.VMEM((tiles, 24, LANE), F32),
            pltpu.VMEM((tiles, LANE), F32),
            att_left,
            right_store,
            pltpu.SemaphoreType.DMA((3, groups)),
            pltpu.SemaphoreType.DMA((3,)),
        ],
        in_specs=[pl.BlockSpec(memory_space=pltpu.HBM)] * 6,
    )(
        *map(
            in_hbm,
            (
                att_view,
                src_view,
                right_side.reshape(columns, LANE),
                tile_rows(block_source),
                tile_rows(block_segment),
                tile_rows(block_count),
            ),
        )
    )

    given = None
    results = []
    scale = None
    for step in range(3):
        other = across(part, 1)
        arrived = exchange(send)
        first_time = step == 0
        last_time = step == 2
        outs = [src_shape]
        if not last_time:
            outs.append(send_shape)
        outs.append(att_shape)
        outs.append(tile_int if first_time else sds((8, LANE)))
        kernel = functools.partial(owner_kernel, narrow, first_time)
        if last_time:
            whole = lambda *refs, k=kernel: k(*refs[:5], None, *refs[5:])
        else:
            whole = kernel
        given_in = seg if first_time else given
        made = call(whole, tuple(outs), [src_left, right_store])(arrived, part, other, given_in)
        src_sum, half, note = made[0], made[-2], made[-1]
        if first_time:
            given = note
            note = jnp.zeros((8, LANE), F32)
        later = None
        total = half
        jump = 2
        while jump < wide:
            if later is not None:
                total = total + later
            later = across(total, jump)
            jump *= 2
        if later is None:
            later = jnp.zeros_like(total)
        if last_time:
            results.append((src_sum, total, later))
            break
        back = exchange(made[1])
        att_sum, part, send, scale = call(
            functools.partial(product_kernel, narrow, first_time),
            (sds((16, SEG_DEV)), att_shape, send_shape, sds((8, LANE))),
            [
                pltpu.VMEM((tiles, 24, LANE), F32),
                pltpu.VMEM((tiles, 24, LANE), F32),
                att_left,
                right_store,
            ],
        )(back, total, later, note, pos, seg, order, table)
        results.append((src_sum, att_sum))

    weight = jnp.where(lax.axis_index("wide") == 0, 1.0, 0.0).astype(F32) * jnp.ones((8, LANE), F32)
    (src0, att0), (src1, att1), (src2, att2a, att2b) = results
    dots, att2 = call(dots_kernel, (sds((devices, LANE)), sds((16, SEG_DEV))))(
        src0, src1, src2, att0, att1, att2a, att2b, square, scale, weight
    )
    dots = lax.all_to_all(dots, ("wide", "narrow"), 0, 0, tiled=True)
    sol_src, sol_att, dir_src, dir_att = call(
        finish_kernel,
        (
            sds((src_rows, SRC_DEV)),
            sds((att_rows, SEG_DEV)),
            sds((src_rows, SRC_DEV)),
            sds((att_rows, SEG_DEV)),
        ),
    )(dots, scale, src0, src1, src2, att0, att1, att2)
    return (sol_src, sol_att, dir_src, dir_att)


def solution(mesh):
    both = ("wide", "narrow")
    in_specs = (P(None, both), P(None, both), P(both), P(both), P(both), P(both))
    out_specs = (P(None, both), P(None, "narrow"), P(None, both), P(None, "narrow"))
    return jax.shard_map(
        on_device, mesh=mesh, in_specs=in_specs, out_specs=out_specs, check_vma=False
    )
```

```python
import functools

import jax
import jax.numpy as jnp
from jax import lax
from jax.experimental import pallas as pl
from jax.experimental.pallas import tpu as pltpu
from jax.sharding import PartitionSpec as P

SRC_DEV = 2048
SEG_DEV = 1024
LANE = 128
HIGH = 256
F32 = jnp.float32
BF16 = jnp.bfloat16
I32 = jnp.int32
MIB = 1 << 20


def lanes_of(values, index):
    return jnp.take_along_axis(values, index, axis=1, mode="promise_in_bounds")


def row_iota(rows, columns=LANE):
    return lax.broadcasted_iota(I32, (rows, columns), 0)


def lane_iota(rows, columns=LANE):
    return lax.broadcasted_iota(I32, (rows, columns), 1)


def to_tiles(rows):
    count = rows.shape[0]
    lane = lane_iota(count)
    first = lanes_of(rows, (2 * lane) % LANE)
    second = lanes_of(rows, (2 * lane + 1) % LANE)
    head = lane < LANE // 2
    even = jnp.where(head, first, pltpu.roll(first, count - 1, 0))
    odd = jnp.where(head, pltpu.roll(second, 1, 0), second)
    return jnp.where(row_iota(count) % 2 == 0, even, odd)


def split_three(values):
    top = values.astype(BF16).astype(F32)
    rest = values - top
    middle = rest.astype(BF16).astype(F32)
    return top, middle, rest - middle


def dot_lanes(left, right):
    return lax.dot_general(left, right, (((1,), (1,)), ((), ())), preferred_element_type=F32)


def spread_rows(store, picked, row, column, levels):
    rows = picked.shape[0]
    for part, piece in enumerate(split_three(picked)):
        for level in range(levels):
            at = (part * levels + level) * rows
            kept = jnp.where(row == level, piece, 0.0)
            store[pl.ds(at, rows), pl.ds(column, LANE)] = kept.astype(BF16)


def rank_blocks(narrow, source_ref, segment_ref, pos_ref, seg_ref, order_ref, ids_ref, left, right):
    tiles = source_ref.shape[0]
    cap = tiles * LANE // narrow
    local = to_tiles(source_ref[...]) & (SRC_DEV * narrow - 1)
    seg_ref[...] = to_tiles(segment_ref[...]) & (SEG_DEV - 1)
    owner = local // SRC_DEV
    inner = local & (SRC_DEV - 1)
    marks = jnp.concatenate([jnp.where(owner == m, 1.0, 0.0) for m in range(narrow)], axis=0)
    marks = marks.astype(BF16)
    total = narrow * tiles
    before = jnp.where(row_iota(LANE) < lane_iota(LANE), 1.0, 0.0).astype(BF16)
    in_row = jnp.dot(marks, before, preferred_element_type=F32)
    at_row, at_lane = row_iota(total, total), lane_iota(total, total)
    earlier = (at_row // tiles == at_lane // tiles) & (at_lane < at_row)
    ahead = jnp.dot(jnp.where(earlier, 1.0, 0.0).astype(BF16), marks, preferred_element_type=F32)
    ahead = jnp.dot(ahead.astype(BF16), jnp.ones((LANE, LANE), BF16), preferred_element_type=F32)
    rank = (in_row + ahead).astype(I32)
    pos = jnp.zeros((tiles, LANE), I32)
    for m in range(narrow):
        pos = jnp.where(owner == m, m * cap + rank[m * tiles : (m + 1) * tiles], pos)
    pos_ref[...] = pos
    levels = tiles * LANE // HIGH
    high_at = row_iota(HIGH)
    lane = lane_iota(1).astype(F32)
    for t in range(tiles):
        here = pos[t : t + 1]
        level = row_iota(levels) == here // HIGH
        mine = inner[t : t + 1]
        pieces = (
            jnp.full((1, LANE), float(t), F32),
            lane,
            (mine // LANE).astype(F32),
            (mine % LANE).astype(F32),
        )
        for part, piece in enumerate(pieces):
            left[part * levels : (part + 1) * levels, t * LANE : (t + 1) * LANE] = jnp.where(
                level, piece, 0.0
            ).astype(BF16)
        right[:, t * LANE : (t + 1) * LANE] = jnp.where(high_at == here % HIGH, 1.0, 0.0).astype(
            BF16
        )
    found = dot_lanes(left[0 : 4 * levels, :], right[...])
    tile_at, lane_at = found[:levels], found[levels : 2 * levels]
    order = (tile_at * LANE + lane_at).astype(I32)
    ids = found[2 * levels : 3 * levels] * LANE + found[3 * levels :]
    for level in range(levels):
        for half in range(HIGH // LANE):
            row = level * (HIGH // LANE) + half
            cut = slice(half * LANE, (half + 1) * LANE)
            order_ref[row : row + 1, :] = order[level : level + 1, cut]
            ids_ref[row : row + 1, :] = ids[level : level + 1, cut]


def scatter_att(blocks, seg_ref, out_ref, left, right):
    tiles = seg_ref.shape[0]
    levels = SEG_DEV // HIGH
    high_at = row_iota(HIGH)

    def fill(t, carry):
        here = seg_ref[pl.ds(t, 1), :]
        column = pl.multiple_of(t * LANE, LANE)
        spread_rows(left, blocks[t, 0:16, :], here // HIGH, column, levels)
        right[:, pl.ds(column, LANE)] = jnp.where(high_at == here % HIGH, 1.0, 0.0).astype(BF16)
        return carry

    lax.fori_loop(0, tiles, fill, 0)
    sums = dot_lanes(left[...], right[...])
    size = 16 * levels
    sums = sums[:size] + (sums[size : 2 * size] + sums[2 * size :])
    for level in range(levels):
        out_ref[:, level * HIGH : (level + 1) * HIGH] = sums[level * 16 : (level + 1) * 16]


def pick(tables, count, index):
    low = index & (LANE - 1)
    high = index // LANE
    rows = tables(0).shape[0]
    low = jnp.broadcast_to(low, (rows, LANE))
    out = lanes_of(tables(0), low)
    for c in range(1, count):
        out = jnp.where(high == c, lanes_of(tables(c), low), out)
    return out


def send_sorted(narrow, blocks, order_ref, extra, out_ref):
    tiles = order_ref.shape[0]
    cap = tiles * LANE // narrow
    per = cap // LANE
    keep = row_iota(8) < 5
    for t in range(tiles):
        values = pick(lambda c: blocks[c, 16:24, :], tiles, order_ref[t : t + 1, :])
        values = jnp.where(keep, values, extra(t))
        out_ref[t // per, :, (t % per) * LANE : (t % per + 1) * LANE] = values


def entry(ref, per, t):
    return ref[t // per, :, (t % per) * LANE : (t % per + 1) * LANE]


def start_kernel(
    narrow,
    att_hbm, src_hbm, rhs_hbm, source_hbm, segment_hbm, count_hbm,
    table_ref, square_ref, pos_ref, seg_ref, order_ref, att_ref, send_ref,
    att_in, src_in, rhs_in, source_in, segment_in, count_in, blocks, ids, left, right, sems, int_sems,
):
    groups, att_sets = att_in.shape[0], att_in.shape[1]
    att_rows, src_rows = att_sets * 8, src_hbm.shape[1]
    att_flat = att_in.reshape(groups * att_sets * LANE * 8, LANE)
    src_flat = src_in.reshape(groups * LANE * 8, LANE)
    obs = table_ref.shape[2]

    def ints():
        pairs = ((source_hbm, source_in), (segment_hbm, segment_in), (count_hbm, count_in))
        return [
            pltpu.make_async_copy(one, two, int_sems.at[at]) for at, (one, two) in enumerate(pairs)
        ]

    def loads(g):
        cut = pl.ds(g * LANE, LANE)
        return [
            pltpu.make_async_copy(att_hbm.at[:, cut], att_in.at[g], sems.at[0, g]),
            pltpu.make_async_copy(src_hbm.at[cut], src_in.at[g, :, 0:src_rows], sems.at[1, g]),
            pltpu.make_async_copy(rhs_hbm.at[cut], rhs_in.at[g], sems.at[2, g]),
        ]

    def begin(g, carry):
        for one in loads(g):
            one.start()
        return carry

    for one in ints():
        one.start()
    lax.fori_loop(0, groups, begin, 0)
    for one in ints():
        one.wait()
    count_in[...] = to_tiles(count_in[...])
    square_ref[...] = jnp.zeros_like(square_ref)
    rank_blocks(narrow, source_in, segment_in, pos_ref, seg_ref, order_ref, ids, left, right)
    place = row_iota(obs)

    def turn(g, carry):
        for one in loads(g):
            one.wait()
        wide_rhs = rhs_in[g].T
        live, rhs = [], []
        for half in range(2):
            alive = place < count_in[pl.ds(g * 2 + half, 1), :]
            live.append(alive)
            part = jnp.where(alive, wide_rhs[half * obs : half * obs + obs], 0.0)
            rhs.append(part)
            square = part * part
            total = square[0:8]
            for at in range(8, obs, 8):
                total = total + square[at : at + 8]
            square_ref[...] += total
        for i in range(att_rows + src_rows):
            if i < att_rows:
                base = pl.multiple_of((g * att_sets + i // 8) * (LANE * 8), LANE * 8)
                values = att_flat[pl.ds(base + i % 8, LANE, stride=8), :]
            else:
                base = pl.multiple_of(g * (LANE * 8), LANE * 8)
                values = src_flat[pl.ds(base + i - att_rows, LANE, stride=8), :]
            turned = values.T
            for half in range(2):
                part = jnp.where(live[half], turned[half * obs : half * obs + obs], 0.0)
                table_ref[g * 2 + half, i] = part
                blocks[g * 2 + half, i : i + 1, :] = jnp.sum(part * rhs[half], axis=0, keepdims=True)
        for half in range(2):
            rest = 24 - att_rows - src_rows
            blocks[g * 2 + half, 24 - rest : 24, :] = jnp.zeros((rest, LANE), F32)
        return carry

    lax.fori_loop(0, groups, turn, 0)
    scatter_att(blocks, seg_ref, att_ref, left, right)
    lane = lane_iota(16)
    att_ref[:, SEG_DEV:] = jnp.where(lane == 0, jnp.sum(square_ref[...]), 0.0)
    row = row_iota(8)
    send_sorted(
        narrow,
        blocks,
        order_ref,
        lambda t: jnp.where(row == 5, ids[t : t + 1, :], 0.0),
        send_ref,
    )


def owner_kernel(
    narrow, first, recv_ref, half_ref, other_ref, given_ref, src_ref, back_ref, att_ref, out_ref,
    left, right,
):
    tiles, cap = given_ref.shape[0], recv_ref.shape[2]
    per = cap // LANE
    levels = SRC_DEV // HIGH
    high_at = row_iota(HIGH)
    keep = row_iota(8) < 5
    att_ref[...] = half_ref[...] + other_ref[...]
    if first:
        for t in range(tiles):
            out_ref[t : t + 1, :] = entry(recv_ref, per, t)[5:6].astype(I32)
        index_ref = out_ref
    else:
        index_ref = given_ref
        known = recv_ref[0, :, 0:LANE]
        for n in range(1, narrow):
            known = known + recv_ref[n, :, 0:LANE]
        out_ref[...] = known
    for t in range(tiles):
        here = index_ref[t : t + 1, :]
        values = jnp.where(keep, entry(recv_ref, per, t), 0.0)
        spread_rows(left, values, here // HIGH, t * LANE, levels)
        right[:, t * LANE : (t + 1) * LANE] = jnp.where(high_at == here % HIGH, 1.0, 0.0).astype(
            BF16
        )
    sums = dot_lanes(left[...], right[...])
    size = 8 * levels
    sums = sums[:size] + (sums[size : 2 * size] + sums[2 * size :])
    for level in range(levels):
        src_ref[:, level * HIGH : (level + 1) * HIGH] = sums[level * 8 : (level + 1) * 8]
    if back_ref is None:
        return
    square = jnp.sum(src_ref[...] * src_ref[...]) if first else 0.0
    mark = jnp.where((row_iota(8) == 6) & (lane_iota(8) == 0), square, 0.0)
    for t in range(tiles):
        values = pick(
            lambda c: src_ref[:, c * LANE : (c + 1) * LANE],
            SRC_DEV // LANE,
            index_ref[t : t + 1, :],
        )
        values = jnp.where(keep, values, mark)
        back_ref[t // per, :, (t % per) * LANE : (t % per + 1) * LANE] = values


def lane_value(row, at):
    return jnp.sum(jnp.where(lane_iota(1) == at, row, 0.0), axis=1, keepdims=True)


def product_kernel(
    narrow, first, recv_ref, half_ref, other_ref, known_ref, pos_ref, seg_ref, order_ref, table_ref,
    full_ref, att_ref, send_ref, scale_ref, vec, blocks, left, right,
):
    tiles, rows = pos_ref.shape[0], table_ref.shape[1]
    cap = recv_ref.shape[2]
    per = cap // LANE

    full = half_ref[...] + other_ref[...]
    full_ref[...] = full[:, :SEG_DEV]
    notes = full[0:1, SEG_DEV:]
    if first:
        scale = jnp.ones((1, 1), F32)
        square_src = recv_ref[0, 6:7, 0:LANE]
        for n in range(1, narrow):
            square_src = square_src + recv_ref[n, 6:7, 0:LANE]
        square_src = lane_value(square_src, 0)
        square_att = jnp.sum(full[:, :SEG_DEV] * full[:, :SEG_DEV], keepdims=True)
        rhs_square = lane_value(notes, 0)
        att_note = jnp.where(lane_iota(16) == 1, square_src, 0.0)
        send_note = jnp.where(
            row_iota(8) == 6,
            jnp.where(lane_iota(8) == 0, rhs_square, jnp.where(lane_iota(8) == 1, square_att, 0.0)),
            0.0,
        )
    else:
        known = known_ref[6:7, :]
        square = lane_value(notes, 1) + lane_value(known, 1)
        scale = lane_value(known, 0) / square
        att_note = jnp.zeros((16, LANE), F32)
        send_note = jnp.zeros((8, LANE), F32)
    scale_ref[...] = jnp.broadcast_to(scale, (8, LANE))

    def gather(t, carry):
        where_src = pos_ref[pl.ds(t, 1), :]
        where_att = seg_ref[pl.ds(t, 1), :]
        for top in range(0, 16, 8):
            picked = pick(
                lambda c: full_ref[top : top + 8, c * LANE : (c + 1) * LANE],
                SEG_DEV // LANE,
                where_att,
            )
            vec[t, top : top + 8, :] = picked * scale
        vec[t, 16:24, :] = pick(lambda c: entry(recv_ref, per, c), tiles, where_src) * scale
        return carry

    lax.fori_loop(0, tiles, gather, 0)

    def multiply(t, carry):
        image = table_ref[t, 0] * vec[t, 0:1, :]
        for i in range(1, rows):
            image = image + table_ref[t, i] * vec[t, i : i + 1, :]
        for i in range(rows):
            blocks[t, i : i + 1, :] = jnp.sum(table_ref[t, i] * image, axis=0, keepdims=True)
        blocks[t, rows:24, :] = jnp.zeros((24 - rows, LANE), F32)
        return carry

    lax.fori_loop(0, tiles, multiply, 0)
    scatter_att(blocks, seg_ref, att_ref, left, right)
    att_ref[:, SEG_DEV:] = att_note
    send_sorted(narrow, blocks, order_ref, lambda t: send_note, send_ref)


def dots_kernel(
    src0, src1, src2, att0, att1, att2a, att2b, square_ref, scale_ref, weight_ref, out_ref, att2
):
    att2[...] = (att2a[...] + att2b[...])[:, :SEG_DEV]
    scale = scale_ref[0:1, 0:1]
    weight = weight_ref[0:1, 0:1]
    src = (src0[...], src1[...] * scale, src2[...] * scale)
    att = (att0[...], att1[...] * scale, att2[...] * scale)
    out = jnp.where(lane_iota(1) == 0, jnp.sum(square_ref[...], keepdims=True), 0.0)
    for at, (one, two) in enumerate(((0, 0), (0, 1), (1, 1), (1, 2), (2, 2))):
        total = jnp.sum(src[one] * src[two], keepdims=True)
        total = total + weight * jnp.sum(att[one] * att[two], keepdims=True)
        out = jnp.where(lane_iota(1) == at + 1, total, out)
    out_ref[...] = jnp.broadcast_to(out, out_ref.shape)


def finish_kernel(
    dots_ref, scale_ref, src0, src1, src2, att0, att1, att2, sol_src, sol_att, dir_src, dir_att
):
    sums = jnp.sum(dots_ref[...], axis=0, keepdims=True)
    rhs_square, m0, m1, m2, m3, m4 = [lane_value(sums, at) for at in range(6)]
    scale = scale_ref[0:1, 0:1]
    mean = m1 / m0
    ww = m2 - mean * m1
    wz = m3 - 2.0 * mean * m2 + mean * mean * m1
    zz = m4 - 2.0 * mean * m3 + mean * mean * m2
    root0, root1 = jnp.sqrt(m0), jnp.sqrt(ww)
    beta1 = jnp.sqrt(rhs_square)
    alpha1 = root0 / beta1
    beta2 = jnp.sqrt(mean / scale - alpha1 * alpha1)
    cross = root1 / (scale * root0)
    alpha2 = cross / beta2
    quotient = wz / ww / scale
    beta3 = jnp.sqrt(quotient - alpha2 * alpha2)
    third = zz / ww / (scale * scale) - quotient * quotient - cross * cross
    alpha3 = jnp.sqrt(third) / beta3
    phi_bar, rho_bar = beta1, alpha1
    steps, turns = [], []
    for beta, alpha in ((beta2, alpha2), (beta3, alpha3)):
        rho = jnp.sqrt(rho_bar * rho_bar + beta * beta)
        cosine, sine = rho_bar / rho, beta / rho
        theta = sine * alpha
        rho_bar = -cosine * alpha
        steps.append(cosine * phi_bar / rho)
        turns.append(theta / rho)
        phi_bar = sine * phi_bar
    sides = (
        (src0, src1, src2, sol_src, dir_src),
        (att0, att1, att2, sol_att, dir_att),
    )
    for zero, one, two, sol, direction in sides:
        rows = sol.shape[0]
        base, once, twice = zero[0:rows], one[0:rows] * scale, two[0:rows] * scale
        v1 = base / root0
        v2 = (once - mean * base) / root1
        v3 = ((twice - mean * once) / (scale * root1) - quotient * v2 - cross * v1) / (
            beta3 * alpha3
        )
        turned = v2 - turns[0] * v1
        sol[...] = steps[0] * v1 + steps[1] * turned
        direction[...] = v3 - turns[1] * turned


def sds(shape, dtype=F32):
    return jax.ShapeDtypeStruct(shape, dtype)


def in_hbm(values):
    return pltpu.with_memory_space_constraint(values, pltpu.HBM)


def call(kernel, outs, scratch=(), limit=24, **more):
    return pl.pallas_call(
        kernel,
        out_shape=outs,
        scratch_shapes=list(scratch),
        compiler_params=pltpu.CompilerParams(vmem_limit_bytes=limit * MIB),
        **more,
    )


def on_device(src_design, att_design, right_side, block_source, block_segment, block_count):
    narrow, wide = lax.axis_size("narrow"), lax.axis_size("wide")
    devices = narrow * wide
    blocks = block_source.shape[0]
    tiles = blocks // LANE
    cap = blocks // narrow
    src_rows, att_rows = src_design.shape[0], att_design.shape[0]
    rows = src_rows + att_rows
    columns = right_side.shape[0] // LANE
    groups = columns // LANE
    obs = right_side.shape[0] // blocks

    def across(values, step):
        return lax.ppermute(values, "wide", [(i, i ^ step) for i in range(wide)])

    def exchange(values):
        return lax.all_to_all(values, "narrow", 0, 0)

    tile_rows = lambda values: values.reshape(tiles, LANE)
    att_view = att_design.reshape(att_rows // 8, 8, columns, LANE).transpose(0, 2, 1, 3)
    src_view = src_design.reshape(src_rows, columns, LANE).transpose(1, 0, 2)

    right_store = pltpu.VMEM((HIGH, blocks), BF16)
    att_left = pltpu.VMEM((3 * 16 * SEG_DEV // HIGH, blocks), BF16)
    src_left = pltpu.VMEM((3 * 8 * SRC_DEV // HIGH, blocks), BF16)
    tile_int = sds((tiles, LANE), I32)
    send_shape = sds((narrow, 8, cap))
    att_shape = sds((16, SEG_DEV + LANE))
    src_shape = sds((8, SRC_DEV))
    table, square, pos, seg, order, part, send = call(
        functools.partial(start_kernel, narrow),
        (
            sds((tiles, rows, obs, LANE)),
            sds((8, LANE)),
            tile_int,
            tile_int,
            tile_int,
            att_shape,
            send_shape,
        ),
        [
            pltpu.VMEM((groups, att_rows // 8, LANE, 8, LANE), F32),
            pltpu.VMEM((groups, LANE, 8, LANE), F32),
            pltpu.VMEM((groups, LANE, LANE), F32),
            pltpu.VMEM((tiles, LANE), I32),
            pltpu.VMEM((tiles, LANE), I32),
            pltpu.VMEM((tiles, LANE), I32),
            pltpu.VMEM((tiles, 24, LANE), F32),
            pltpu.VMEM((tiles, LANE), F32),
            att_left,
            right_store,
            pltpu.SemaphoreType.DMA((3, groups)),
            pltpu.SemaphoreType.DMA((3,)),
        ],
        in_specs=[pl.BlockSpec(memory_space=pltpu.HBM)] * 6,
    )(
        *map(
            in_hbm,
            (
                att_view,
                src_view,
                right_side.reshape(columns, LANE),
                tile_rows(block_source),
                tile_rows(block_segment),
                tile_rows(block_count),
            ),
        )
    )

    given = None
    results = []
    scale = None
    for step in range(3):
        other = across(part, 1)
        arrived = exchange(send)
        first_time = step == 0
        last_time = step == 2
        outs = [src_shape]
        if not last_time:
            outs.append(send_shape)
        outs.append(att_shape)
        outs.append(tile_int if first_time else sds((8, LANE)))
        kernel = functools.partial(owner_kernel, narrow, first_time)
        if last_time:
            whole = lambda *refs, k=kernel: k(*refs[:5], None, *refs[5:])
        else:
            whole = kernel
        given_in = seg if first_time else given
        made = call(whole, tuple(outs), [src_left, right_store])(arrived, part, other, given_in)
        src_sum, half, note = made[0], made[-2], made[-1]
        if first_time:
            given = note
            note = jnp.zeros((8, LANE), F32)
        later = None
        total = half
        jump = 2
        while jump < wide:
            if later is not None:
                total = total + later
            later = across(total, jump)
            jump *= 2
        if later is None:
            later = jnp.zeros_like(total)
        if last_time:
            results.append((src_sum, total, later))
            break
        back = exchange(made[1])
        att_sum, part, send, scale = call(
            functools.partial(product_kernel, narrow, first_time),
            (sds((16, SEG_DEV)), att_shape, send_shape, sds((8, LANE))),
            [
                pltpu.VMEM((tiles, 24, LANE), F32),
                pltpu.VMEM((tiles, 24, LANE), F32),
                att_left,
                right_store,
            ],
        )(back, total, later, note, pos, seg, order, table)
        results.append((src_sum, att_sum))

    weight = jnp.where(lax.axis_index("wide") == 0, 1.0, 0.0).astype(F32) * jnp.ones((8, LANE), F32)
    (src0, att0), (src1, att1), (src2, att2a, att2b) = results
    dots, att2 = call(dots_kernel, (sds((devices, LANE)), sds((16, SEG_DEV))))(
        src0, src1, src2, att0, att1, att2a, att2b, square, scale, weight
    )
    dots = lax.all_to_all(dots, ("wide", "narrow"), 0, 0, tiled=True)
    sol_src, sol_att, dir_src, dir_att = call(
        finish_kernel,
        (
            sds((src_rows, SRC_DEV)),
            sds((att_rows, SEG_DEV)),
            sds((src_rows, SRC_DEV)),
            sds((att_rows, SEG_DEV)),
        ),
    )(dots, scale, src0, src1, src2, att0, att1, att2)
    return (sol_src, sol_att, dir_src, dir_att)


def solution(mesh):
    both = ("wide", "narrow")
    in_specs = (P(None, both), P(None, both), P(both), P(both), P(both), P(both))
    out_specs = (P(None, both), P(None, "narrow"), P(None, both), P(None, "narrow"))
    return jax.shard_map(
        on_device, mesh=mesh, in_specs=in_specs, out_specs=out_specs, check_vma=False
    )
```

```python
import functools

import jax
import jax.numpy as jnp
from jax import lax
from jax.experimental import pallas as pl
from jax.experimental.pallas import tpu as pltpu
from jax.sharding import PartitionSpec as P


SRC_DEV = 2048
SEG_DEV = 1024
LANE = 128
HIGH = 256
F32 = jnp.float32
BF16 = jnp.bfloat16
I32 = jnp.int32
MIB = 1 << 20


def lanes_of(values, index):
    return jnp.take_along_axis(values, index, axis=1, mode="promise_in_bounds")


def row_iota(rows, columns=LANE):
    return lax.broadcasted_iota(I32, (rows, columns), 0)


def lane_iota(rows, columns=LANE):
    return lax.broadcasted_iota(I32, (rows, columns), 1)


def to_tiles(rows):
    count = rows.shape[0]
    lane = lane_iota(count)
    first = lanes_of(rows, (2 * lane) % LANE)
    second = lanes_of(rows, (2 * lane + 1) % LANE)
    head = lane < LANE // 2
    even = jnp.where(head, first, pltpu.roll(first, count - 1, 0))
    odd = jnp.where(head, pltpu.roll(second, 1, 0), second)
    return jnp.where(row_iota(count) % 2 == 0, even, odd)


def split_three(values):
    top = values.astype(BF16).astype(F32)
    rest = values - top
    middle = rest.astype(BF16).astype(F32)
    return top, middle, rest - middle


def dot_lanes(left, right):
    return lax.dot_general(left, right, (((1,), (1,)), ((), ())), preferred_element_type=F32)


def spread_rows(store, picked, row, column, levels):
    rows = picked.shape[0]
    for part, piece in enumerate(split_three(picked)):
        for level in range(levels):
            at = (part * levels + level) * rows
            kept = jnp.where(row == level, piece, 0.0)
            store[pl.ds(at, rows), pl.ds(column, LANE)] = kept.astype(BF16)


def rank_blocks(narrow, source_ref, segment_ref, pos_ref, seg_ref, order_ref, ids_ref, left, right):
    tiles = source_ref.shape[0]
    cap = tiles * LANE // narrow
    local = to_tiles(source_ref[...]) & (SRC_DEV * narrow - 1)
    seg_ref[...] = to_tiles(segment_ref[...]) & (SEG_DEV - 1)
    owner = local // SRC_DEV
    inner = local & (SRC_DEV - 1)
    marks = jnp.concatenate([jnp.where(owner == m, 1.0, 0.0) for m in range(narrow)], axis=0)
    marks = marks.astype(BF16)
    total = narrow * tiles
    before = jnp.where(row_iota(LANE) < lane_iota(LANE), 1.0, 0.0).astype(BF16)
    in_row = jnp.dot(marks, before, preferred_element_type=F32)
    at_row, at_lane = row_iota(total, total), lane_iota(total, total)
    earlier = (at_row // tiles == at_lane // tiles) & (at_lane < at_row)
    ahead = jnp.dot(jnp.where(earlier, 1.0, 0.0).astype(BF16), marks, preferred_element_type=F32)
    ahead = jnp.dot(ahead.astype(BF16), jnp.ones((LANE, LANE), BF16), preferred_element_type=F32)
    rank = (in_row + ahead).astype(I32)
    pos = jnp.zeros((tiles, LANE), I32)
    for m in range(narrow):
        pos = jnp.where(owner == m, m * cap + rank[m * tiles : (m + 1) * tiles], pos)
    pos_ref[...] = pos
    levels = tiles * LANE // HIGH
    lane = lane_iota(1).astype(F32)
    for t in range(tiles):
        here = pos[t : t + 1]
        level = row_iota(levels) == here // HIGH
        mine = inner[t : t + 1]
        pieces = (
            jnp.full((1, LANE), float(t), F32),
            lane,
            (mine // LANE).astype(F32),
            (mine % LANE).astype(F32),
        )
        for part, piece in enumerate(pieces):
            left[part * levels : (part + 1) * levels, t * LANE : (t + 1) * LANE] = jnp.where(
                level, piece, 0.0
            ).astype(BF16)
    mark_high(right, lambda t: pos[t : t + 1], tiles)
    found = dot_lanes(left[0 : 4 * levels, :], right[...])
    tile_at, lane_at = found[:levels], found[levels : 2 * levels]
    order = (tile_at * LANE + lane_at).astype(I32)
    ids = found[2 * levels : 3 * levels] * LANE + found[3 * levels :]
    for level in range(levels):
        for half in range(HIGH // LANE):
            row = level * (HIGH // LANE) + half
            cut = slice(half * LANE, (half + 1) * LANE)
            order_ref[row : row + 1, :] = order[level : level + 1, cut]
            ids_ref[row : row + 1, :] = ids[level : level + 1, cut]


def mark_high(right, rows_of, tiles):
    high_at = row_iota(HIGH)
    for t in range(tiles):
        here = rows_of(t) & (HIGH - 1)
        right[:, t * LANE : (t + 1) * LANE] = jnp.where(high_at == here, 1.0, 0.0).astype(BF16)


def scatter_att(blocks, seg_ref, out_ref, left, right):
    tiles = seg_ref.shape[0]
    levels = SEG_DEV // HIGH

    def fill(t, carry):
        here = seg_ref[pl.ds(t, 1), :]
        column = pl.multiple_of(t * LANE, LANE)
        spread_rows(left, blocks[t, 0:16, :], here // HIGH, column, levels)
        return carry

    lax.fori_loop(0, tiles, fill, 0)
    sums = dot_lanes(left[...], right[...])
    size = 16 * levels
    sums = sums[:size] + (sums[size : 2 * size] + sums[2 * size :])
    for level in range(levels):
        out_ref[:, level * HIGH : (level + 1) * HIGH] = sums[level * 16 : (level + 1) * 16]


def pick(tables, count, index):
    low = index & (LANE - 1)
    high = index // LANE
    rows = tables(0).shape[0]
    low = jnp.broadcast_to(low, (rows, LANE))
    out = lanes_of(tables(0), low)
    for c in range(1, count):
        out = jnp.where(high == c, lanes_of(tables(c), low), out)
    return out


def send_sorted(narrow, blocks, order_ref, extra, out_ref):
    tiles = order_ref.shape[0]
    cap = tiles * LANE // narrow
    per = cap // LANE
    keep = row_iota(8) < 5
    for t in range(tiles):
        values = pick(lambda c: blocks[c, 16:24, :], tiles, order_ref[t : t + 1, :])
        values = jnp.where(keep, values, extra(t))
        out_ref[t // per, :, (t % per) * LANE : (t % per + 1) * LANE] = values


def entry(ref, per, t):
    return ref[t // per, :, (t % per) * LANE : (t % per + 1) * LANE]


def start_kernel(
    narrow,
    att_hbm, src_hbm, rhs_hbm, source_hbm, segment_hbm, count_hbm,
    table_hbm, square_ref, pos_ref, seg_ref, order_ref, right, att_ref, send_ref,
    table_ref, att_in, src_in, rhs_in, source_in, segment_in, count_in, blocks, ids, left, sems, int_sems,
    out_sems,
):
    groups, att_sets = att_in.shape[0], att_in.shape[1]
    att_rows, src_rows = att_sets * 8, src_hbm.shape[1]
    att_flat = att_in.reshape(groups * att_sets * LANE * 8, LANE)
    src_flat = src_in.reshape(groups * LANE * 8, LANE)
    obs = table_ref.shape[2]

    def ints():
        pairs = ((source_hbm, source_in), (segment_hbm, segment_in), (count_hbm, count_in))
        return [
            pltpu.make_async_copy(one, two, int_sems.at[at]) for at, (one, two) in enumerate(pairs)
        ]

    def loads(g):
        cut = pl.ds(g * LANE, LANE)
        return [
            pltpu.make_async_copy(att_hbm.at[:, cut], att_in.at[g], sems.at[0, g]),
            pltpu.make_async_copy(src_hbm.at[cut], src_in.at[g, :, 0:src_rows], sems.at[1, g]),
            pltpu.make_async_copy(rhs_hbm.at[cut], rhs_in.at[g], sems.at[2, g]),
        ]

    def store(g):
        cut = pl.ds(g * 2, 2)
        return pltpu.make_async_copy(table_ref.at[cut], table_hbm.at[cut], out_sems.at[g])

    def finish(g, carry):
        store(g).wait()
        return carry

    def begin(g, carry):
        for one in loads(g):
            one.start()
        return carry

    for one in ints():
        one.start()
    lax.fori_loop(0, groups, begin, 0)
    for one in ints():
        one.wait()
    count_in[...] = to_tiles(count_in[...])
    square_ref[...] = jnp.zeros_like(square_ref)
    rank_blocks(narrow, source_in, segment_in, pos_ref, seg_ref, order_ref, ids, left, right)
    mark_high(right, lambda t: seg_ref[t : t + 1, :], seg_ref.shape[0])
    place = row_iota(obs)

    def turn(g, carry):
        for one in loads(g):
            one.wait()
        wide_rhs = rhs_in[g].T
        live, rhs = [], []
        for half in range(2):
            alive = place < count_in[pl.ds(g * 2 + half, 1), :]
            live.append(alive)
            part = jnp.where(alive, wide_rhs[half * obs : half * obs + obs], 0.0)
            rhs.append(part)
            square = part * part
            total = square[0:8]
            for at in range(8, obs, 8):
                total = total + square[at : at + 8]
            square_ref[...] += total
        for i in range(att_rows + src_rows):
            if i < att_rows:
                base = pl.multiple_of((g * att_sets + i // 8) * (LANE * 8), LANE * 8)
                values = att_flat[pl.ds(base + i % 8, LANE, stride=8), :]
            else:
                base = pl.multiple_of(g * (LANE * 8), LANE * 8)
                values = src_flat[pl.ds(base + i - att_rows, LANE, stride=8), :]
            turned = values.T
            for half in range(2):
                part = jnp.where(live[half], turned[half * obs : half * obs + obs], 0.0)
                table_ref[g * 2 + half, i] = part
                blocks[g * 2 + half, i : i + 1, :] = jnp.sum(part * rhs[half], axis=0, keepdims=True)
        for half in range(2):
            rest = 24 - att_rows - src_rows
            blocks[g * 2 + half, 24 - rest : 24, :] = jnp.zeros((rest, LANE), F32)
        store(g).start()
        return carry

    lax.fori_loop(0, groups, turn, 0)
    scatter_att(blocks, seg_ref, att_ref, left, right)
    lane = lane_iota(16)
    att_ref[:, SEG_DEV:] = jnp.where(lane == 0, jnp.sum(square_ref[...]), 0.0)
    row = row_iota(8)
    send_sorted(
        narrow,
        blocks,
        order_ref,
        lambda t: jnp.where(row == 5, ids[t : t + 1, :], 0.0),
        send_ref,
    )
    lax.fori_loop(0, groups, finish, 0)


def owner_kernel(narrow, first, last, *refs):
    if first:
        recv_ref, src_ref, back_ref, index_ref, right, left = refs
    elif last:
        recv_ref, index_ref, right, src_ref, left = refs
    else:
        recv_ref, index_ref, right, src_ref, back_ref, known_ref, left = refs
    tiles, cap = index_ref.shape[0], recv_ref.shape[2]
    per = cap // LANE
    levels = SRC_DEV // HIGH
    keep = row_iota(8) < 5
    if first:
        for t in range(tiles):
            index_ref[t : t + 1, :] = entry(recv_ref, per, t)[5:6].astype(I32)
        mark_high(right, lambda t: index_ref[t : t + 1, :], tiles)
    elif not last:
        known = recv_ref[0, :, 0:LANE]
        for n in range(1, narrow):
            known = known + recv_ref[n, :, 0:LANE]
        known_ref[...] = known
    for t in range(tiles):
        here = index_ref[t : t + 1, :]
        values = jnp.where(keep, entry(recv_ref, per, t), 0.0)
        spread_rows(left, values, here // HIGH, t * LANE, levels)
    sums = dot_lanes(left[...], right[...])
    size = 8 * levels
    sums = sums[:size] + (sums[size : 2 * size] + sums[2 * size :])
    for level in range(levels):
        src_ref[:, level * HIGH : (level + 1) * HIGH] = sums[level * 8 : (level + 1) * 8]
    if last:
        return
    square = jnp.sum(src_ref[...] * src_ref[...]) if first else 0.0
    mark = jnp.where((row_iota(8) == 6) & (lane_iota(8) == 0), square, 0.0)
    for t in range(tiles):
        values = pick(
            lambda c: src_ref[:, c * LANE : (c + 1) * LANE],
            SRC_DEV // LANE,
            index_ref[t : t + 1, :],
        )
        values = jnp.where(keep, values, mark)
        back_ref[t // per, :, (t % per) * LANE : (t % per + 1) * LANE] = values


def lane_value(row, at):
    return jnp.sum(jnp.where(lane_iota(1) == at, row, 0.0), axis=1, keepdims=True)


def product_kernel(
    narrow, first, recv_ref, half_ref, later_ref, known_ref, pos_ref, seg_ref, order_ref, right,
    table_hbm, full_ref, att_ref, send_ref, scale_ref, vec, blocks, left, table_ref, sems,
):
    tiles, rows = pos_ref.shape[0], table_ref.shape[1]

    def load(t):
        return pltpu.make_async_copy(table_hbm.at[t], table_ref.at[t], sems.at[t])

    def begin(t, carry):
        load(t).start()
        return carry

    lax.fori_loop(0, tiles, begin, 0)
    cap = recv_ref.shape[2]
    per = cap // LANE
    full = half_ref[...] + later_ref[...]
    full_ref[...] = full[:, :SEG_DEV]
    notes = full[0:1, SEG_DEV:]
    lane, row = lane_iota(8), row_iota(8)
    send_note = jnp.zeros((8, LANE), F32)
    att_note = jnp.zeros((16, LANE), F32)
    if first:
        scale = jnp.ones((1, 1), F32)
        square_src = recv_ref[0, 6:7, 0:LANE]
        for n in range(1, narrow):
            square_src = square_src + recv_ref[n, 6:7, 0:LANE]
        att_note = jnp.where(lane_iota(16) == 1, lane_value(square_src, 0), 0.0)
        square_att = jnp.sum(full[:, :SEG_DEV] * full[:, :SEG_DEV], keepdims=True)
        send_note = jnp.where(lane == 0, lane_value(notes, 0), 0.0)
        send_note = jnp.where(lane == 1, square_att, send_note)
        send_note = jnp.where(row == 6, send_note, 0.0)
    else:
        known = known_ref[6:7, :]
        square = lane_value(notes, 1) + lane_value(known, 1)
        scale = lane_value(known, 0) / square
    scale_ref[...] = jnp.broadcast_to(scale, (8, LANE))
    att_ref[:, SEG_DEV:] = att_note

    def gather(t, carry):
        where_att = seg_ref[pl.ds(t, 1), :]
        for top in range(0, 24, 8):
            if top < 16:
                picked = pick(
                    lambda c: full_ref[top : top + 8, c * LANE : (c + 1) * LANE],
                    SEG_DEV // LANE,
                    where_att,
                )
            else:
                picked = pick(lambda c: entry(recv_ref, per, c), tiles, pos_ref[pl.ds(t, 1), :])
            vec[t, top : top + 8, :] = picked if first else picked * scale
        return carry

    lax.fori_loop(0, tiles, gather, 0)

    def multiply(t, carry):
        load(t).wait()
        image = None
        for i in range(rows):
            part = table_ref[t, i] * vec[t, i : i + 1, :]
            image = part if image is None else image + part
        for i in range(rows):
            blocks[t, i : i + 1, :] = jnp.sum(table_ref[t, i] * image, axis=0, keepdims=True)
        blocks[t, rows:24, :] = jnp.zeros((24 - rows, LANE), F32)
        return carry

    lax.fori_loop(0, tiles, multiply, 0)
    scatter_att(blocks, seg_ref, att_ref, left, right)
    send_sorted(narrow, blocks, order_ref, lambda t: send_note, send_ref)


def dots_kernel(
    src0, src1, src2, att0, att1, att2a, att2b, square_ref, scale_ref, weight_ref, out_ref, att2
):
    att2[...] = (att2a[...] + att2b[...])[:, :SEG_DEV]
    scale = scale_ref[0:1, 0:1]
    weight = weight_ref[0:1, 0:1]
    src = (src0[...], src1[...] * scale, src2[...] * scale)
    att = (att0[...], att1[...] * scale, att2[...] * scale)
    out = jnp.where(lane_iota(1) == 0, jnp.sum(square_ref[...], keepdims=True), 0.0)
    for at, (one, two) in enumerate(((0, 0), (0, 1), (1, 1), (1, 2), (2, 2))):
        total = jnp.sum(src[one] * src[two], keepdims=True)
        total = total + weight * jnp.sum(att[one] * att[two], keepdims=True)
        out = jnp.where(lane_iota(1) == at + 1, total, out)
    out_ref[...] = jnp.broadcast_to(out, out_ref.shape)


def finish_kernel(
    dots_ref, scale_ref, src0, src1, src2, att0, att1, att2, sol_src, sol_att, dir_src, dir_att
):
    sums = jnp.sum(dots_ref[...], axis=0, keepdims=True)
    rhs_square, m0, m1, m2, m3, m4 = [lane_value(sums, at) for at in range(6)]
    scale = scale_ref[0:1, 0:1]
    mean = m1 / m0
    ww = m2 - mean * m1
    wz = m3 - 2.0 * mean * m2 + mean * mean * m1
    zz = m4 - 2.0 * mean * m3 + mean * mean * m2
    root0, root1 = jnp.sqrt(m0), jnp.sqrt(ww)
    beta1 = jnp.sqrt(rhs_square)
    alpha1 = root0 / beta1
    beta2 = jnp.sqrt(mean / scale - alpha1 * alpha1)
    cross = root1 / (scale * root0)
    alpha2 = cross / beta2
    quotient = wz / ww / scale
    beta3 = jnp.sqrt(quotient - alpha2 * alpha2)
    third = zz / ww / (scale * scale) - quotient * quotient - cross * cross
    alpha3 = jnp.sqrt(third) / beta3
    phi_bar, rho_bar = beta1, alpha1
    steps, turns = [], []
    for beta, alpha in ((beta2, alpha2), (beta3, alpha3)):
        rho = jnp.sqrt(rho_bar * rho_bar + beta * beta)
        cosine, sine = rho_bar / rho, beta / rho
        theta = sine * alpha
        rho_bar = -cosine * alpha
        steps.append(cosine * phi_bar / rho)
        turns.append(theta / rho)
        phi_bar = sine * phi_bar
    sides = (
        (src0, src1, src2, sol_src, dir_src),
        (att0, att1, att2, sol_att, dir_att),
    )
    for zero, one, two, sol, direction in sides:
        rows = sol.shape[0]
        base, once, twice = zero[0:rows], one[0:rows] * scale, two[0:rows] * scale
        v1 = base / root0
        v2 = (once - mean * base) / root1
        v3 = ((twice - mean * once) / (scale * root1) - quotient * v2 - cross * v1) / (
            beta3 * alpha3
        )
        turned = v2 - turns[0] * v1
        sol[...] = steps[0] * v1 + steps[1] * turned
        direction[...] = v3 - turns[1] * turned


def sds(shape, dtype=F32):
    return jax.ShapeDtypeStruct(shape, dtype)


def in_hbm(values):
    return pltpu.with_memory_space_constraint(values, pltpu.HBM)


def call(kernel, outs, scratch=(), limit=8, **more):
    return pl.pallas_call(
        kernel,
        out_shape=outs,
        scratch_shapes=list(scratch),
        compiler_params=pltpu.CompilerParams(vmem_limit_bytes=limit * MIB),
        **more,
    )


def on_device(src_design, att_design, right_side, block_source, block_segment, block_count):
    narrow, wide = lax.axis_size("narrow"), lax.axis_size("wide")
    devices = narrow * wide
    blocks = block_source.shape[0]
    tiles = blocks // LANE
    cap = blocks // narrow
    src_rows, att_rows = src_design.shape[0], att_design.shape[0]
    rows = src_rows + att_rows
    columns = right_side.shape[0] // LANE
    groups = columns // LANE
    obs = right_side.shape[0] // blocks

    def across(values, step):
        return lax.ppermute(values, "wide", [(i, i ^ step) for i in range(wide)])

    def exchange(values):
        return lax.all_to_all(values, "narrow", 0, 0)

    tile_rows = lambda values: values.reshape(tiles, LANE)
    att_view = att_design.reshape(att_rows // 8, 8, columns, LANE).transpose(0, 2, 1, 3)
    src_view = src_design.reshape(src_rows, columns, LANE).transpose(1, 0, 2)

    right_shape = sds((HIGH, blocks), BF16)
    att_left = pltpu.VMEM((3 * 16 * SEG_DEV // HIGH, blocks), BF16)
    src_left = pltpu.VMEM((3 * 8 * SRC_DEV // HIGH, blocks), BF16)
    tile_int = sds((tiles, LANE), I32)
    send_shape = sds((narrow, 8, cap))
    att_shape = sds((16, SEG_DEV + LANE))
    src_shape = sds((8, SRC_DEV))
    table_shape = (tiles, rows, obs, LANE)
    table, square, pos, seg, order, att_right, part, send = call(
        functools.partial(start_kernel, narrow),
        (
            pltpu.HBM(table_shape, F32),
            sds((8, LANE)),
            tile_int,
            tile_int,
            tile_int,
            right_shape,
            att_shape,
            send_shape,
        ),
        [
            pltpu.VMEM(table_shape, F32),
            pltpu.VMEM((groups, att_rows // 8, LANE, 8, LANE), F32),
            pltpu.VMEM((groups, LANE, 8, LANE), F32),
            pltpu.VMEM((groups, LANE, LANE), F32),
            pltpu.VMEM((tiles, LANE), I32),
            pltpu.VMEM((tiles, LANE), I32),
            pltpu.VMEM((tiles, LANE), I32),
            pltpu.VMEM((tiles, 24, LANE), F32),
            pltpu.VMEM((tiles, LANE), F32),
            att_left,
            pltpu.SemaphoreType.DMA((3, groups)),
            pltpu.SemaphoreType.DMA((3,)),
            pltpu.SemaphoreType.DMA((groups,)),
        ],
        in_specs=[pl.BlockSpec(memory_space=pltpu.HBM)] * 6,
        out_specs=(pl.BlockSpec(memory_space=pltpu.HBM),)
        + (pl.BlockSpec(memory_space=pltpu.VMEM),) * 7,
        limit=32,
    )(
        *map(
            in_hbm,
            (
                att_view,
                src_view,
                right_side.reshape(columns, LANE),
                tile_rows(block_source),
                tile_rows(block_segment),
                tile_rows(block_count),
            ),
        )
    )

    results = []
    note = jnp.zeros((8, LANE), F32)
    owners = None
    for step in range(3):
        first_time, last_time = step == 0, step == 2
        other = across(part, 1)
        arrived = exchange(send)
        total, jump = part + other, 2
        later = None
        while jump < wide:
            if later is not None:
                total = total + later
            later = across(total, jump)
            jump *= 2
        if later is None:
            later = jnp.zeros_like(total)
        kernel = functools.partial(owner_kernel, narrow, first_time, last_time)
        if first_time:
            src_sum, back, *owners = call(
                kernel, (src_shape, send_shape, tile_int, right_shape), [src_left]
            )(arrived)
        elif last_time:
            src_sum = call(kernel, src_shape, [src_left])(arrived, *owners)
            results.append((src_sum, total, later))
            break
        else:
            src_sum, back, note = call(
                kernel, (src_shape, send_shape, sds((8, LANE))), [src_left]
            )(arrived, *owners)
        back = exchange(back)
        att_sum, part, send, scale = call(
            functools.partial(product_kernel, narrow, first_time),
            (sds((16, SEG_DEV)), att_shape, send_shape, sds((8, LANE))),
            [
                pltpu.VMEM((tiles, 24, LANE), F32),
                pltpu.VMEM((tiles, 24, LANE), F32),
                att_left,
                pltpu.VMEM(table_shape, F32),
                pltpu.SemaphoreType.DMA((tiles,)),
            ],
            in_specs=[pl.BlockSpec(memory_space=pltpu.VMEM)] * 8
            + [pl.BlockSpec(memory_space=pltpu.HBM)],
            limit=20,
        )(back, total, later, note, pos, seg, order, att_right, in_hbm(table))
        results.append((src_sum, att_sum))
    weight = jnp.where(lax.axis_index("wide") == 0, 1.0, 0.0).astype(F32) * jnp.ones((8, LANE), F32)
    (src0, att0), (src1, att1), (src2, att2a, att2b) = results
    dots, att2 = call(dots_kernel, (sds((devices, LANE)), sds((16, SEG_DEV))))(
        src0, src1, src2, att0, att1, att2a, att2b, square, scale, weight
    )
    dots = lax.all_to_all(dots, ("wide", "narrow"), 0, 0, tiled=True)
    sol_src, sol_att, dir_src, dir_att = call(
        finish_kernel,
        (
            sds((src_rows, SRC_DEV)),
            sds((att_rows, SEG_DEV)),
            sds((src_rows, SRC_DEV)),
            sds((att_rows, SEG_DEV)),
        ),
    )(dots, scale, src0, src1, src2, att0, att1, att2)
    return (sol_src, sol_att, dir_src, dir_att)


def solution(mesh):
    both = ("wide", "narrow")
    in_specs = (P(None, both), P(None, both), P(both), P(both), P(both), P(both))
    out_specs = (P(None, both), P(None, "narrow"), P(None, both), P(None, "narrow"))

    return jax.shard_map(
        on_device, mesh=mesh, in_specs=in_specs, out_specs=out_specs, check_vma=False
    )
```

```python
import functools

import jax
import jax.numpy as jnp
from jax import lax
from jax.experimental import pallas as pl
from jax.experimental.pallas import tpu as pltpu
from jax.sharding import PartitionSpec as P


SRC_DEV = 2048
SEG_DEV = 1024
LANE = 128
HIGH = 256
F32 = jnp.float32
BF16 = jnp.bfloat16
I32 = jnp.int32
MIB = 1 << 20


def lanes_of(values, index):
    return jnp.take_along_axis(values, index, axis=1, mode="promise_in_bounds")


def row_iota(rows, columns=LANE):
    return lax.broadcasted_iota(I32, (rows, columns), 0)


def lane_iota(rows, columns=LANE):
    return lax.broadcasted_iota(I32, (rows, columns), 1)


def to_tiles(rows):
    count = rows.shape[0]
    lane = lane_iota(count)
    first = lanes_of(rows, (2 * lane) % LANE)
    second = lanes_of(rows, (2 * lane + 1) % LANE)
    head = lane < LANE // 2
    even = jnp.where(head, first, pltpu.roll(first, count - 1, 0))
    odd = jnp.where(head, pltpu.roll(second, 1, 0), second)
    return jnp.where(row_iota(count) % 2 == 0, even, odd)


def split_three(values):
    top = values.astype(BF16).astype(F32)
    rest = values - top
    middle = rest.astype(BF16).astype(F32)
    return top, middle, rest - middle


def dot_lanes(left, right):
    return lax.dot_general(left, right, (((1,), (1,)), ((), ())), preferred_element_type=F32)


def spread_rows(store, picked, row, column, levels):
    rows = picked.shape[0]
    for part, piece in enumerate(split_three(picked)):
        for level in range(levels):
            at = (part * levels + level) * rows
            kept = jnp.where(row == level, piece, 0.0)
            store[pl.ds(at, rows), pl.ds(column, LANE)] = kept.astype(BF16)


def rank_blocks(narrow, source_ref, segment_ref, pos_ref, seg_ref, order_ref, ids_ref, left, right):
    tiles = source_ref.shape[0]
    cap = tiles * LANE // narrow
    local = to_tiles(source_ref[...]) & (SRC_DEV * narrow - 1)
    seg_ref[...] = to_tiles(segment_ref[...]) & (SEG_DEV - 1)
    owner = local // SRC_DEV
    inner = local & (SRC_DEV - 1)
    marks = jnp.concatenate([jnp.where(owner == m, 1.0, 0.0) for m in range(narrow)], axis=0)
    marks = marks.astype(BF16)
    total = narrow * tiles
    before = jnp.where(row_iota(LANE) < lane_iota(LANE), 1.0, 0.0).astype(BF16)
    in_row = jnp.dot(marks, before, preferred_element_type=F32)
    at_row, at_lane = row_iota(total, total), lane_iota(total, total)
    earlier = (at_row // tiles == at_lane // tiles) & (at_lane < at_row)
    ahead = jnp.dot(jnp.where(earlier, 1.0, 0.0).astype(BF16), marks, preferred_element_type=F32)
    ahead = jnp.dot(ahead.astype(BF16), jnp.ones((LANE, LANE), BF16), preferred_element_type=F32)
    rank = (in_row + ahead).astype(I32)
    pos = jnp.zeros((tiles, LANE), I32)
    for m in range(narrow):
        pos = jnp.where(owner == m, m * cap + rank[m * tiles : (m + 1) * tiles], pos)
    pos_ref[...] = pos
    levels = tiles * LANE // HIGH
    lane = lane_iota(1).astype(F32)
    for t in range(tiles):
        here = pos[t : t + 1]
        level = row_iota(levels) == here // HIGH
        mine = inner[t : t + 1]
        pieces = (
            jnp.full((1, LANE), float(t), F32),
            lane,
            (mine // LANE).astype(F32),
            (mine % LANE).astype(F32),
        )
        for part, piece in enumerate(pieces):
            left[part * levels : (part + 1) * levels, t * LANE : (t + 1) * LANE] = jnp.where(
                level, piece, 0.0
            ).astype(BF16)
    mark_high(right, lambda t: pos[t : t + 1], tiles)
    found = dot_lanes(left[0 : 4 * levels, :], right[...])
    tile_at, lane_at = found[:levels], found[levels : 2 * levels]
    order = (tile_at * LANE + lane_at).astype(I32)
    ids = found[2 * levels : 3 * levels] * LANE + found[3 * levels :]
    for level in range(levels):
        for half in range(HIGH // LANE):
            row = level * (HIGH // LANE) + half
            cut = slice(half * LANE, (half + 1) * LANE)
            order_ref[row : row + 1, :] = order[level : level + 1, cut]
            ids_ref[row : row + 1, :] = ids[level : level + 1, cut]


def mark_high(right, rows_of, tiles):
    high_at = row_iota(HIGH)
    for t in range(tiles):
        here = rows_of(t) & (HIGH - 1)
        right[:, t * LANE : (t + 1) * LANE] = jnp.where(high_at == here, 1.0, 0.0).astype(BF16)


def scatter_att(blocks, seg_ref, out_ref, left, right):
    tiles = seg_ref.shape[0]
    levels = SEG_DEV // HIGH

    def fill(t, carry):
        here = seg_ref[pl.ds(t, 1), :]
        column = pl.multiple_of(t * LANE, LANE)
        spread_rows(left, blocks[t, 0:16, :], here // HIGH, column, levels)
        return carry

    lax.fori_loop(0, tiles, fill, 0)
    sums = dot_lanes(left[...], right[...])
    size = 16 * levels
    sums = sums[:size] + (sums[size : 2 * size] + sums[2 * size :])
    for level in range(levels):
        out_ref[:, level * HIGH : (level + 1) * HIGH] = sums[level * 16 : (level + 1) * 16]


def pick(tables, count, index):
    low = index & (LANE - 1)
    high = index // LANE
    rows = tables(0).shape[0]
    low = jnp.broadcast_to(low, (rows, LANE))
    out = lanes_of(tables(0), low)
    for c in range(1, count):
        out = jnp.where(high == c, lanes_of(tables(c), low), out)
    return out


def send_sorted(narrow, blocks, order_ref, extra, out_ref):
    tiles = order_ref.shape[0]
    cap = tiles * LANE // narrow
    per = cap // LANE
    keep = row_iota(8) < 5
    for t in range(tiles):
        values = pick(lambda c: blocks[c, 16:24, :], tiles, order_ref[t : t + 1, :])
        values = jnp.where(keep, values, extra(t))
        out_ref[t // per, :, (t % per) * LANE : (t % per + 1) * LANE] = values


def entry(ref, per, t):
    return ref[t // per, :, (t % per) * LANE : (t % per + 1) * LANE]


def start_kernel(
    narrow,
    att_hbm, src_hbm, rhs_hbm, source_hbm, segment_hbm, count_hbm,
    table_ref, square_ref, pos_ref, seg_ref, order_ref, right, att_ref, send_ref,
    att_in, src_in, rhs_in, source_in, segment_in, count_in, blocks, ids, left, sems, int_sems,
):
    groups, att_sets = att_in.shape[0], att_in.shape[1]
    att_rows, src_rows = att_sets * 8, src_hbm.shape[1]
    att_flat = att_in.reshape(groups * att_sets * LANE * 8, LANE)
    src_flat = src_in.reshape(groups * LANE * 8, LANE)
    obs = table_ref.shape[2]

    def ints():
        pairs = ((source_hbm, source_in), (segment_hbm, segment_in), (count_hbm, count_in))
        return [
            pltpu.make_async_copy(one, two, int_sems.at[at]) for at, (one, two) in enumerate(pairs)
        ]

    def loads(g):
        cut = pl.ds(g * LANE, LANE)
        return [
            pltpu.make_async_copy(att_hbm.at[:, cut], att_in.at[g], sems.at[0, g]),
            pltpu.make_async_copy(src_hbm.at[cut], src_in.at[g, :, 0:src_rows], sems.at[1, g]),
            pltpu.make_async_copy(rhs_hbm.at[cut], rhs_in.at[g], sems.at[2, g]),
        ]

    def begin(g, carry):
        for one in loads(g):
            one.start()
        return carry

    for one in ints():
        one.start()
    lax.fori_loop(0, groups, begin, 0)
    for one in ints():
        one.wait()
    count_in[...] = to_tiles(count_in[...])
    square_ref[...] = jnp.zeros_like(square_ref)
    rank_blocks(narrow, source_in, segment_in, pos_ref, seg_ref, order_ref, ids, left, right)
    mark_high(right, lambda t: seg_ref[t : t + 1, :], seg_ref.shape[0])
    place = row_iota(obs)

    def turn(g, carry):
        for one in loads(g):
            one.wait()
        wide_rhs = rhs_in[g].T
        live, rhs = [], []
        for half in range(2):
            alive = place < count_in[pl.ds(g * 2 + half, 1), :]
            live.append(alive)
            part = jnp.where(alive, wide_rhs[half * obs : half * obs + obs], 0.0)
            rhs.append(part)
            square = part * part
            total = square[0:8]
            for at in range(8, obs, 8):
                total = total + square[at : at + 8]
            square_ref[...] += total
        for i in range(att_rows + src_rows):
            if i < att_rows:
                base = pl.multiple_of((g * att_sets + i // 8) * (LANE * 8), LANE * 8)
                values = att_flat[pl.ds(base + i % 8, LANE, stride=8), :]
            else:
                base = pl.multiple_of(g * (LANE * 8), LANE * 8)
                values = src_flat[pl.ds(base + i - att_rows, LANE, stride=8), :]
            turned = values.T
            for half in range(2):
                part = jnp.where(live[half], turned[half * obs : half * obs + obs], 0.0)
                table_ref[g * 2 + half, i] = part
                blocks[g * 2 + half, i : i + 1, :] = jnp.sum(part * rhs[half], axis=0, keepdims=True)
        for half in range(2):
            rest = 24 - att_rows - src_rows
            blocks[g * 2 + half, 24 - rest : 24, :] = jnp.zeros((rest, LANE), F32)
        return carry

    lax.fori_loop(0, groups, turn, 0)
    scatter_att(blocks, seg_ref, att_ref, left, right)
    lane = lane_iota(16)
    att_ref[:, SEG_DEV:] = jnp.where(lane == 0, jnp.sum(square_ref[...]), 0.0)
    row = row_iota(8)
    send_sorted(
        narrow,
        blocks,
        order_ref,
        lambda t: jnp.where(row == 5, ids[t : t + 1, :], 0.0),
        send_ref,
    )


def owner_kernel(narrow, first, last, *refs):
    if first:
        recv_ref, part_ref, other_ref, src_ref, back_ref, half_ref, index_ref, right, left = refs
    elif last:
        recv_ref, index_ref, right, src_ref, left = refs
    else:
        recv_ref, part_ref, other_ref, index_ref, right = refs[:5]
        src_ref, back_ref, half_ref, known_ref, left = refs[5:]
    if not last:
        half_ref[...] = part_ref[...] + other_ref[...]
    tiles, cap = index_ref.shape[0], recv_ref.shape[2]
    per = cap // LANE
    levels = SRC_DEV // HIGH
    keep = row_iota(8) < 5
    if first:
        for t in range(tiles):
            index_ref[t : t + 1, :] = entry(recv_ref, per, t)[5:6].astype(I32)
        mark_high(right, lambda t: index_ref[t : t + 1, :], tiles)
    elif not last:
        known = recv_ref[0, :, 0:LANE]
        for n in range(1, narrow):
            known = known + recv_ref[n, :, 0:LANE]
        known_ref[...] = known
    for t in range(tiles):
        here = index_ref[t : t + 1, :]
        values = jnp.where(keep, entry(recv_ref, per, t), 0.0)
        spread_rows(left, values, here // HIGH, t * LANE, levels)
    sums = dot_lanes(left[...], right[...])
    size = 8 * levels
    sums = sums[:size] + (sums[size : 2 * size] + sums[2 * size :])
    for level in range(levels):
        src_ref[:, level * HIGH : (level + 1) * HIGH] = sums[level * 8 : (level + 1) * 8]
    if last:
        return
    square = jnp.sum(src_ref[...] * src_ref[...]) if first else 0.0
    mark = jnp.where((row_iota(8) == 6) & (lane_iota(8) == 0), square, 0.0)
    for t in range(tiles):
        values = pick(
            lambda c: src_ref[:, c * LANE : (c + 1) * LANE],
            SRC_DEV // LANE,
            index_ref[t : t + 1, :],
        )
        values = jnp.where(keep, values, mark)
        back_ref[t // per, :, (t % per) * LANE : (t % per + 1) * LANE] = values


def lane_value(row, at):
    return jnp.sum(jnp.where(lane_iota(1) == at, row, 0.0), axis=1, keepdims=True)


def product_kernel(
    narrow, first, recv_ref, half_ref, later_ref, known_ref, pos_ref, seg_ref, order_ref, right,
    table_ref, full_ref, att_ref, send_ref, scale_ref, vec, blocks, left,
):
    tiles, rows = pos_ref.shape[0], table_ref.shape[1]
    per = recv_ref.shape[2] // LANE
    full = half_ref[...] + later_ref[...]
    full_ref[...] = full[:, :SEG_DEV]
    notes = full[0:1, SEG_DEV:]
    lane, row = lane_iota(8), row_iota(8)
    send_note = jnp.zeros((8, LANE), F32)
    att_note = jnp.zeros((16, LANE), F32)
    if first:
        scale = jnp.ones((1, 1), F32)
        square_src = recv_ref[0, 6:7, 0:LANE]
        for n in range(1, narrow):
            square_src = square_src + recv_ref[n, 6:7, 0:LANE]
        att_note = jnp.where(lane_iota(16) == 1, lane_value(square_src, 0), 0.0)
        square_att = jnp.sum(full[:, :SEG_DEV] * full[:, :SEG_DEV], keepdims=True)
        send_note = jnp.where(lane == 0, lane_value(notes, 0), 0.0)
        send_note = jnp.where(lane == 1, square_att, send_note)
        send_note = jnp.where(row == 6, send_note, 0.0)
    else:
        known = known_ref[6:7, :]
        square = lane_value(notes, 1) + lane_value(known, 1)
        scale = lane_value(known, 0) / square
    scale_ref[...] = jnp.broadcast_to(scale, (8, LANE))
    att_ref[:, SEG_DEV:] = att_note

    def gather(t, carry):
        where_att = seg_ref[pl.ds(t, 1), :]
        for top in range(0, 24, 8):
            if top < 16:
                picked = pick(
                    lambda c: full_ref[top : top + 8, c * LANE : (c + 1) * LANE],
                    SEG_DEV // LANE,
                    where_att,
                )
            else:
                picked = pick(lambda c: entry(recv_ref, per, c), tiles, pos_ref[pl.ds(t, 1), :])
            vec[t, top : top + 8, :] = picked if first else picked * scale
        return carry

    lax.fori_loop(0, tiles, gather, 0)

    def multiply(t, carry):
        image = None
        for i in range(rows):
            part = table_ref[t, i] * vec[t, i : i + 1, :]
            image = part if image is None else image + part
        for i in range(rows):
            blocks[t, i : i + 1, :] = jnp.sum(table_ref[t, i] * image, axis=0, keepdims=True)
        blocks[t, rows:24, :] = jnp.zeros((24 - rows, LANE), F32)
        return carry

    lax.fori_loop(0, tiles, multiply, 0)
    scatter_att(blocks, seg_ref, att_ref, left, right)
    send_sorted(narrow, blocks, order_ref, lambda t: send_note, send_ref)


def dots_kernel(
    src0, src1, src2, att0, att1, att2a, att2b, square_ref, scale_ref, weight_ref, out_ref, att2
):
    att2[...] = (att2a[...] + att2b[...])[:, :SEG_DEV]
    scale = scale_ref[0:1, 0:1]
    weight = weight_ref[0:1, 0:1]
    src = (src0[...], src1[...] * scale, src2[...] * scale)
    att = (att0[...], att1[...] * scale, att2[...] * scale)
    out = jnp.where(lane_iota(1) == 0, jnp.sum(square_ref[...], keepdims=True), 0.0)
    for at, (one, two) in enumerate(((0, 0), (0, 1), (1, 1), (1, 2), (2, 2))):
        total = jnp.sum(src[one] * src[two], keepdims=True)
        total = total + weight * jnp.sum(att[one] * att[two], keepdims=True)
        out = jnp.where(lane_iota(1) == at + 1, total, out)
    out_ref[...] = jnp.broadcast_to(out, out_ref.shape)


def finish_kernel(
    dots_ref, scale_ref, src0, src1, src2, att0, att1, att2, sol_src, sol_att, dir_src, dir_att
):
    sums = jnp.sum(dots_ref[...], axis=0, keepdims=True)
    rhs_square, m0, m1, m2, m3, m4 = [lane_value(sums, at) for at in range(6)]
    scale = scale_ref[0:1, 0:1]
    mean = m1 / m0
    ww = m2 - mean * m1
    wz = m3 - 2.0 * mean * m2 + mean * mean * m1
    zz = m4 - 2.0 * mean * m3 + mean * mean * m2
    root0, root1 = jnp.sqrt(m0), jnp.sqrt(ww)
    beta1 = jnp.sqrt(rhs_square)
    alpha1 = root0 / beta1
    beta2 = jnp.sqrt(mean / scale - alpha1 * alpha1)
    cross = root1 / (scale * root0)
    alpha2 = cross / beta2
    quotient = wz / ww / scale
    beta3 = jnp.sqrt(quotient - alpha2 * alpha2)
    third = zz / ww / (scale * scale) - quotient * quotient - cross * cross
    alpha3 = jnp.sqrt(third) / beta3
    phi_bar, rho_bar = beta1, alpha1
    steps, turns = [], []
    for beta, alpha in ((beta2, alpha2), (beta3, alpha3)):
        rho = jnp.sqrt(rho_bar * rho_bar + beta * beta)
        cosine, sine = rho_bar / rho, beta / rho
        theta = sine * alpha
        rho_bar = -cosine * alpha
        steps.append(cosine * phi_bar / rho)
        turns.append(theta / rho)
        phi_bar = sine * phi_bar
    sides = (
        (src0, src1, src2, sol_src, dir_src),
        (att0, att1, att2, sol_att, dir_att),
    )
    for zero, one, two, sol, direction in sides:
        rows = sol.shape[0]
        base, once, twice = zero[0:rows], one[0:rows] * scale, two[0:rows] * scale
        v1 = base / root0
        v2 = (once - mean * base) / root1
        v3 = ((twice - mean * once) / (scale * root1) - quotient * v2 - cross * v1) / (
            beta3 * alpha3
        )
        turned = v2 - turns[0] * v1
        sol[...] = steps[0] * v1 + steps[1] * turned
        direction[...] = v3 - turns[1] * turned


def sds(shape, dtype=F32):
    return jax.ShapeDtypeStruct(shape, dtype)


def in_hbm(values):
    return pltpu.with_memory_space_constraint(values, pltpu.HBM)


def call(kernel, outs, scratch=(), limit=8, **more):
    return pl.pallas_call(
        kernel,
        out_shape=outs,
        scratch_shapes=list(scratch),
        compiler_params=pltpu.CompilerParams(vmem_limit_bytes=limit * MIB),
        **more,
    )


def on_device(src_design, att_design, right_side, block_source, block_segment, block_count):
    narrow, wide = lax.axis_size("narrow"), lax.axis_size("wide")
    devices = narrow * wide
    blocks = block_source.shape[0]
    tiles = blocks // LANE
    cap = blocks // narrow
    src_rows, att_rows = src_design.shape[0], att_design.shape[0]
    rows = src_rows + att_rows
    columns = right_side.shape[0] // LANE
    groups = columns // LANE
    obs = right_side.shape[0] // blocks

    def across(values, step):
        return lax.ppermute(values, "wide", [(i, i ^ step) for i in range(wide)])

    def exchange(values):
        return lax.all_to_all(values, "narrow", 0, 0)

    def far_sums(total):
        later, jump = None, 2
        while jump < wide:
            if later is not None:
                total = total + later
            later = across(total, jump)
            jump *= 2
        return total, jnp.zeros_like(total) if later is None else later

    tile_rows = lambda values: values.reshape(tiles, LANE)
    att_view = att_design.reshape(att_rows // 8, 8, columns, LANE).transpose(0, 2, 1, 3)
    src_view = src_design.reshape(src_rows, columns, LANE).transpose(1, 0, 2)

    right_shape = sds((HIGH, blocks), BF16)
    att_left = pltpu.VMEM((3 * 16 * SEG_DEV // HIGH, blocks), BF16)
    src_left = pltpu.VMEM((3 * 8 * SRC_DEV // HIGH, blocks), BF16)
    tile_int = sds((tiles, LANE), I32)
    send_shape = sds((narrow, 8, cap))
    att_shape = sds((16, SEG_DEV + LANE))
    src_shape = sds((8, SRC_DEV))
    table_shape = (tiles, rows, obs, LANE)
    table, square, pos, seg, order, att_right, part, send = call(
        functools.partial(start_kernel, narrow),
        (
            sds(table_shape),
            sds((8, LANE)),
            tile_int,
            tile_int,
            tile_int,
            right_shape,
            att_shape,
            send_shape,
        ),
        [
            pltpu.VMEM((groups, att_rows // 8, LANE, 8, LANE), F32),
            pltpu.VMEM((groups, LANE, 8, LANE), F32),
            pltpu.VMEM((groups, LANE, LANE), F32),
            pltpu.VMEM((tiles, LANE), I32),
            pltpu.VMEM((tiles, LANE), I32),
            pltpu.VMEM((tiles, LANE), I32),
            pltpu.VMEM((tiles, 24, LANE), F32),
            pltpu.VMEM((tiles, LANE), F32),
            att_left,
            pltpu.SemaphoreType.DMA((3, groups)),
            pltpu.SemaphoreType.DMA((3,)),
        ],
        in_specs=[pl.BlockSpec(memory_space=pltpu.HBM)] * 6,
        limit=20,
    )(
        *map(
            in_hbm,
            (
                att_view,
                src_view,
                right_side.reshape(columns, LANE),
                tile_rows(block_source),
                tile_rows(block_segment),
                tile_rows(block_count),
            ),
        )
    )

    results = []
    note = jnp.zeros((8, LANE), F32)
    owners = None
    for step in range(3):
        first_time, last_time = step == 0, step == 2
        other = across(part, 1)
        arrived = exchange(send)
        kernel = functools.partial(owner_kernel, narrow, first_time, last_time)
        if last_time:
            total, later = far_sums(part + other)
            src_sum = call(kernel, src_shape, [src_left])(arrived, *owners)
            results.append((src_sum, total, later))
            break
        outs = (src_shape, send_shape, att_shape)
        if first_time:
            src_sum, back, half, *owners = call(
                kernel, outs + (tile_int, right_shape), [src_left]
            )(arrived, part, other)
        else:
            src_sum, back, half, note = call(kernel, outs + (sds((8, LANE)),), [src_left])(
                arrived, part, other, *owners
            )
        total, later = far_sums(half)
        back = exchange(back)
        att_sum, part, send, scale = call(
            functools.partial(product_kernel, narrow, first_time),
            (sds((16, SEG_DEV)), att_shape, send_shape, sds((8, LANE))),
            [
                pltpu.VMEM((tiles, 24, LANE), F32),
                pltpu.VMEM((tiles, 24, LANE), F32),
                att_left,
            ],
        )(back, total, later, note, pos, seg, order, att_right, table)
        results.append((src_sum, att_sum))
    weight = jnp.where(lax.axis_index("wide") == 0, 1.0, 0.0).astype(F32) * jnp.ones((8, LANE), F32)
    (src0, att0), (src1, att1), (src2, att2a, att2b) = results
    dots, att2 = call(dots_kernel, (sds((devices, LANE)), sds((16, SEG_DEV))))(
        src0, src1, src2, att0, att1, att2a, att2b, square, scale, weight
    )
    dots = lax.all_to_all(dots, ("wide", "narrow"), 0, 0, tiled=True)
    sol_src, sol_att, dir_src, dir_att = call(
        finish_kernel,
        (
            sds((src_rows, SRC_DEV)),
            sds((att_rows, SEG_DEV)),
            sds((src_rows, SRC_DEV)),
            sds((att_rows, SEG_DEV)),
        ),
    )(dots, scale, src0, src1, src2, att0, att1, att2)
    return (sol_src, sol_att, dir_src, dir_att)


def solution(mesh):
    both = ("wide", "narrow")
    in_specs = (P(None, both), P(None, both), P(both), P(both), P(both), P(both))
    out_specs = (P(None, both), P(None, "narrow"), P(None, both), P(None, "narrow"))

    return jax.shard_map(
        on_device, mesh=mesh, in_specs=in_specs, out_specs=out_specs, check_vma=False
    )
```

```python
import functools

import jax
import jax.numpy as jnp
from jax import lax
from jax.experimental import pallas as pl
from jax.experimental.pallas import tpu as pltpu
from jax.sharding import PartitionSpec as P


SRC_DEV = 2048
SEG_DEV = 1024
LANE = 128
HIGH = 256
F32 = jnp.float32
BF16 = jnp.bfloat16
I32 = jnp.int32
MIB = 1 << 20


def lanes_of(values, index):
    return jnp.take_along_axis(values, index, axis=1, mode="promise_in_bounds")


def row_iota(rows, columns=LANE):
    return lax.broadcasted_iota(I32, (rows, columns), 0)


def lane_iota(rows, columns=LANE):
    return lax.broadcasted_iota(I32, (rows, columns), 1)


def to_tiles(rows):
    count = rows.shape[0]
    lane = lane_iota(count)
    first = lanes_of(rows, (2 * lane) % LANE)
    second = lanes_of(rows, (2 * lane + 1) % LANE)
    head = lane < LANE // 2
    even = jnp.where(head, first, pltpu.roll(first, count - 1, 0))
    odd = jnp.where(head, pltpu.roll(second, 1, 0), second)
    return jnp.where(row_iota(count) % 2 == 0, even, odd)


def split_three(values):
    top = values.astype(BF16).astype(F32)
    rest = values - top
    middle = rest.astype(BF16).astype(F32)
    return top, middle, rest - middle


def spread_rows(store, picked, row, column, levels):
    rows = picked.shape[0]
    size = levels * rows
    mask = jnp.where(row_iota(size) // rows == row, 1.0, 0.0).astype(BF16)
    for part, piece in enumerate(split_three(picked)):
        whole = jnp.concatenate([piece] * (16 // rows), axis=0).astype(BF16)
        whole = jnp.concatenate([whole] * (size // 16), axis=0)
        store[pl.ds(part * size, size), pl.ds(column, LANE)] = whole * mask


def rank_blocks(narrow, source_ref, segment_ref, pos_ref, seg_ref, order_ref, ids_ref, left, right):
    tiles = source_ref.shape[0]
    cap = tiles * LANE // narrow
    local = to_tiles(source_ref[...]) & (SRC_DEV * narrow - 1)
    seg_ref[...] = to_tiles(segment_ref[...]) & (SEG_DEV - 1)
    owner = local // SRC_DEV
    inner = local & (SRC_DEV - 1)
    marks = jnp.concatenate([jnp.where(owner == m, 1.0, 0.0) for m in range(narrow)], axis=0)
    marks = marks.astype(BF16)
    total = narrow * tiles
    before = jnp.where(row_iota(LANE) < lane_iota(LANE), 1.0, 0.0).astype(BF16)
    in_row = jnp.dot(marks, before, preferred_element_type=F32)
    at_row, at_lane = row_iota(total, total), lane_iota(total, total)
    earlier = (at_row // tiles == at_lane // tiles) & (at_lane < at_row)
    ahead = jnp.dot(jnp.where(earlier, 1.0, 0.0).astype(BF16), marks, preferred_element_type=F32)
    ahead = jnp.dot(ahead.astype(BF16), jnp.ones((LANE, LANE), BF16), preferred_element_type=F32)
    rank = (in_row + ahead).astype(I32)
    pos = jnp.zeros((tiles, LANE), I32)
    for m in range(narrow):
        pos = jnp.where(owner == m, m * cap + rank[m * tiles : (m + 1) * tiles], pos)
    pos_ref[...] = pos
    levels = tiles * LANE // HIGH
    lane = lane_iota(1).astype(F32)
    for t in range(tiles):
        here = pos[t : t + 1]
        level = row_iota(levels) == here // HIGH
        mine = inner[t : t + 1]
        pieces = (
            jnp.full((1, LANE), float(t), F32),
            lane,
            (mine // LANE).astype(F32),
            (mine % LANE).astype(F32),
        )
        for part, piece in enumerate(pieces):
            left[part * levels : (part + 1) * levels, t * LANE : (t + 1) * LANE] = jnp.where(
                level, piece, 0.0
            ).astype(BF16)
    mark_high(right, pos)
    found = jnp.dot(left[0 : 4 * levels, :], right[...], preferred_element_type=F32)
    tile_at, lane_at = found[:levels], found[levels : 2 * levels]
    order = (tile_at * LANE + lane_at).astype(I32)
    ids = found[2 * levels : 3 * levels] * LANE + found[3 * levels :]
    for level in range(levels):
        for half in range(HIGH // LANE):
            row = level * (HIGH // LANE) + half
            cut = slice(half * LANE, (half + 1) * LANE)
            order_ref[row : row + 1, :] = order[level : level + 1, cut]
            ids_ref[row : row + 1, :] = ids[level : level + 1, cut]


def mark_high(right, index):
    columns = (index & (HIGH - 1)).astype(F32).T
    high_at = lane_iota(LANE, HIGH).astype(F32).astype(BF16)
    one, zero = jnp.ones((), BF16), jnp.zeros((), BF16)
    for t in range(index.shape[0]):
        here = jnp.broadcast_to(columns[:, t : t + 1], (LANE, HIGH)).astype(BF16)
        right[t * LANE : (t + 1) * LANE, :] = jnp.where(high_at == here, one, zero)


def fill_att(blocks, seg_ref, left, t):
    here = seg_ref[pl.ds(t, 1), :]
    column = pl.multiple_of(t * LANE, LANE)
    spread_rows(left, blocks[t, 0:16, :], here // HIGH, column, SEG_DEV // HIGH)


def scatter_att(out_ref, left, right):
    levels = SEG_DEV // HIGH
    sums = jnp.dot(left[...], right[...], preferred_element_type=F32)
    size = 16 * levels
    sums = sums[:size] + (sums[size : 2 * size] + sums[2 * size :])
    for level in range(levels):
        out_ref[:, level * HIGH : (level + 1) * HIGH] = sums[level * 16 : (level + 1) * 16]


def pick(tables, count, index):
    low = index & (LANE - 1)
    high = index // LANE
    rows = tables(0).shape[0]
    low = jnp.broadcast_to(low, (rows, LANE))
    out = lanes_of(tables(0), low)
    for c in range(1, count):
        out = jnp.where(high == c, lanes_of(tables(c), low), out)
    return out


def send_sorted(narrow, blocks, order_ref, extra, out_ref):
    tiles = order_ref.shape[0]
    cap = tiles * LANE // narrow
    per = cap // LANE
    keep = row_iota(8) < 5
    for t in range(tiles):
        values = pick(lambda c: blocks[c, 16:24, :], tiles, order_ref[t : t + 1, :])
        values = jnp.where(keep, values, extra(t))
        out_ref[t // per, :, (t % per) * LANE : (t % per + 1) * LANE] = values


def entry(ref, per, t):
    return ref[t // per, :, (t % per) * LANE : (t % per + 1) * LANE]


def start_kernel(
    narrow,
    att_hbm, src_hbm, rhs_hbm, source_hbm, segment_hbm, count_hbm,
    table_ref, square_ref, pos_ref, seg_ref, order_ref, right, att_ref, send_ref,
    att_in, src_in, rhs_in, source_in, segment_in, count_in, blocks, ids, left, sems, int_sems,
):
    groups, att_sets = att_in.shape[0], att_in.shape[1]
    att_rows, src_rows = att_sets * 8, src_hbm.shape[1]
    att_flat = att_in.reshape(groups * att_sets * LANE * 8, LANE)
    src_flat = src_in.reshape(groups * LANE * 8, LANE)
    obs = table_ref.shape[2]

    def ints():
        pairs = ((source_hbm, source_in), (segment_hbm, segment_in), (count_hbm, count_in))
        return [
            pltpu.make_async_copy(one, two, int_sems.at[at]) for at, (one, two) in enumerate(pairs)
        ]

    def loads(g):
        cut = pl.ds(g * LANE, LANE)
        return [
            pltpu.make_async_copy(att_hbm.at[:, cut], att_in.at[g], sems.at[0, g]),
            pltpu.make_async_copy(src_hbm.at[cut], src_in.at[g, :, 0:src_rows], sems.at[1, g]),
            pltpu.make_async_copy(rhs_hbm.at[cut], rhs_in.at[g], sems.at[2, g]),
        ]

    def begin(g, carry):
        for one in loads(g):
            one.start()
        return carry

    for one in ints():
        one.start()
    lax.fori_loop(0, groups, begin, 0)
    for one in ints():
        one.wait()
    count_in[...] = to_tiles(count_in[...])
    square_ref[...] = jnp.zeros_like(square_ref)
    rank_blocks(narrow, source_in, segment_in, pos_ref, seg_ref, order_ref, ids, left, right)
    mark_high(right, seg_ref[...])
    place = row_iota(obs)

    def turn(g, carry):
        for half in range(2):
            fill_att(blocks, seg_ref, left, jnp.maximum(g * 2 - 2 + half, half))
        for one in loads(g):
            one.wait()
        wide_rhs = rhs_in[g].T
        live, rhs = [], []
        for half in range(2):
            alive = place < count_in[pl.ds(g * 2 + half, 1), :]
            live.append(alive)
            part = jnp.where(alive, wide_rhs[half * obs : half * obs + obs], 0.0)
            rhs.append(part)
            square = part * part
            total = square[0:8]
            for at in range(8, obs, 8):
                total = total + square[at : at + 8]
            square_ref[...] += total
        for i in range(att_rows + src_rows):
            if i < att_rows:
                base = pl.multiple_of((g * att_sets + i // 8) * (LANE * 8), LANE * 8)
                values = att_flat[pl.ds(base + i % 8, LANE, stride=8), :]
            else:
                base = pl.multiple_of(g * (LANE * 8), LANE * 8)
                values = src_flat[pl.ds(base + i - att_rows, LANE, stride=8), :]
            turned = values.T
            for half in range(2):
                part = jnp.where(live[half], turned[half * obs : half * obs + obs], 0.0)
                table_ref[g * 2 + half, i] = part
                blocks[g * 2 + half, i : i + 1, :] = jnp.sum(part * rhs[half], axis=0, keepdims=True)
        for half in range(2):
            rest = 24 - att_rows - src_rows
            blocks[g * 2 + half, 24 - rest : 24, :] = jnp.zeros((rest, LANE), F32)
        return carry

    lax.fori_loop(0, groups, turn, 0)
    for half in range(2):
        fill_att(blocks, seg_ref, left, groups * 2 - 2 + half)
    scatter_att(att_ref, left, right)
    lane = lane_iota(16)
    att_ref[:, SEG_DEV:] = jnp.where(lane == 0, jnp.sum(square_ref[...]), 0.0)
    row = row_iota(8)
    send_sorted(
        narrow,
        blocks,
        order_ref,
        lambda t: jnp.where(row == 5, ids[t : t + 1, :], 0.0),
        send_ref,
    )


def owner_kernel(narrow, first, last, *refs):
    if first:
        recv_ref, part_ref, other_ref, src_ref, back_ref, half_ref, index_ref, right, left = refs
    elif last:
        recv_ref, index_ref, right, src_ref, left = refs
    else:
        recv_ref, part_ref, other_ref, index_ref, right = refs[:5]
        src_ref, back_ref, half_ref, known_ref, left = refs[5:]
    if not last:
        half_ref[...] = part_ref[...] + other_ref[...]
    tiles, cap = index_ref.shape[0], recv_ref.shape[2]
    per = cap // LANE
    levels = SRC_DEV // HIGH
    keep = row_iota(8) < 5
    if first:
        for t in range(tiles):
            index_ref[t : t + 1, :] = entry(recv_ref, per, t)[5:6].astype(I32)
        mark_high(right, index_ref[...])
    elif not last:
        known = recv_ref[0, :, 0:LANE]
        for n in range(1, narrow):
            known = known + recv_ref[n, :, 0:LANE]
        known_ref[...] = known
    for t in range(tiles):
        here = index_ref[t : t + 1, :]
        values = jnp.where(keep, entry(recv_ref, per, t), 0.0)
        spread_rows(left, values, here // HIGH, t * LANE, levels)
    sums = jnp.dot(left[...], right[...], preferred_element_type=F32)
    size = 8 * levels
    sums = sums[:size] + (sums[size : 2 * size] + sums[2 * size :])
    for level in range(levels):
        src_ref[:, level * HIGH : (level + 1) * HIGH] = sums[level * 8 : (level + 1) * 8]
    if last:
        return
    square = jnp.sum(src_ref[...] * src_ref[...]) if first else 0.0
    mark = jnp.where((row_iota(8) == 6) & (lane_iota(8) == 0), square, 0.0)
    for t in range(tiles):
        values = pick(
            lambda c: src_ref[:, c * LANE : (c + 1) * LANE],
            SRC_DEV // LANE,
            index_ref[t : t + 1, :],
        )
        values = jnp.where(keep, values, mark)
        back_ref[t // per, :, (t % per) * LANE : (t % per + 1) * LANE] = values


def lane_value(row, at):
    return jnp.sum(jnp.where(lane_iota(1) == at, row, 0.0), axis=1, keepdims=True)


def product_kernel(
    narrow, first, recv_ref, half_ref, later_ref, known_ref, pos_ref, seg_ref, order_ref, right,
    table_ref, full_ref, att_ref, send_ref, scale_ref, vec, blocks, left,
):
    tiles, rows = pos_ref.shape[0], table_ref.shape[1]
    per = recv_ref.shape[2] // LANE
    full = half_ref[...] + later_ref[...]
    full_ref[...] = full[:, :SEG_DEV]
    notes = full[0:1, SEG_DEV:]
    lane, row = lane_iota(8), row_iota(8)
    send_note = jnp.zeros((8, LANE), F32)
    att_note = jnp.zeros((16, LANE), F32)
    if first:
        scale = jnp.ones((1, 1), F32)
        square_src = recv_ref[0, 6:7, 0:LANE]
        for n in range(1, narrow):
            square_src = square_src + recv_ref[n, 6:7, 0:LANE]
        att_note = jnp.where(lane_iota(16) == 1, lane_value(square_src, 0), 0.0)
        square_att = jnp.sum(full[:, :SEG_DEV] * full[:, :SEG_DEV], keepdims=True)
        send_note = jnp.where(lane == 0, lane_value(notes, 0), 0.0)
        send_note = jnp.where(lane == 1, square_att, send_note)
        send_note = jnp.where(row == 6, send_note, 0.0)
    else:
        known = known_ref[6:7, :]
        square = lane_value(notes, 1) + lane_value(known, 1)
        scale = lane_value(known, 0) / square
    scale_ref[...] = jnp.broadcast_to(scale, (8, LANE))
    att_ref[:, SEG_DEV:] = att_note

    def gather(t):
        where_att = seg_ref[pl.ds(t, 1), :]
        for top in range(0, 24, 8):
            if top < 16:
                picked = pick(
                    lambda c: full_ref[top : top + 8, c * LANE : (c + 1) * LANE],
                    SEG_DEV // LANE,
                    where_att,
                )
            else:
                picked = pick(lambda c: entry(recv_ref, per, c), tiles, pos_ref[pl.ds(t, 1), :])
            vec[t, top : top + 8, :] = picked if first else picked * scale

    def multiply(t, carry):
        fill_att(blocks, seg_ref, left, jnp.maximum(t - 1, 0))
        image = None
        for i in range(rows):
            part = table_ref[t, i] * vec[t, i : i + 1, :]
            image = part if image is None else image + part
        for i in range(rows):
            blocks[t, i : i + 1, :] = jnp.sum(table_ref[t, i] * image, axis=0, keepdims=True)
        blocks[t, rows:24, :] = jnp.zeros((24 - rows, LANE), F32)
        gather(jnp.minimum(t + 1, tiles - 1))
        return carry

    gather(0)
    lax.fori_loop(0, tiles, multiply, 0)
    fill_att(blocks, seg_ref, left, tiles - 1)
    scatter_att(att_ref, left, right)
    send_sorted(narrow, blocks, order_ref, lambda t: send_note, send_ref)


def dots_kernel(
    src0, src1, src2, att0, att1, att2a, att2b, square_ref, scale_ref, weight_ref, out_ref, att2
):
    att2[...] = (att2a[...] + att2b[...])[:, :SEG_DEV]
    scale = scale_ref[0:1, 0:1]
    weight = weight_ref[0:1, 0:1]
    src = (src0[...], src1[...] * scale, src2[...] * scale)
    att = (att0[...], att1[...] * scale, att2[...] * scale)
    out = jnp.where(lane_iota(1) == 0, jnp.sum(square_ref[...], keepdims=True), 0.0)
    for at, (one, two) in enumerate(((0, 0), (0, 1), (1, 1), (1, 2), (2, 2))):
        total = jnp.sum(src[one] * src[two], keepdims=True)
        total = total + weight * jnp.sum(att[one] * att[two], keepdims=True)
        out = jnp.where(lane_iota(1) == at + 1, total, out)
    out_ref[...] = jnp.broadcast_to(out, out_ref.shape)


def finish_kernel(
    dots_ref, scale_ref, src0, src1, src2, att0, att1, att2, sol_src, sol_att, dir_src, dir_att
):
    sums = jnp.sum(dots_ref[...], axis=0, keepdims=True)
    rhs_square, m0, m1, m2, m3, m4 = [lane_value(sums, at) for at in range(6)]
    scale = scale_ref[0:1, 0:1]
    mean = m1 / m0
    ww = m2 - mean * m1
    wz = m3 - 2.0 * mean * m2 + mean * mean * m1
    zz = m4 - 2.0 * mean * m3 + mean * mean * m2
    root0, root1 = jnp.sqrt(m0), jnp.sqrt(ww)
    beta1 = jnp.sqrt(rhs_square)
    alpha1 = root0 / beta1
    beta2 = jnp.sqrt(mean / scale - alpha1 * alpha1)
    cross = root1 / (scale * root0)
    alpha2 = cross / beta2
    quotient = wz / ww / scale
    beta3 = jnp.sqrt(quotient - alpha2 * alpha2)
    third = zz / ww / (scale * scale) - quotient * quotient - cross * cross
    alpha3 = jnp.sqrt(third) / beta3
    phi_bar, rho_bar = beta1, alpha1
    steps, turns = [], []
    for beta, alpha in ((beta2, alpha2), (beta3, alpha3)):
        rho = jnp.sqrt(rho_bar * rho_bar + beta * beta)
        cosine, sine = rho_bar / rho, beta / rho
        theta = sine * alpha
        rho_bar = -cosine * alpha
        steps.append(cosine * phi_bar / rho)
        turns.append(theta / rho)
        phi_bar = sine * phi_bar
    sides = (
        (src0, src1, src2, sol_src, dir_src),
        (att0, att1, att2, sol_att, dir_att),
    )
    for zero, one, two, sol, direction in sides:
        rows = sol.shape[0]
        base, once, twice = zero[0:rows], one[0:rows] * scale, two[0:rows] * scale
        v1 = base / root0
        v2 = (once - mean * base) / root1
        v3 = ((twice - mean * once) / (scale * root1) - quotient * v2 - cross * v1) / (
            beta3 * alpha3
        )
        turned = v2 - turns[0] * v1
        sol[...] = steps[0] * v1 + steps[1] * turned
        direction[...] = v3 - turns[1] * turned


def sds(shape, dtype=F32):
    return jax.ShapeDtypeStruct(shape, dtype)


def in_hbm(values):
    return pltpu.with_memory_space_constraint(values, pltpu.HBM)


def call(kernel, outs, scratch=(), limit=8, **more):
    return pl.pallas_call(
        kernel,
        out_shape=outs,
        scratch_shapes=list(scratch),
        compiler_params=pltpu.CompilerParams(vmem_limit_bytes=limit * MIB),
        **more,
    )


def on_device(src_design, att_design, right_side, block_source, block_segment, block_count):
    narrow, wide = lax.axis_size("narrow"), lax.axis_size("wide")
    devices = narrow * wide
    blocks = block_source.shape[0]
    tiles = blocks // LANE
    cap = blocks // narrow
    src_rows, att_rows = src_design.shape[0], att_design.shape[0]
    rows = src_rows + att_rows
    columns = right_side.shape[0] // LANE
    groups = columns // LANE
    obs = right_side.shape[0] // blocks

    def across(values, step):
        return lax.ppermute(values, "wide", [(i, i ^ step) for i in range(wide)])

    def exchange(values):
        return lax.all_to_all(values, "narrow", 0, 0)

    def far_sums(total):
        later, jump = None, 2
        while jump < wide:
            if later is not None:
                total = total + later
            later = across(total, jump)
            jump *= 2
        return total, jnp.zeros_like(total) if later is None else later

    tile_rows = lambda values: values.reshape(tiles, LANE)
    att_view = att_design.reshape(att_rows // 8, 8, columns, LANE).transpose(0, 2, 1, 3)
    src_view = src_design.reshape(src_rows, columns, LANE).transpose(1, 0, 2)

    right_shape = sds((blocks, HIGH), BF16)
    att_left = pltpu.VMEM((3 * 16 * SEG_DEV // HIGH, blocks), BF16)
    src_left = pltpu.VMEM((3 * 8 * SRC_DEV // HIGH, blocks), BF16)
    tile_int = sds((tiles, LANE), I32)
    send_shape = sds((narrow, 8, cap))
    att_shape = sds((16, SEG_DEV + LANE))
    src_shape = sds((8, SRC_DEV))
    table_shape = (tiles, rows, obs, LANE)
    table, square, pos, seg, order, att_right, part, send = call(
        functools.partial(start_kernel, narrow),
        (
            sds(table_shape),
            sds((8, LANE)),
            tile_int,
            tile_int,
            tile_int,
            right_shape,
            att_shape,
            send_shape,
        ),
        [
            pltpu.VMEM((groups, att_rows // 8, LANE, 8, LANE), F32),
            pltpu.VMEM((groups, LANE, 8, LANE), F32),
            pltpu.VMEM((groups, LANE, LANE), F32),
            pltpu.VMEM((tiles, LANE), I32),
            pltpu.VMEM((tiles, LANE), I32),
            pltpu.VMEM((tiles, LANE), I32),
            pltpu.VMEM((tiles, 24, LANE), F32),
            pltpu.VMEM((tiles, LANE), F32),
            att_left,
            pltpu.SemaphoreType.DMA((3, groups)),
            pltpu.SemaphoreType.DMA((3,)),
        ],
        in_specs=[pl.BlockSpec(memory_space=pltpu.HBM)] * 6,
        limit=20,
    )(
        *map(
            in_hbm,
            (
                att_view,
                src_view,
                right_side.reshape(columns, LANE),
                tile_rows(block_source),
                tile_rows(block_segment),
                tile_rows(block_count),
            ),
        )
    )

    results = []
    note = jnp.zeros((8, LANE), F32)
    owners = None
    for step in range(3):
        first_time, last_time = step == 0, step == 2
        other = across(part, 1)
        arrived = exchange(send)
        kernel = functools.partial(owner_kernel, narrow, first_time, last_time)
        if last_time:
            total, later = far_sums(part + other)
            src_sum = call(kernel, src_shape, [src_left])(arrived, *owners)
            results.append((src_sum, total, later))
            break
        outs = (src_shape, send_shape, att_shape)
        if first_time:
            src_sum, back, half, *owners = call(
                kernel, outs + (tile_int, right_shape), [src_left]
            )(arrived, part, other)
        else:
            src_sum, back, half, note = call(kernel, outs + (sds((8, LANE)),), [src_left])(
                arrived, part, other, *owners
            )
        total, later = far_sums(half)
        back = exchange(back)
        att_sum, part, send, scale = call(
            functools.partial(product_kernel, narrow, first_time),
            (sds((16, SEG_DEV)), att_shape, send_shape, sds((8, LANE))),
            [
                pltpu.VMEM((tiles, 24, LANE), F32),
                pltpu.VMEM((tiles, 24, LANE), F32),
                att_left,
            ],
        )(back, total, later, note, pos, seg, order, att_right, table)
        results.append((src_sum, att_sum))
    weight = jnp.where(lax.axis_index("wide") == 0, 1.0, 0.0).astype(F32) * jnp.ones((8, LANE), F32)
    (src0, att0), (src1, att1), (src2, att2a, att2b) = results
    dots, att2 = call(dots_kernel, (sds((devices, LANE)), sds((16, SEG_DEV))))(
        src0, src1, src2, att0, att1, att2a, att2b, square, scale, weight
    )
    dots = lax.all_to_all(dots, ("wide", "narrow"), 0, 0, tiled=True)
    sol_src, sol_att, dir_src, dir_att = call(
        finish_kernel,
        (
            sds((src_rows, SRC_DEV)),
            sds((att_rows, SEG_DEV)),
            sds((src_rows, SRC_DEV)),
            sds((att_rows, SEG_DEV)),
        ),
    )(dots, scale, src0, src1, src2, att0, att1, att2)
    return (sol_src, sol_att, dir_src, dir_att)


def solution(mesh):
    both = ("wide", "narrow")
    in_specs = (P(None, both), P(None, both), P(both), P(both), P(both), P(both))
    out_specs = (P(None, both), P(None, "narrow"), P(None, both), P(None, "narrow"))

    return jax.shard_map(
        on_device, mesh=mesh, in_specs=in_specs, out_specs=out_specs, check_vma=False
    )
```

```python
import functools

import jax
import jax.numpy as jnp
from jax import lax
from jax.experimental import pallas as pl
from jax.experimental.pallas import tpu as pltpu
from jax.sharding import PartitionSpec as P


SRC_DEV = 2048
SEG_DEV = 1024
LANE = 128
HIGH = 256
F32 = jnp.float32
BF16 = jnp.bfloat16
I32 = jnp.int32
MIB = 1 << 20


def lanes_of(values, index):
    return jnp.take_along_axis(values, index, axis=1, mode="promise_in_bounds")


def row_iota(rows, columns=LANE):
    return lax.broadcasted_iota(I32, (rows, columns), 0)


def lane_iota(rows, columns=LANE):
    return lax.broadcasted_iota(I32, (rows, columns), 1)


def to_tiles(rows):
    count = rows.shape[0]
    lane = lane_iota(count)
    first = lanes_of(rows, (2 * lane) % LANE)
    second = lanes_of(rows, (2 * lane + 1) % LANE)
    head = lane < LANE // 2
    even = jnp.where(head, first, pltpu.roll(first, count - 1, 0))
    odd = jnp.where(head, pltpu.roll(second, 1, 0), second)
    return jnp.where(row_iota(count) % 2 == 0, even, odd)


def split_three(values):
    top = values.astype(BF16).astype(F32)
    rest = values - top
    middle = rest.astype(BF16).astype(F32)
    return top, middle, rest - middle


def spread_rows(store, picked, row, column, levels):
    rows = picked.shape[0]
    size = levels * rows
    mask = jnp.where(row_iota(size) // rows == row, 1.0, 0.0).astype(BF16)
    for part, piece in enumerate(split_three(picked)):
        whole = jnp.concatenate([piece] * (16 // rows), axis=0).astype(BF16)
        whole = jnp.concatenate([whole] * (size // 16), axis=0)
        store[pl.ds(part * size, size), pl.ds(column, LANE)] = whole * mask


def fold_rows(values):
    total = values[0:8]
    for at in range(8, values.shape[0], 8):
        total = total + values[at : at + 8]
    return total


def row_sums(sums):
    rows = sums.shape[0] // 8
    total = sums[pl.ds(0, rows, stride=8), :]
    for at in range(1, 8):
        total = total + sums[pl.ds(at, rows, stride=8), :]
    return total


def rank_blocks(narrow, source_ref, segment_ref, pos_ref, seg_ref, order_ref, ids_ref, left, right):
    tiles = source_ref.shape[0]
    cap = tiles * LANE // narrow
    local = to_tiles(source_ref[...]) & (SRC_DEV * narrow - 1)
    seg_ref[...] = to_tiles(segment_ref[...]) & (SEG_DEV - 1)
    owner = local // SRC_DEV
    inner = local & (SRC_DEV - 1)
    marks = jnp.concatenate([jnp.where(owner == m, 1.0, 0.0) for m in range(narrow)], axis=0)
    marks = marks.astype(BF16)
    total = narrow * tiles
    before = jnp.where(row_iota(LANE) < lane_iota(LANE), 1.0, 0.0).astype(BF16)
    in_row = jnp.dot(marks, before, preferred_element_type=F32)
    at_row, at_lane = row_iota(total, total), lane_iota(total, total)
    earlier = (at_row // tiles == at_lane // tiles) & (at_lane < at_row)
    ahead = jnp.dot(jnp.where(earlier, 1.0, 0.0).astype(BF16), marks, preferred_element_type=F32)
    ahead = jnp.dot(ahead.astype(BF16), jnp.ones((LANE, LANE), BF16), preferred_element_type=F32)
    rank = (in_row + ahead).astype(I32)
    pos = jnp.zeros((tiles, LANE), I32)
    for m in range(narrow):
        pos = jnp.where(owner == m, m * cap + rank[m * tiles : (m + 1) * tiles], pos)
    pos_ref[...] = pos
    levels = tiles * LANE // HIGH
    lane = lane_iota(1).astype(F32)
    for t in range(tiles):
        here = pos[t : t + 1]
        level = row_iota(levels) == here // HIGH
        mine = inner[t : t + 1]
        pieces = (
            jnp.full((1, LANE), float(t), F32),
            lane,
            (mine // LANE).astype(F32),
            (mine % LANE).astype(F32),
        )
        for part, piece in enumerate(pieces):
            left[part * levels : (part + 1) * levels, t * LANE : (t + 1) * LANE] = jnp.where(
                level, piece, 0.0
            ).astype(BF16)
    mark_high(right, pos)
    found = jnp.dot(left[0 : 4 * levels, :], right[...], preferred_element_type=F32)
    tile_at, lane_at = found[:levels], found[levels : 2 * levels]
    order = (tile_at * LANE + lane_at).astype(I32)
    ids = found[2 * levels : 3 * levels] * LANE + found[3 * levels :]
    for level in range(levels):
        for half in range(HIGH // LANE):
            row = level * (HIGH // LANE) + half
            cut = slice(half * LANE, (half + 1) * LANE)
            order_ref[row : row + 1, :] = order[level : level + 1, cut]
            ids_ref[row : row + 1, :] = ids[level : level + 1, cut]


def mark_high(right, index):
    columns = (index & (HIGH - 1)).astype(F32).T
    high_at = lane_iota(LANE, HIGH).astype(F32).astype(BF16)
    one, zero = jnp.ones((), BF16), jnp.zeros((), BF16)
    for t in range(index.shape[0]):
        here = jnp.broadcast_to(columns[:, t : t + 1], (LANE, HIGH)).astype(BF16)
        right[t * LANE : (t + 1) * LANE, :] = jnp.where(high_at == here, one, zero)


def fill_att(blocks, seg_ref, left, t):
    here = seg_ref[pl.ds(t, 1), :]
    column = pl.multiple_of(t * LANE, LANE)
    spread_rows(left, blocks[t, 0:16, :], here // HIGH, column, SEG_DEV // HIGH)


def scatter_att(out_ref, left, right):
    levels = SEG_DEV // HIGH
    sums = jnp.dot(left[...], right[...], preferred_element_type=F32)
    size = 16 * levels
    sums = sums[:size] + (sums[size : 2 * size] + sums[2 * size :])
    for level in range(levels):
        out_ref[:, level * HIGH : (level + 1) * HIGH] = sums[level * 16 : (level + 1) * 16]


def pick(tables, count, index):
    low = index & (LANE - 1)
    high = index // LANE
    rows = tables(0).shape[0]
    low = jnp.broadcast_to(low, (rows, LANE))
    out = lanes_of(tables(0), low)
    for c in range(1, count):
        out = jnp.where(high == c, lanes_of(tables(c), low), out)
    return out


def send_sorted(narrow, blocks, order_ref, extra, out_ref):
    tiles = order_ref.shape[0]
    cap = tiles * LANE // narrow
    per = cap // LANE
    keep = row_iota(8) < 5
    for t in range(tiles):
        values = pick(lambda c: blocks[c, 16:24, :], tiles, order_ref[t : t + 1, :])
        values = jnp.where(keep, values, extra(t))
        out_ref[t // per, :, (t % per) * LANE : (t % per + 1) * LANE] = values


def entry(ref, per, t):
    return ref[t // per, :, (t % per) * LANE : (t % per + 1) * LANE]


def start_kernel(
    narrow,
    att_hbm, src_hbm, rhs_hbm, source_hbm, segment_hbm, count_hbm,
    table_ref, square_ref, pos_ref, seg_ref, order_ref, right, att_ref, send_ref,
    att_in, src_in, rhs_in, source_in, segment_in, count_in, blocks, ids, sums, left, sems, int_sems,
):
    groups, att_sets = att_in.shape[0], att_in.shape[1]
    att_rows, src_rows = att_sets * 8, src_hbm.shape[1]
    att_flat = att_in.reshape(groups * att_sets * LANE * 8, LANE)
    src_flat = src_in.reshape(groups * LANE * 8, LANE)
    obs = table_ref.shape[2]

    def ints():
        pairs = ((source_hbm, source_in), (segment_hbm, segment_in), (count_hbm, count_in))
        return [
            pltpu.make_async_copy(one, two, int_sems.at[at]) for at, (one, two) in enumerate(pairs)
        ]

    def loads(g):
        cut = pl.ds(g * LANE, LANE)
        return [
            pltpu.make_async_copy(att_hbm.at[:, cut], att_in.at[g], sems.at[0, g]),
            pltpu.make_async_copy(src_hbm.at[cut], src_in.at[g, :, 0:src_rows], sems.at[1, g]),
            pltpu.make_async_copy(rhs_hbm.at[cut], rhs_in.at[g], sems.at[2, g]),
        ]

    def begin(g, carry):
        for one in loads(g):
            one.start()
        return carry

    for one in ints():
        one.start()
    lax.fori_loop(0, groups, begin, 0)
    for one in ints():
        one.wait()
    count_in[...] = to_tiles(count_in[...])
    square_ref[...] = jnp.zeros_like(square_ref)
    sums[...] = jnp.zeros_like(sums)
    rank_blocks(narrow, source_in, segment_in, pos_ref, seg_ref, order_ref, ids, left, right)
    mark_high(right, seg_ref[...])
    place = row_iota(obs)

    def turn(g, carry):
        for half in range(2):
            fill_att(blocks, seg_ref, left, jnp.maximum(g * 2 - 2 + half, half))
        for one in loads(g):
            one.wait()
        wide_rhs = rhs_in[g].T
        live, rhs = [], []
        for half in range(2):
            alive = place < count_in[pl.ds(g * 2 + half, 1), :]
            live.append(alive)
            part = jnp.where(alive, wide_rhs[half * obs : half * obs + obs], 0.0)
            rhs.append(part)
            square_ref[...] += fold_rows(part * part)
        for i in range(att_rows + src_rows):
            if i < att_rows:
                base = pl.multiple_of((g * att_sets + i // 8) * (LANE * 8), LANE * 8)
                values = att_flat[pl.ds(base + i % 8, LANE, stride=8), :]
            else:
                base = pl.multiple_of(g * (LANE * 8), LANE * 8)
                values = src_flat[pl.ds(base + i - att_rows, LANE, stride=8), :]
            turned = values.T
            for half in range(2):
                part = jnp.where(live[half], turned[half * obs : half * obs + obs], 0.0)
                table_ref[g * 2 + half, i] = part
                sums[half, i * 8 : i * 8 + 8, :] = fold_rows(part * rhs[half])
        for half in range(2):
            blocks[g * 2 + half] = row_sums(sums.at[half])
        return carry

    lax.fori_loop(0, groups, turn, 0)
    for half in range(2):
        fill_att(blocks, seg_ref, left, groups * 2 - 2 + half)
    scatter_att(att_ref, left, right)
    lane = lane_iota(16)
    att_ref[:, SEG_DEV:] = jnp.where(lane == 0, jnp.sum(square_ref[...]), 0.0)
    row = row_iota(8)
    send_sorted(
        narrow,
        blocks,
        order_ref,
        lambda t: jnp.where(row == 5, ids[t : t + 1, :], 0.0),
        send_ref,
    )


def owner_kernel(narrow, first, last, *refs):
    if first:
        recv_ref, part_ref, other_ref, src_ref, back_ref, half_ref, index_ref, right, left = refs
    elif last:
        recv_ref, index_ref, right, src_ref, left = refs
    else:
        recv_ref, part_ref, other_ref, index_ref, right = refs[:5]
        src_ref, back_ref, half_ref, known_ref, left = refs[5:]
    if not last:
        half_ref[...] = part_ref[...] + other_ref[...]
    tiles, cap = index_ref.shape[0], recv_ref.shape[2]
    per = cap // LANE
    levels = SRC_DEV // HIGH
    keep = row_iota(8) < 5
    if first:
        for t in range(tiles):
            index_ref[t : t + 1, :] = entry(recv_ref, per, t)[5:6].astype(I32)
        mark_high(right, index_ref[...])
    elif not last:
        known = recv_ref[0, :, 0:LANE]
        for n in range(1, narrow):
            known = known + recv_ref[n, :, 0:LANE]
        known_ref[...] = known
    for t in range(tiles):
        here = index_ref[t : t + 1, :]
        values = jnp.where(keep, entry(recv_ref, per, t), 0.0)
        spread_rows(left, values, here // HIGH, t * LANE, levels)
    sums = jnp.dot(left[...], right[...], preferred_element_type=F32)
    size = 8 * levels
    sums = sums[:size] + (sums[size : 2 * size] + sums[2 * size :])
    for level in range(levels):
        src_ref[:, level * HIGH : (level + 1) * HIGH] = sums[level * 8 : (level + 1) * 8]
    if last:
        return
    square = jnp.sum(src_ref[...] * src_ref[...]) if first else 0.0
    mark = jnp.where((row_iota(8) == 6) & (lane_iota(8) == 0), square, 0.0)
    for t in range(tiles):
        values = pick(
            lambda c: src_ref[:, c * LANE : (c + 1) * LANE],
            SRC_DEV // LANE,
            index_ref[t : t + 1, :],
        )
        values = jnp.where(keep, values, mark)
        back_ref[t // per, :, (t % per) * LANE : (t % per + 1) * LANE] = values


def lane_value(row, at):
    return jnp.sum(jnp.where(lane_iota(1) == at, row, 0.0), axis=1, keepdims=True)


def product_kernel(
    narrow, first, recv_ref, half_ref, later_ref, known_ref, pos_ref, seg_ref, order_ref, right,
    table_ref, full_ref, att_ref, sent_ref, scale_ref, vec, blocks, sums, left, *own,
):
    send_ref = sent_ref if first else own[0]
    tiles, rows = pos_ref.shape[0], table_ref.shape[1]
    per = recv_ref.shape[2] // LANE
    full = half_ref[...] + later_ref[...]
    full_ref[...] = full[:, :SEG_DEV]
    notes = full[0:1, SEG_DEV:]
    lane, row = lane_iota(8), row_iota(8)
    send_note = jnp.zeros((8, LANE), F32)
    att_note = jnp.zeros((16, LANE), F32)
    if first:
        scale = jnp.ones((1, 1), F32)
        square_src = recv_ref[0, 6:7, 0:LANE]
        for n in range(1, narrow):
            square_src = square_src + recv_ref[n, 6:7, 0:LANE]
        att_note = jnp.where(lane_iota(16) == 1, lane_value(square_src, 0), 0.0)
        square_att = jnp.sum(full[:, :SEG_DEV] * full[:, :SEG_DEV], keepdims=True)
        send_note = jnp.where(lane == 0, lane_value(notes, 0), 0.0)
        send_note = jnp.where(lane == 1, square_att, send_note)
        send_note = jnp.where(row == 6, send_note, 0.0)
    else:
        known = known_ref[6:7, :]
        square = lane_value(notes, 1) + lane_value(known, 1)
        scale = lane_value(known, 0) / square
    scale_ref[...] = jnp.broadcast_to(scale, (8, LANE))
    att_ref[:, SEG_DEV:] = att_note

    def gather(t):
        where_att = seg_ref[pl.ds(t, 1), :]
        for top in range(0, 24, 8):
            if top < 16:
                picked = pick(
                    lambda c: full_ref[top : top + 8, c * LANE : (c + 1) * LANE],
                    SEG_DEV // LANE,
                    where_att,
                )
            else:
                picked = pick(lambda c: entry(recv_ref, per, c), tiles, pos_ref[pl.ds(t, 1), :])
            vec[t, top : top + 8, :] = picked if first else picked * scale

    def multiply(t, carry):
        fill_att(blocks, seg_ref, left, jnp.maximum(t - 1, 0))
        image = None
        for i in range(rows):
            part = table_ref[t, i] * vec[t, i : i + 1, :]
            image = part if image is None else image + part
        for i in range(rows):
            sums[i * 8 : i * 8 + 8, :] = fold_rows(table_ref[t, i] * image)
        blocks[t] = row_sums(sums)
        gather(jnp.minimum(t + 1, tiles - 1))
        return carry

    sums[...] = jnp.zeros_like(sums)
    gather(0)
    lax.fori_loop(0, tiles, multiply, 0)
    send_sorted(narrow, blocks, order_ref, lambda t: send_note, send_ref)
    if not first:
        sending = pltpu.make_async_copy(send_ref, sent_ref, own[1])
        sending.start()
    fill_att(blocks, seg_ref, left, tiles - 1)
    scatter_att(att_ref, left, right)
    if not first:
        sending.wait()


def dots_kernel(
    src0, src1, src2, att0, att1, mine, later, square_ref, scale_ref, side_ref, out_ref, kept_ref
):
    kept_ref[...] = mine[...] + later[...]
    scale = scale_ref[0:1, 0:1]
    upper, weight = side_ref[0:1, 0:1] > 0.5, side_ref[1:2, 0:1]
    half = kept_ref.shape[1]

    def own_half(ref):
        return jnp.where(upper, ref[:, half:], ref[:, :half])

    src = (src0[...], src1[...] * scale, src2[...] * scale)
    att = (own_half(att0), own_half(att1) * scale, kept_ref[...] * scale)
    out = jnp.where(lane_iota(1) == 0, jnp.sum(square_ref[...], keepdims=True), 0.0)
    for at, (one, two) in enumerate(((0, 0), (0, 1), (1, 1), (1, 2), (2, 2))):
        total = jnp.sum(src[one] * src[two], keepdims=True)
        total = total + weight * jnp.sum(att[one] * att[two], keepdims=True)
        out = jnp.where(lane_iota(1) == at + 1, total, out)
    out_ref[...] = jnp.broadcast_to(out, out_ref.shape)


def finish_kernel(
    dots_ref, scale_ref, side_ref, src0, src1, src2, att0, att1, kept, back,
    sol_src, sol_att, dir_src, dir_att, att2,
):
    upper = side_ref[0:1, 0:1] > 0.5
    half = kept.shape[1]
    att2[:, :half] = jnp.where(upper, back[...], kept[...])
    att2[:, half:] = jnp.where(upper, kept[...], back[...])
    sums = jnp.sum(dots_ref[...], axis=0, keepdims=True)
    rhs_square, m0, m1, m2, m3, m4 = [lane_value(sums, at) for at in range(6)]
    scale = scale_ref[0:1, 0:1]
    mean = m1 / m0
    ww = m2 - mean * m1
    wz = m3 - 2.0 * mean * m2 + mean * mean * m1
    zz = m4 - 2.0 * mean * m3 + mean * mean * m2
    root0, root1 = jnp.sqrt(m0), jnp.sqrt(ww)
    beta1 = jnp.sqrt(rhs_square)
    alpha1 = root0 / beta1
    beta2 = jnp.sqrt(mean / scale - alpha1 * alpha1)
    cross = root1 / (scale * root0)
    alpha2 = cross / beta2
    quotient = wz / ww / scale
    beta3 = jnp.sqrt(quotient - alpha2 * alpha2)
    third = zz / ww / (scale * scale) - quotient * quotient - cross * cross
    alpha3 = jnp.sqrt(third) / beta3
    phi_bar, rho_bar = beta1, alpha1
    steps, turns = [], []
    for beta, alpha in ((beta2, alpha2), (beta3, alpha3)):
        rho = jnp.sqrt(rho_bar * rho_bar + beta * beta)
        cosine, sine = rho_bar / rho, beta / rho
        theta = sine * alpha
        rho_bar = -cosine * alpha
        steps.append(cosine * phi_bar / rho)
        turns.append(theta / rho)
        phi_bar = sine * phi_bar
    sides = (
        (src0, src1, src2, sol_src, dir_src),
        (att0, att1, att2, sol_att, dir_att),
    )
    for zero, one, two, sol, direction in sides:
        rows = sol.shape[0]
        base, once, twice = zero[0:rows], one[0:rows] * scale, two[0:rows] * scale
        v1 = base / root0
        v2 = (once - mean * base) / root1
        v3 = ((twice - mean * once) / (scale * root1) - quotient * v2 - cross * v1) / (
            beta3 * alpha3
        )
        turned = v2 - turns[0] * v1
        sol[...] = steps[0] * v1 + steps[1] * turned
        direction[...] = v3 - turns[1] * turned


def sds(shape, dtype=F32):
    return jax.ShapeDtypeStruct(shape, dtype)


def in_hbm(values):
    return pltpu.with_memory_space_constraint(values, pltpu.HBM)


def call(kernel, outs, scratch=(), limit=8, **more):
    return pl.pallas_call(
        kernel,
        out_shape=outs,
        scratch_shapes=list(scratch),
        compiler_params=pltpu.CompilerParams(vmem_limit_bytes=limit * MIB),
        **more,
    )


def on_device(src_design, att_design, right_side, block_source, block_segment, block_count):
    narrow, wide = lax.axis_size("narrow"), lax.axis_size("wide")
    devices = narrow * wide
    blocks = block_source.shape[0]
    tiles = blocks // LANE
    cap = blocks // narrow
    src_rows, att_rows = src_design.shape[0], att_design.shape[0]
    rows = src_rows + att_rows
    columns = right_side.shape[0] // LANE
    groups = columns // LANE
    obs = right_side.shape[0] // blocks

    def across(values, step):
        return lax.ppermute(values, "wide", [(i, i ^ step) for i in range(wide)])

    def exchange(values):
        return lax.all_to_all(values, "narrow", 0, 0)

    def far_sums(total, end):
        later, jump = None, 2
        while jump < end:
            if later is not None:
                total = total + later
            later = across(total, jump)
            jump *= 2
        return total, later

    upper = lax.axis_index("wide") >= wide // 2

    tile_rows = lambda values: values.reshape(tiles, LANE)
    att_view = att_design.reshape(att_rows // 8, 8, columns, LANE).transpose(0, 2, 1, 3)
    src_view = src_design.reshape(src_rows, columns, LANE).transpose(1, 0, 2)

    right_shape = sds((blocks, HIGH), BF16)
    att_left = pltpu.VMEM((3 * 16 * SEG_DEV // HIGH, blocks), BF16)
    src_left = pltpu.VMEM((3 * 8 * SRC_DEV // HIGH, blocks), BF16)
    tile_int = sds((tiles, LANE), I32)
    send_shape = sds((narrow, 8, cap))
    att_shape = sds((16, SEG_DEV + LANE))
    src_shape = sds((8, SRC_DEV))
    table_shape = (tiles, rows, obs, LANE)
    table, square, pos, seg, order, att_right, part, send = call(
        functools.partial(start_kernel, narrow),
        (
            sds(table_shape),
            sds((8, LANE)),
            tile_int,
            tile_int,
            tile_int,
            right_shape,
            att_shape,
            send_shape,
        ),
        [
            pltpu.VMEM((groups, att_rows // 8, LANE, 8, LANE), F32),
            pltpu.VMEM((groups, LANE, 8, LANE), F32),
            pltpu.VMEM((groups, LANE, LANE), F32),
            pltpu.VMEM((tiles, LANE), I32),
            pltpu.VMEM((tiles, LANE), I32),
            pltpu.VMEM((tiles, LANE), I32),
            pltpu.VMEM((tiles, 24, LANE), F32),
            pltpu.VMEM((tiles, LANE), F32),
            pltpu.VMEM((2, 24 * 8, LANE), F32),
            att_left,
            pltpu.SemaphoreType.DMA((3, groups)),
            pltpu.SemaphoreType.DMA((3,)),
        ],
        in_specs=[pl.BlockSpec(memory_space=pltpu.HBM)] * 6,
        limit=20,
    )(
        *map(
            in_hbm,
            (
                att_view,
                src_view,
                right_side.reshape(columns, LANE),
                tile_rows(block_source),
                tile_rows(block_segment),
                tile_rows(block_count),
            ),
        )
    )

    results = []
    note = jnp.zeros((8, LANE), F32)
    owners = None
    for step in range(3):
        first_time, last_time = step == 0, step == 2
        other = across(part, 1)
        arrived = exchange(send)
        kernel = functools.partial(owner_kernel, narrow, first_time, last_time)
        if last_time:
            total, later = far_sums(part + other, wide // 2)
            if later is not None:
                total = total + later
            low, high = total[:, : SEG_DEV // 2], total[:, SEG_DEV // 2 : SEG_DEV]
            mine, other = jnp.where(upper, high, low), jnp.where(upper, low, high)
            later = across(other, wide // 2)
            src_sum = call(kernel, src_shape, [src_left])(arrived, *owners)
            results.append((src_sum, mine, later))
            break
        outs = (src_shape, send_shape, att_shape)
        if first_time:
            src_sum, back, half, *owners = call(
                kernel, outs + (tile_int, right_shape), [src_left]
            )(arrived, part, other)
        else:
            src_sum, back, half, note = call(kernel, outs + (sds((8, LANE)),), [src_left])(
                arrived, part, other, *owners
            )
        total, later = far_sums(half, wide)
        back = exchange(back)
        own, specs = [], {}
        if not first_time:
            in_vmem = pl.BlockSpec(memory_space=pltpu.VMEM)
            own = [pltpu.VMEM(send_shape.shape, F32), pltpu.SemaphoreType.DMA(())]
            specs = dict(
                out_specs=(in_vmem, in_vmem, pl.BlockSpec(memory_space=pltpu.HBM), in_vmem)
            )
        att_sum, part, send, scale = call(
            functools.partial(product_kernel, narrow, first_time),
            (
                sds((16, SEG_DEV)),
                att_shape,
                send_shape if first_time else pltpu.HBM(send_shape.shape, F32),
                sds((8, LANE)),
            ),
            [
                pltpu.VMEM((tiles, 24, LANE), F32),
                pltpu.VMEM((tiles, 24, LANE), F32),
                pltpu.VMEM((24 * 8, LANE), F32),
                att_left,
            ]
            + own,
            **specs,
        )(back, total, later, note, pos, seg, order, att_right, table)
        results.append((src_sum, att_sum))
    counted = lax.axis_index("wide") % (wide // 2) == 0
    side = jnp.where(row_iota(8) == 0, upper, counted).astype(F32)
    (src0, att0), (src1, att1), (src2, mine, later) = results
    dots, kept = call(dots_kernel, (sds((devices, LANE)), sds((16, SEG_DEV // 2))))(
        src0, src1, src2, att0, att1, mine, later, square, scale, side
    )
    dots = lax.all_to_all(dots, ("wide", "narrow"), 0, 0, tiled=True)
    back = across(kept, wide // 2)
    sol_src, sol_att, dir_src, dir_att = call(
        finish_kernel,
        (
            sds((src_rows, SRC_DEV)),
            sds((att_rows, SEG_DEV)),
            sds((src_rows, SRC_DEV)),
            sds((att_rows, SEG_DEV)),
        ),
        [pltpu.VMEM((16, SEG_DEV), F32)],
    )(dots, scale, side, src0, src1, src2, att0, att1, kept, back)
    return (sol_src, sol_att, dir_src, dir_att)


def solution(mesh):
    both = ("wide", "narrow")
    in_specs = (P(None, both), P(None, both), P(both), P(both), P(both), P(both))
    out_specs = (P(None, both), P(None, "narrow"), P(None, both), P(None, "narrow"))

    return jax.shard_map(
        on_device, mesh=mesh, in_specs=in_specs, out_specs=out_specs, check_vma=False
    )
```

```python
import functools

import jax
import jax.numpy as jnp
from jax import lax
from jax.experimental import pallas as pl
from jax.experimental.pallas import tpu as pltpu
from jax.sharding import PartitionSpec as P


SRC_DEV = 2048
SEG_DEV = 1024
LANE = 128
HIGH = 256
F32 = jnp.float32
BF16 = jnp.bfloat16
I32 = jnp.int32
MIB = 1 << 20
PERIOD = 7


def lanes_of(values, index):
    return jnp.take_along_axis(values, index, axis=1, mode="promise_in_bounds")


def row_iota(rows, columns=LANE):
    return lax.broadcasted_iota(I32, (rows, columns), 0)


def lane_iota(rows, columns=LANE):
    return lax.broadcasted_iota(I32, (rows, columns), 1)


def to_tiles(rows):
    count = rows.shape[0]
    lane = lane_iota(count)
    first = lanes_of(rows, (2 * lane) % LANE)
    second = lanes_of(rows, (2 * lane + 1) % LANE)
    head = lane < LANE // 2
    even = jnp.where(head, first, pltpu.roll(first, count - 1, 0))
    odd = jnp.where(head, pltpu.roll(second, 1, 0), second)
    return jnp.where(row_iota(count) % 2 == 0, even, odd)


def split_three(values):
    top = values.astype(BF16).astype(F32)
    rest = values - top
    middle = rest.astype(BF16).astype(F32)
    return top, middle, rest - middle


def spread_rows(store, picked, row, column, levels):
    rows = picked.shape[0]
    size = levels * rows
    levels_at = (row_iota(size) // rows).astype(F32).astype(BF16)
    named = jnp.broadcast_to(row.astype(F32), (size, LANE)).astype(BF16)
    mask = jnp.where(levels_at == named, jnp.ones((), BF16), jnp.zeros((), BF16))
    for part, piece in enumerate(split_three(picked)):
        whole = jnp.concatenate([piece] * (16 // rows), axis=0).astype(BF16)
        whole = jnp.concatenate([whole] * (size // 16), axis=0)
        store[pl.ds(part * size, size), pl.ds(column, LANE)] = whole * mask


def fold_rows(values):
    total = values[0:8]
    for at in range(8, values.shape[0], 8):
        total = total + values[at : at + 8]
    return total


def row_sums(sums):
    rows = sums.shape[0] // 8
    total = sums[pl.ds(0, rows, stride=8), :]
    for at in range(1, 8):
        total = total + sums[pl.ds(at, rows, stride=8), :]
    return total


def rank_blocks(narrow, source_ref, segment_ref, pos_ref, seg_ref, order_ref, ids_ref, left, right):
    tiles = source_ref.shape[0]
    cap = tiles * LANE // narrow
    local = to_tiles(source_ref[...]) & (SRC_DEV * narrow - 1)
    seg_ref[...] = to_tiles(segment_ref[...]) & (SEG_DEV - 1)
    owner = local // SRC_DEV
    inner = local & (SRC_DEV - 1)
    marks = jnp.concatenate([jnp.where(owner == m, 1.0, 0.0) for m in range(narrow)], axis=0)
    marks = marks.astype(BF16)
    total = narrow * tiles
    before = jnp.where(row_iota(LANE) < lane_iota(LANE), 1.0, 0.0).astype(BF16)
    in_row = jnp.dot(marks, before, preferred_element_type=F32)
    at_row, at_lane = row_iota(total, total), lane_iota(total, total)
    earlier = (at_row // tiles == at_lane // tiles) & (at_lane < at_row)
    ahead = jnp.dot(jnp.where(earlier, 1.0, 0.0).astype(BF16), marks, preferred_element_type=F32)
    ahead = jnp.dot(ahead.astype(BF16), jnp.ones((LANE, LANE), BF16), preferred_element_type=F32)
    rank = (in_row + ahead).astype(I32)
    pos = jnp.zeros((tiles, LANE), I32)
    for m in range(narrow):
        pos = jnp.where(owner == m, m * cap + rank[m * tiles : (m + 1) * tiles], pos)
    pos_ref[...] = pos
    levels = tiles * LANE // HIGH
    lane = lane_iota(1).astype(F32)
    for t in range(tiles):
        here = pos[t : t + 1]
        level = row_iota(levels) == here // HIGH
        mine = inner[t : t + 1]
        pieces = (
            jnp.full((1, LANE), float(t), F32),
            lane,
            (mine // LANE).astype(F32),
            (mine % LANE).astype(F32),
        )
        for part, piece in enumerate(pieces):
            left[part * levels : (part + 1) * levels, t * LANE : (t + 1) * LANE] = jnp.where(
                level, piece, 0.0
            ).astype(BF16)
    mark_high(right, pos)
    found = jnp.dot(left[0 : 4 * levels, :], right[...], preferred_element_type=F32)
    tile_at, lane_at = found[:levels], found[levels : 2 * levels]
    order = (tile_at * LANE + lane_at).astype(I32)
    ids = found[2 * levels : 3 * levels] * LANE + found[3 * levels :]
    for level in range(levels):
        for half in range(HIGH // LANE):
            row = level * (HIGH // LANE) + half
            cut = slice(half * LANE, (half + 1) * LANE)
            order_ref[row : row + 1, :] = order[level : level + 1, cut]
            ids_ref[row : row + 1, :] = ids[level : level + 1, cut]


def mark_high(right, index):
    columns = (index & (HIGH - 1)).astype(F32).T
    high_at = lane_iota(LANE, HIGH).astype(F32).astype(BF16)
    one, zero = jnp.ones((), BF16), jnp.zeros((), BF16)
    for t in range(index.shape[0]):
        here = jnp.broadcast_to(columns[:, t : t + 1], (LANE, HIGH)).astype(BF16)
        right[t * LANE : (t + 1) * LANE, :] = jnp.where(high_at == here, one, zero)


def fill_att(blocks, seg_ref, left, t):
    here = seg_ref[pl.ds(t, 1), :]
    column = pl.multiple_of(t * LANE, LANE)
    spread_rows(left, blocks[t, 0:16, :], here // HIGH, column, SEG_DEV // HIGH)


def scatter_att(out_ref, left, right):
    levels = SEG_DEV // HIGH
    sums = jnp.dot(left[...], right[...], preferred_element_type=F32)
    size = 16 * levels
    sums = sums[:size] + (sums[size : 2 * size] + sums[2 * size :])
    for level in range(levels):
        out_ref[:, level * HIGH : (level + 1) * HIGH] = sums[level * 16 : (level + 1) * 16]


def pick(tables, count, index):
    low = index & (LANE - 1)
    high = index // LANE
    rows = tables(0).shape[0]
    low = jnp.broadcast_to(low, (rows, LANE))
    out = lanes_of(tables(0), low)
    for c in range(1, count):
        out = jnp.where(high == c, lanes_of(tables(c), low), out)
    return out


def send_sorted(narrow, blocks, order_ref, extra, out_ref):
    tiles = order_ref.shape[0]
    cap = tiles * LANE // narrow
    per = cap // LANE
    keep = row_iota(8) < 5
    for t in range(tiles):
        values = pick(lambda c: blocks[c, 16:24, :], tiles, order_ref[t : t + 1, :])
        values = jnp.where(keep, values, extra(t))
        out_ref[t // per, :, (t % per) * LANE : (t % per + 1) * LANE] = values


def entry(ref, per, t):
    return ref[t // per, :, (t % per) * LANE : (t % per + 1) * LANE]


def start_kernel(
    narrow,
    att_hbm, src_hbm, rhs_hbm, source_hbm, segment_hbm, count_hbm,
    table_ref, square_ref, pos_ref, seg_ref, order_ref, right, att_ref, send_ref,
    att_in, src_in, rhs_in, source_in, segment_in, count_in, blocks, ids, sums, same, left, sems, int_sems,
):
    groups, att_sets = att_in.shape[0], att_in.shape[1]
    att_rows, src_rows = att_sets * 8, src_hbm.shape[1]
    att_flat = att_in.reshape(groups * att_sets * LANE * 8, LANE)
    src_flat = src_in.reshape(groups * LANE * 8, LANE)
    obs = table_ref.shape[2]

    def ints():
        pairs = ((source_hbm, source_in), (segment_hbm, segment_in), (count_hbm, count_in))
        return [
            pltpu.make_async_copy(one, two, int_sems.at[at]) for at, (one, two) in enumerate(pairs)
        ]

    def loads(g):
        cut = pl.ds(g * LANE, LANE)
        return [
            pltpu.make_async_copy(att_hbm.at[:, cut], att_in.at[g], sems.at[0, g]),
            pltpu.make_async_copy(src_hbm.at[cut], src_in.at[g, :, 0:src_rows], sems.at[1, g]),
            pltpu.make_async_copy(rhs_hbm.at[cut], rhs_in.at[g], sems.at[2, g]),
        ]

    def begin(g, carry):
        for one in loads(g):
            one.start()
        return carry

    for one in ints():
        one.start()
    lax.fori_loop(0, groups, begin, 0)
    for one in ints():
        one.wait()
    count_in[...] = to_tiles(count_in[...])
    square_ref[...] = jnp.zeros_like(square_ref)
    sums[...] = jnp.zeros_like(sums)
    diagonal = jnp.where(row_iota(LANE) == lane_iota(LANE), 1.0, 0.0).astype(BF16)
    for part in range(3):
        same[:, part * LANE : (part + 1) * LANE] = diagonal
    rank_blocks(narrow, source_in, segment_in, pos_ref, seg_ref, order_ref, ids, left, right)
    mark_high(right, seg_ref[...])
    place = row_iota(obs)

    def turn(g, carry):
        for half in range(2):
            fill_att(blocks, seg_ref, left, jnp.maximum(g * 2 - 2 + half, half))
        for one in loads(g):
            one.wait()
        wide_rhs = rhs_in[g].T
        live, rhs = [], []
        for half in range(2):
            alive = place < count_in[pl.ds(g * 2 + half, 1), :]
            live.append(alive)
            part = jnp.where(alive, wide_rhs[half * obs : half * obs + obs], 0.0)
            rhs.append(part)
            square_ref[...] += fold_rows(part * part)

        def rows_of(i):
            if i < att_rows:
                base = pl.multiple_of((g * att_sets + i // 8) * (LANE * 8), LANE * 8)
                return att_flat[pl.ds(base + i % 8, LANE, stride=8), :]
            base = pl.multiple_of(g * (LANE * 8), LANE * 8)
            return src_flat[pl.ds(base + i - att_rows, LANE, stride=8), :]

        def keep(i, turned):
            for half in range(2):
                part = jnp.where(live[half], turned[half * obs : half * obs + obs], 0.0)
                table_ref[g * 2 + half, i] = part
                sums[half, i * 8 : i * 8 + 8, :] = fold_rows(part * rhs[half])

        total = att_rows + src_rows
        i = 0
        while i < total:
            if i % PERIOD == 0 and i + 1 < total:
                both = jnp.concatenate([rows_of(i), rows_of(i + 1)], axis=0)
                split = jnp.concatenate([part.astype(BF16) for part in split_three(both)], axis=1)
                turned = lax.dot_general(
                    same[...], split, (((1,), (1,)), ((), ())), preferred_element_type=F32
                )
                keep(i, turned[:, :LANE])
                keep(i + 1, turned[:, LANE:])
                i += 2
            else:
                keep(i, rows_of(i).T)
                i += 1
        for half in range(2):
            blocks[g * 2 + half] = row_sums(sums.at[half])
        return carry

    lax.fori_loop(0, groups, turn, 0)
    for half in range(2):
        fill_att(blocks, seg_ref, left, groups * 2 - 2 + half)
    scatter_att(att_ref, left, right)
    lane = lane_iota(16)
    att_ref[:, SEG_DEV:] = jnp.where(lane == 0, jnp.sum(square_ref[...]), 0.0)
    row = row_iota(8)
    send_sorted(
        narrow,
        blocks,
        order_ref,
        lambda t: jnp.where(row == 5, ids[t : t + 1, :], 0.0),
        send_ref,
    )


def owner_kernel(narrow, first, last, *refs):
    if first:
        recv_ref, part_ref, other_ref, src_ref, back_ref, half_ref, index_ref, right, left = refs
    elif last:
        recv_ref, index_ref, right, src_ref, left = refs
    else:
        recv_ref, part_ref, other_ref, index_ref, right = refs[:5]
        src_ref, back_ref, half_ref, known_ref, left = refs[5:]
    if not last:
        half_ref[...] = part_ref[...] + other_ref[...]
    tiles, cap = index_ref.shape[0], recv_ref.shape[2]
    per = cap // LANE
    levels = SRC_DEV // HIGH
    keep = row_iota(8) < 5
    if first:
        for t in range(tiles):
            index_ref[t : t + 1, :] = entry(recv_ref, per, t)[5:6].astype(I32)
        mark_high(right, index_ref[...])
    elif not last:
        known = recv_ref[0, :, 0:LANE]
        for n in range(1, narrow):
            known = known + recv_ref[n, :, 0:LANE]
        known_ref[...] = known
    for t in range(tiles):
        here = index_ref[t : t + 1, :]
        values = jnp.where(keep, entry(recv_ref, per, t), 0.0)
        spread_rows(left, values, here // HIGH, t * LANE, levels)
    sums = jnp.dot(left[...], right[...], preferred_element_type=F32)
    size = 8 * levels
    sums = sums[:size] + (sums[size : 2 * size] + sums[2 * size :])
    for level in range(levels):
        src_ref[:, level * HIGH : (level + 1) * HIGH] = sums[level * 8 : (level + 1) * 8]
    if last:
        return
    square = jnp.sum(src_ref[...] * src_ref[...]) if first else 0.0
    mark = jnp.where((row_iota(8) == 6) & (lane_iota(8) == 0), square, 0.0)
    for t in range(tiles):
        values = pick(
            lambda c: src_ref[:, c * LANE : (c + 1) * LANE],
            SRC_DEV // LANE,
            index_ref[t : t + 1, :],
        )
        values = jnp.where(keep, values, mark)
        back_ref[t // per, :, (t % per) * LANE : (t % per + 1) * LANE] = values


def lane_value(row, at):
    return jnp.sum(jnp.where(lane_iota(1) == at, row, 0.0), axis=1, keepdims=True)


def product_kernel(
    narrow, first, recv_ref, half_ref, later_ref, known_ref, pos_ref, seg_ref, order_ref, right,
    table_ref, full_ref, att_ref, sent_ref, scale_ref, vec, blocks, left, *own,
):
    send_ref = sent_ref if first else own[0]
    tiles, rows = pos_ref.shape[0], table_ref.shape[1]
    per = recv_ref.shape[2] // LANE
    full = half_ref[...] + later_ref[...]
    full_ref[...] = full[:, :SEG_DEV]
    notes = full[0:1, SEG_DEV:]
    lane, row = lane_iota(8), row_iota(8)
    send_note = jnp.zeros((8, LANE), F32)
    att_note = jnp.zeros((16, LANE), F32)
    if first:
        scale = jnp.ones((1, 1), F32)
        square_src = recv_ref[0, 6:7, 0:LANE]
        for n in range(1, narrow):
            square_src = square_src + recv_ref[n, 6:7, 0:LANE]
        att_note = jnp.where(lane_iota(16) == 1, lane_value(square_src, 0), 0.0)
        square_att = jnp.sum(full[:, :SEG_DEV] * full[:, :SEG_DEV], keepdims=True)
        send_note = jnp.where(lane == 0, lane_value(notes, 0), 0.0)
        send_note = jnp.where(lane == 1, square_att, send_note)
        send_note = jnp.where(row == 6, send_note, 0.0)
    else:
        known = known_ref[6:7, :]
        square = lane_value(notes, 1) + lane_value(known, 1)
        scale = lane_value(known, 0) / square
    scale_ref[...] = jnp.broadcast_to(scale, (8, LANE))
    att_ref[:, SEG_DEV:] = att_note

    def gather(t):
        where_att = seg_ref[pl.ds(t, 1), :]
        for top in range(0, 24, 8):
            if top < 16:
                picked = pick(
                    lambda c: full_ref[top : top + 8, c * LANE : (c + 1) * LANE],
                    SEG_DEV // LANE,
                    where_att,
                )
            else:
                picked = pick(lambda c: entry(recv_ref, per, c), tiles, pos_ref[pl.ds(t, 1), :])
            vec[t, top : top + 8, :] = picked if first else picked * scale

    def multiply(t, carry):
        fill_att(blocks, seg_ref, left, jnp.maximum(t - 1, 0))
        image = None
        for i in range(rows):
            part = table_ref[t, i] * vec[t, i : i + 1, :]
            image = part if image is None else image + part
        for i in range(rows):
            blocks[t, i : i + 1, :] = jnp.sum(table_ref[t, i] * image, axis=0, keepdims=True)
        blocks[t, rows:24, :] = jnp.zeros((24 - rows, LANE), F32)
        gather(jnp.minimum(t + 1, tiles - 1))
        return carry

    gather(0)
    lax.fori_loop(0, tiles, multiply, 0)
    send_sorted(narrow, blocks, order_ref, lambda t: send_note, send_ref)
    if not first:
        sending = pltpu.make_async_copy(send_ref, sent_ref, own[1])
        sending.start()
    fill_att(blocks, seg_ref, left, tiles - 1)
    scatter_att(att_ref, left, right)
    if not first:
        sending.wait()


def dots_kernel(
    src0, src1, src2, att0, att1, mine, later, square_ref, scale_ref, side_ref, out_ref, kept_ref
):
    kept_ref[...] = mine[...] + later[...]
    scale = scale_ref[0:1, 0:1]
    upper, weight = side_ref[0:1, 0:1] > 0.5, side_ref[1:2, 0:1]
    half = kept_ref.shape[1]

    def own_half(ref):
        return jnp.where(upper, ref[:, half:], ref[:, :half])

    src = (src0[...], src1[...] * scale, src2[...] * scale)
    att = (own_half(att0), own_half(att1) * scale, kept_ref[...] * scale)
    out = jnp.where(lane_iota(1) == 0, jnp.sum(square_ref[...], keepdims=True), 0.0)
    for at, (one, two) in enumerate(((0, 0), (0, 1), (1, 1), (1, 2), (2, 2))):
        total = jnp.sum(src[one] * src[two], keepdims=True)
        total = total + weight * jnp.sum(att[one] * att[two], keepdims=True)
        out = jnp.where(lane_iota(1) == at + 1, total, out)
    out_ref[...] = jnp.broadcast_to(out, out_ref.shape)


def finish_kernel(
    dots_ref, scale_ref, side_ref, src0, src1, src2, att0, att1, kept, other, rest,
    sol_src, sol_att, dir_src, dir_att, att2,
):
    upper = side_ref[0:1, 0:1] > 0.5
    half = kept.shape[1]
    dropped = other[...] + rest[...]
    att2[:, :half] = jnp.where(upper, dropped, kept[...])
    att2[:, half:] = jnp.where(upper, kept[...], dropped)
    sums = jnp.sum(dots_ref[...], axis=0, keepdims=True)
    rhs_square, m0, m1, m2, m3, m4 = [lane_value(sums, at) for at in range(6)]
    scale = scale_ref[0:1, 0:1]
    mean = m1 / m0
    ww = m2 - mean * m1
    wz = m3 - 2.0 * mean * m2 + mean * mean * m1
    zz = m4 - 2.0 * mean * m3 + mean * mean * m2
    root0, root1 = jnp.sqrt(m0), jnp.sqrt(ww)
    beta1 = jnp.sqrt(rhs_square)
    alpha1 = root0 / beta1
    beta2 = jnp.sqrt(mean / scale - alpha1 * alpha1)
    cross = root1 / (scale * root0)
    alpha2 = cross / beta2
    quotient = wz / ww / scale
    beta3 = jnp.sqrt(quotient - alpha2 * alpha2)
    third = zz / ww / (scale * scale) - quotient * quotient - cross * cross
    alpha3 = jnp.sqrt(third) / beta3
    phi_bar, rho_bar = beta1, alpha1
    steps, turns = [], []
    for beta, alpha in ((beta2, alpha2), (beta3, alpha3)):
        rho = jnp.sqrt(rho_bar * rho_bar + beta * beta)
        cosine, sine = rho_bar / rho, beta / rho
        theta = sine * alpha
        rho_bar = -cosine * alpha
        steps.append(cosine * phi_bar / rho)
        turns.append(theta / rho)
        phi_bar = sine * phi_bar
    sides = (
        (src0, src1, src2, sol_src, dir_src),
        (att0, att1, att2, sol_att, dir_att),
    )
    for zero, one, two, sol, direction in sides:
        rows = sol.shape[0]
        base, once, twice = zero[0:rows], one[0:rows] * scale, two[0:rows] * scale
        v1 = base / root0
        v2 = (once - mean * base) / root1
        v3 = ((twice - mean * once) / (scale * root1) - quotient * v2 - cross * v1) / (
            beta3 * alpha3
        )
        turned = v2 - turns[0] * v1
        sol[...] = steps[0] * v1 + steps[1] * turned
        direction[...] = v3 - turns[1] * turned


def sds(shape, dtype=F32):
    return jax.ShapeDtypeStruct(shape, dtype)


def in_hbm(values):
    return pltpu.with_memory_space_constraint(values, pltpu.HBM)


def call(kernel, outs, scratch=(), limit=8, **more):
    return pl.pallas_call(
        kernel,
        out_shape=outs,
        scratch_shapes=list(scratch),
        compiler_params=pltpu.CompilerParams(vmem_limit_bytes=limit * MIB),
        **more,
    )


def on_device(src_design, att_design, right_side, block_source, block_segment, block_count):
    narrow, wide = lax.axis_size("narrow"), lax.axis_size("wide")
    devices = narrow * wide
    blocks = block_source.shape[0]
    tiles = blocks // LANE
    cap = blocks // narrow
    src_rows, att_rows = src_design.shape[0], att_design.shape[0]
    rows = src_rows + att_rows
    columns = right_side.shape[0] // LANE
    groups = columns // LANE
    obs = right_side.shape[0] // blocks

    def across(values, step):
        return lax.ppermute(values, "wide", [(i, i ^ step) for i in range(wide)])

    def exchange(values):
        return lax.all_to_all(values, "narrow", 0, 0)

    def far_sums(total, end):
        later, jump = None, 2
        while jump < end:
            if later is not None:
                total = total + later
            later = across(total, jump)
            jump *= 2
        return total, later

    upper = lax.axis_index("wide") >= wide // 2

    tile_rows = lambda values: values.reshape(tiles, LANE)
    att_view = att_design.reshape(att_rows // 8, 8, columns, LANE).transpose(0, 2, 1, 3)
    src_view = src_design.reshape(src_rows, columns, LANE).transpose(1, 0, 2)

    right_shape = sds((blocks, HIGH), BF16)
    att_left = pltpu.VMEM((3 * 16 * SEG_DEV // HIGH, blocks), BF16)
    src_left = pltpu.VMEM((3 * 8 * SRC_DEV // HIGH, blocks), BF16)
    tile_int = sds((tiles, LANE), I32)
    send_shape = sds((narrow, 8, cap))
    att_shape = sds((16, SEG_DEV + LANE))
    src_shape = sds((8, SRC_DEV))
    table_shape = (tiles, rows, obs, LANE)
    table, square, pos, seg, order, att_right, part, send = call(
        functools.partial(start_kernel, narrow),
        (
            sds(table_shape),
            sds((8, LANE)),
            tile_int,
            tile_int,
            tile_int,
            right_shape,
            att_shape,
            send_shape,
        ),
        [
            pltpu.VMEM((groups, att_rows // 8, LANE, 8, LANE), F32),
            pltpu.VMEM((groups, LANE, 8, LANE), F32),
            pltpu.VMEM((groups, LANE, LANE), F32),
            pltpu.VMEM((tiles, LANE), I32),
            pltpu.VMEM((tiles, LANE), I32),
            pltpu.VMEM((tiles, LANE), I32),
            pltpu.VMEM((tiles, 24, LANE), F32),
            pltpu.VMEM((tiles, LANE), F32),
            pltpu.VMEM((2, 24 * 8, LANE), F32),
            pltpu.VMEM((LANE, 3 * LANE), BF16),
            att_left,
            pltpu.SemaphoreType.DMA((3, groups)),
            pltpu.SemaphoreType.DMA((3,)),
        ],
        in_specs=[pl.BlockSpec(memory_space=pltpu.HBM)] * 6,
        limit=20,
    )(
        *map(
            in_hbm,
            (
                att_view,
                src_view,
                right_side.reshape(columns, LANE),
                tile_rows(block_source),
                tile_rows(block_segment),
                tile_rows(block_count),
            ),
        )
    )

    results = []
    note = jnp.zeros((8, LANE), F32)
    owners = None
    for step in range(3):
        first_time, last_time = step == 0, step == 2
        other = across(part, 1)
        arrived = exchange(send)
        kernel = functools.partial(owner_kernel, narrow, first_time, last_time)
        if last_time:
            total, later = far_sums(part + other, wide // 2)
            if later is not None:
                total = total + later
            low, high = total[:, : SEG_DEV // 2], total[:, SEG_DEV // 2 : SEG_DEV]
            mine, other = jnp.where(upper, high, low), jnp.where(upper, low, high)
            later = across(other, wide // 2)
            rest = across(mine, wide // 2)
            src_sum = call(kernel, src_shape, [src_left])(arrived, *owners)
            results.append((src_sum, mine, later))
            break
        outs = (src_shape, send_shape, att_shape)
        if first_time:
            src_sum, back, half, *owners = call(
                kernel, outs + (tile_int, right_shape), [src_left]
            )(arrived, part, other)
        else:
            src_sum, back, half, note = call(kernel, outs + (sds((8, LANE)),), [src_left])(
                arrived, part, other, *owners
            )
        total, later = far_sums(half, wide)
        back = exchange(back)
        own, specs = [], {}
        if not first_time:
            in_vmem = pl.BlockSpec(memory_space=pltpu.VMEM)
            own = [pltpu.VMEM(send_shape.shape, F32), pltpu.SemaphoreType.DMA(())]
            specs = dict(
                out_specs=(in_vmem, in_vmem, pl.BlockSpec(memory_space=pltpu.HBM), in_vmem)
            )
        att_sum, part, send, scale = call(
            functools.partial(product_kernel, narrow, first_time),
            (
                sds((16, SEG_DEV)),
                att_shape,
                send_shape if first_time else pltpu.HBM(send_shape.shape, F32),
                sds((8, LANE)),
            ),
            [
                pltpu.VMEM((tiles, 24, LANE), F32),
                pltpu.VMEM((tiles, 24, LANE), F32),
                att_left,
            ]
            + own,
            **specs,
        )(back, total, later, note, pos, seg, order, att_right, table)
        results.append((src_sum, att_sum))
    counted = lax.axis_index("wide") % (wide // 2) == 0
    side = jnp.where(row_iota(8) == 0, upper, counted).astype(F32)
    (src0, att0), (src1, att1), (src2, mine, later) = results
    dots, kept = call(dots_kernel, (sds((devices, LANE)), sds((16, SEG_DEV // 2))))(
        src0, src1, src2, att0, att1, mine, later, square, scale, side
    )
    dots = lax.all_to_all(dots, ("wide", "narrow"), 0, 0, tiled=True)
    sol_src, sol_att, dir_src, dir_att = call(
        finish_kernel,
        (
            sds((src_rows, SRC_DEV)),
            sds((att_rows, SEG_DEV)),
            sds((src_rows, SRC_DEV)),
            sds((att_rows, SEG_DEV)),
        ),
        [pltpu.VMEM((16, SEG_DEV), F32)],
    )(dots, scale, side, src0, src1, src2, att0, att1, kept, other, rest)
    return (sol_src, sol_att, dir_src, dir_att)


def solution(mesh):
    both = ("wide", "narrow")
    in_specs = (P(None, both), P(None, both), P(both), P(both), P(both), P(both))
    out_specs = (P(None, both), P(None, "narrow"), P(None, both), P(None, "narrow"))

    return jax.shard_map(
        on_device, mesh=mesh, in_specs=in_specs, out_specs=out_specs, check_vma=False
    )
```

```python
import functools

import jax
import jax.numpy as jnp
from jax import lax
from jax.experimental import pallas as pl
from jax.experimental.pallas import tpu as pltpu
from jax.sharding import PartitionSpec as P


SRC_DEV = 2048
SEG_DEV = 1024
LANE = 128
HIGH = 256
F32 = jnp.float32
BF16 = jnp.bfloat16
I32 = jnp.int32
MIB = 1 << 20
PERIOD = 7


def lanes_of(values, index):
    return jnp.take_along_axis(values, index, axis=1, mode="promise_in_bounds")


def row_iota(rows, columns=LANE):
    return lax.broadcasted_iota(I32, (rows, columns), 0)


def lane_iota(rows, columns=LANE):
    return lax.broadcasted_iota(I32, (rows, columns), 1)


def to_tiles(rows):
    count = rows.shape[0]
    lane = lane_iota(count)
    first = lanes_of(rows, (2 * lane) % LANE)
    second = lanes_of(rows, (2 * lane + 1) % LANE)
    head = lane < LANE // 2
    even = jnp.where(head, first, pltpu.roll(first, count - 1, 0))
    odd = jnp.where(head, pltpu.roll(second, 1, 0), second)
    return jnp.where(row_iota(count) % 2 == 0, even, odd)


def split_three(values):
    top = values.astype(BF16).astype(F32)
    rest = values - top
    middle = rest.astype(BF16).astype(F32)
    return top, middle, rest - middle


def spread_rows(store, picked, row, column, levels):
    rows = picked.shape[0]
    size = levels * rows
    levels_at = (row_iota(size) // rows).astype(F32).astype(BF16)
    named = jnp.broadcast_to(row.astype(F32), (size, LANE)).astype(BF16)
    mask = jnp.where(levels_at == named, jnp.ones((), BF16), jnp.zeros((), BF16))
    for part, piece in enumerate(split_three(picked)):
        whole = jnp.concatenate([piece] * (16 // rows), axis=0).astype(BF16)
        whole = jnp.concatenate([whole] * (size // 16), axis=0)
        store[pl.ds(part * size, size), pl.ds(column, LANE)] = whole * mask


def fold_rows(values):
    total = values[0:8]
    for at in range(8, values.shape[0], 8):
        total = total + values[at : at + 8]
    return total


def row_sums(sums):
    rows = sums.shape[0] // 8
    total = sums[pl.ds(0, rows, stride=8), :]
    for at in range(1, 8):
        total = total + sums[pl.ds(at, rows, stride=8), :]
    return total


def rank_blocks(narrow, source_ref, segment_ref, pos_ref, seg_ref, order_ref, ids_ref, left, right):
    tiles = source_ref.shape[0]
    cap = tiles * LANE // narrow
    local = to_tiles(source_ref[...]) & (SRC_DEV * narrow - 1)
    seg_ref[...] = to_tiles(segment_ref[...]) & (SEG_DEV - 1)
    owner = local // SRC_DEV
    inner = local & (SRC_DEV - 1)
    marks = jnp.concatenate([jnp.where(owner == m, 1.0, 0.0) for m in range(narrow)], axis=0)
    marks = marks.astype(BF16)
    total = narrow * tiles
    before = jnp.where(row_iota(LANE) < lane_iota(LANE), 1.0, 0.0).astype(BF16)
    in_row = jnp.dot(marks, before, preferred_element_type=F32)
    at_row, at_lane = row_iota(total, total), lane_iota(total, total)
    earlier = (at_row // tiles == at_lane // tiles) & (at_lane < at_row)
    ahead = jnp.dot(jnp.where(earlier, 1.0, 0.0).astype(BF16), marks, preferred_element_type=F32)
    ahead = jnp.dot(ahead.astype(BF16), jnp.ones((LANE, LANE), BF16), preferred_element_type=F32)
    rank = (in_row + ahead).astype(I32)
    pos = jnp.zeros((tiles, LANE), I32)
    for m in range(narrow):
        pos = jnp.where(owner == m, m * cap + rank[m * tiles : (m + 1) * tiles], pos)
    pos_ref[...] = pos
    levels = tiles * LANE // HIGH
    lane = lane_iota(1).astype(F32)
    for t in range(tiles):
        here = pos[t : t + 1]
        level = row_iota(levels) == here // HIGH
        mine = inner[t : t + 1]
        pieces = (
            jnp.full((1, LANE), float(t), F32),
            lane,
            (mine // LANE).astype(F32),
            (mine % LANE).astype(F32),
        )
        for part, piece in enumerate(pieces):
            left[part * levels : (part + 1) * levels, t * LANE : (t + 1) * LANE] = jnp.where(
                level, piece, 0.0
            ).astype(BF16)
    mark_high(right, pos)
    found = jnp.dot(left[0 : 4 * levels, :], right[...], preferred_element_type=F32)
    tile_at, lane_at = found[:levels], found[levels : 2 * levels]
    order = (tile_at * LANE + lane_at).astype(I32)
    ids = found[2 * levels : 3 * levels] * LANE + found[3 * levels :]
    for level in range(levels):
        for half in range(HIGH // LANE):
            row = level * (HIGH // LANE) + half
            cut = slice(half * LANE, (half + 1) * LANE)
            order_ref[row : row + 1, :] = order[level : level + 1, cut]
            ids_ref[row : row + 1, :] = ids[level : level + 1, cut]


def mark_high(right, index):
    columns = (index & (HIGH - 1)).astype(F32).T
    high_at = lane_iota(LANE, HIGH).astype(F32).astype(BF16)
    one, zero = jnp.ones((), BF16), jnp.zeros((), BF16)
    for t in range(index.shape[0]):
        here = jnp.broadcast_to(columns[:, t : t + 1], (LANE, HIGH)).astype(BF16)
        right[t * LANE : (t + 1) * LANE, :] = jnp.where(high_at == here, one, zero)


def fill_att(blocks, seg_ref, left, t):
    here = seg_ref[pl.ds(t, 1), :]
    column = pl.multiple_of(t * LANE, LANE)
    spread_rows(left, blocks[t, 0:16, :], here // HIGH, column, SEG_DEV // HIGH)


def scatter_att(out_ref, left, right):
    levels = SEG_DEV // HIGH
    sums = jnp.dot(left[...], right[...], preferred_element_type=F32)
    size = 16 * levels
    sums = sums[:size] + (sums[size : 2 * size] + sums[2 * size :])
    for level in range(levels):
        out_ref[:, level * HIGH : (level + 1) * HIGH] = sums[level * 16 : (level + 1) * 16]


def pick(tables, count, index):
    low = index & (LANE - 1)
    high = index // LANE
    rows = tables(0).shape[0]
    low = jnp.broadcast_to(low, (rows, LANE))
    out = lanes_of(tables(0), low)
    for c in range(1, count):
        out = jnp.where(high == c, lanes_of(tables(c), low), out)
    return out


def send_sorted(narrow, blocks, order_ref, extra, out_ref):
    tiles = order_ref.shape[0]
    cap = tiles * LANE // narrow
    per = cap // LANE
    keep = row_iota(8) < 5
    for t in range(tiles):
        values = pick(lambda c: blocks[c, 16:24, :], tiles, order_ref[t : t + 1, :])
        values = jnp.where(keep, values, extra(t))
        out_ref[t // per, :, (t % per) * LANE : (t % per + 1) * LANE] = values


def entry(ref, per, t):
    return ref[t // per, :, (t % per) * LANE : (t % per + 1) * LANE]


def start_kernel(
    narrow,
    att_hbm, src_hbm, rhs_hbm, source_hbm, segment_hbm, count_hbm,
    table_ref, square_ref, pos_ref, seg_ref, order_ref, right, att_ref, send_ref,
    att_in, src_in, rhs_in, source_in, segment_in, count_in, blocks, ids, sums, same, left, sems, int_sems,
):
    groups, att_sets = att_in.shape[0], att_in.shape[1]
    att_rows, src_rows = att_sets * 8, src_hbm.shape[1]
    att_flat = att_in.reshape(groups * att_sets * LANE * 8, LANE)
    src_flat = src_in.reshape(groups * LANE * 8, LANE)
    obs = table_ref.shape[2]

    def ints():
        pairs = ((source_hbm, source_in), (segment_hbm, segment_in), (count_hbm, count_in))
        return [
            pltpu.make_async_copy(one, two, int_sems.at[at]) for at, (one, two) in enumerate(pairs)
        ]

    def loads(g):
        cut = pl.ds(g * LANE, LANE)
        return [
            pltpu.make_async_copy(att_hbm.at[:, cut], att_in.at[g], sems.at[0, g]),
            pltpu.make_async_copy(src_hbm.at[cut], src_in.at[g, :, 0:src_rows], sems.at[1, g]),
            pltpu.make_async_copy(rhs_hbm.at[cut], rhs_in.at[g], sems.at[2, g]),
        ]

    def begin(g, carry):
        for one in loads(g):
            one.start()
        return carry

    for one in ints():
        one.start()
    lax.fori_loop(0, groups, begin, 0)
    for one in ints():
        one.wait()
    count_in[...] = to_tiles(count_in[...])
    square_ref[...] = jnp.zeros_like(square_ref)
    sums[...] = jnp.zeros_like(sums)
    diagonal = jnp.where(row_iota(LANE) == lane_iota(LANE), 1.0, 0.0).astype(BF16)
    for part in range(3):
        same[:, part * LANE : (part + 1) * LANE] = diagonal
    rank_blocks(narrow, source_in, segment_in, pos_ref, seg_ref, order_ref, ids, left, right)
    mark_high(right, seg_ref[...])
    place = row_iota(obs)

    def turn(g, carry):
        for half in range(2):
            fill_att(blocks, seg_ref, left, jnp.maximum(g * 2 - 2 + half, half))
        for one in loads(g):
            one.wait()
        wide_rhs = rhs_in[g].T
        live, rhs = [], []
        for half in range(2):
            alive = place < count_in[pl.ds(g * 2 + half, 1), :]
            live.append(alive)
            part = jnp.where(alive, wide_rhs[half * obs : half * obs + obs], 0.0)
            rhs.append(part)
            square_ref[...] += fold_rows(part * part)

        def rows_of(i):
            if i < att_rows:
                base = pl.multiple_of((g * att_sets + i // 8) * (LANE * 8), LANE * 8)
                return att_flat[pl.ds(base + i % 8, LANE, stride=8), :]
            base = pl.multiple_of(g * (LANE * 8), LANE * 8)
            return src_flat[pl.ds(base + i - att_rows, LANE, stride=8), :]

        def keep(i, turned):
            for half in range(2):
                part = jnp.where(live[half], turned[half * obs : half * obs + obs], 0.0)
                table_ref[g * 2 + half, i] = part
                sums[half, i * 8 : i * 8 + 8, :] = fold_rows(part * rhs[half])

        total = att_rows + src_rows
        i = 0
        while i < total:
            if i % PERIOD == 0 and i + 1 < total:
                both = jnp.concatenate([rows_of(i), rows_of(i + 1)], axis=0)
                split = jnp.concatenate([part.astype(BF16) for part in split_three(both)], axis=1)
                turned = lax.dot_general(
                    same[...], split, (((1,), (1,)), ((), ())), preferred_element_type=F32
                )
                keep(i, turned[:, :LANE])
                keep(i + 1, turned[:, LANE:])
                i += 2
            else:
                keep(i, rows_of(i).T)
                i += 1
        for half in range(2):
            blocks[g * 2 + half] = row_sums(sums.at[half])
        return carry

    lax.fori_loop(0, groups, turn, 0)
    for half in range(2):
        fill_att(blocks, seg_ref, left, groups * 2 - 2 + half)
    scatter_att(att_ref, left, right)
    lane = lane_iota(16)
    att_ref[:, SEG_DEV:] = jnp.where(lane == 0, jnp.sum(square_ref[...]), 0.0)
    row = row_iota(8)
    send_sorted(
        narrow,
        blocks,
        order_ref,
        lambda t: jnp.where(row == 5, ids[t : t + 1, :], 0.0),
        send_ref,
    )


def owner_kernel(narrow, first, last, *refs):
    if first:
        recv_ref, part_ref, other_ref, src_ref, back_ref, half_ref, index_ref, right, left = refs
    elif last:
        recv_ref, index_ref, right, src_ref, left = refs
    else:
        recv_ref, part_ref, other_ref, index_ref, right = refs[:5]
        src_ref, back_ref, half_ref, known_ref, left = refs[5:]
    if not last:
        half_ref[...] = part_ref[...] + other_ref[...]
    tiles, cap = index_ref.shape[0], recv_ref.shape[2]
    per = cap // LANE
    levels = SRC_DEV // HIGH
    keep = row_iota(8) < 5
    if first:
        for t in range(tiles):
            index_ref[t : t + 1, :] = entry(recv_ref, per, t)[5:6].astype(I32)
        mark_high(right, index_ref[...])
    elif not last:
        known = recv_ref[0, :, 0:LANE]
        for n in range(1, narrow):
            known = known + recv_ref[n, :, 0:LANE]
        known_ref[...] = known
    for t in range(tiles):
        here = index_ref[t : t + 1, :]
        values = jnp.where(keep, entry(recv_ref, per, t), 0.0)
        spread_rows(left, values, here // HIGH, t * LANE, levels)
    sums = jnp.dot(left[...], right[...], preferred_element_type=F32)
    size = 8 * levels
    sums = sums[:size] + (sums[size : 2 * size] + sums[2 * size :])
    for level in range(levels):
        src_ref[:, level * HIGH : (level + 1) * HIGH] = sums[level * 8 : (level + 1) * 8]
    if last:
        return
    square = jnp.sum(src_ref[...] * src_ref[...]) if first else 0.0
    mark = jnp.where((row_iota(8) == 6) & (lane_iota(8) == 0), square, 0.0)
    for t in range(tiles):
        values = pick(
            lambda c: src_ref[:, c * LANE : (c + 1) * LANE],
            SRC_DEV // LANE,
            index_ref[t : t + 1, :],
        )
        values = jnp.where(keep, values, mark)
        back_ref[t // per, :, (t % per) * LANE : (t % per + 1) * LANE] = values


def lane_value(row, at):
    return jnp.sum(jnp.where(lane_iota(1) == at, row, 0.0), axis=1, keepdims=True)


def product_kernel(
    narrow, first, recv_ref, half_ref, later_ref, known_ref, pos_ref, seg_ref, order_ref, right,
    table_ref, full_ref, att_ref, sent_ref, scale_ref, vec, blocks, left, *own,
):
    send_ref = sent_ref if first else own[0]
    tiles, rows = pos_ref.shape[0], table_ref.shape[1]
    per = recv_ref.shape[2] // LANE
    full = half_ref[...] + later_ref[...]
    full_ref[...] = full[:, :SEG_DEV]
    notes = full[0:1, SEG_DEV:]
    lane, row = lane_iota(8), row_iota(8)
    send_note = jnp.zeros((8, LANE), F32)
    att_note = jnp.zeros((16, LANE), F32)
    if first:
        scale = jnp.ones((1, 1), F32)
        square_src = recv_ref[0, 6:7, 0:LANE]
        for n in range(1, narrow):
            square_src = square_src + recv_ref[n, 6:7, 0:LANE]
        att_note = jnp.where(lane_iota(16) == 1, lane_value(square_src, 0), 0.0)
        square_att = jnp.sum(full[:, :SEG_DEV] * full[:, :SEG_DEV], keepdims=True)
        send_note = jnp.where(lane == 0, lane_value(notes, 0), 0.0)
        send_note = jnp.where(lane == 1, square_att, send_note)
        send_note = jnp.where(row == 6, send_note, 0.0)
    else:
        known = known_ref[6:7, :]
        square = lane_value(notes, 1) + lane_value(known, 1)
        scale = lane_value(known, 0) / square
    scale_ref[...] = jnp.broadcast_to(scale, (8, LANE))
    att_ref[:, SEG_DEV:] = att_note

    def gather(t):
        where_att = seg_ref[pl.ds(t, 1), :]
        for top in range(0, 24, 8):
            if top < 16:
                picked = pick(
                    lambda c: full_ref[top : top + 8, c * LANE : (c + 1) * LANE],
                    SEG_DEV // LANE,
                    where_att,
                )
            else:
                picked = pick(lambda c: entry(recv_ref, per, c), tiles, pos_ref[pl.ds(t, 1), :])
            vec[t, top : top + 8, :] = picked if first else picked * scale

    def multiply(t, carry):
        fill_att(blocks, seg_ref, left, jnp.maximum(t - 1, 0))
        image = None
        for i in range(rows):
            part = table_ref[t, i] * vec[t, i : i + 1, :]
            image = part if image is None else image + part
        for i in range(rows):
            blocks[t, i : i + 1, :] = jnp.sum(table_ref[t, i] * image, axis=0, keepdims=True)
        blocks[t, rows:24, :] = jnp.zeros((24 - rows, LANE), F32)
        gather(jnp.minimum(t + 1, tiles - 1))
        return carry

    gather(0)
    lax.fori_loop(0, tiles, multiply, 0, unroll=4)
    send_sorted(narrow, blocks, order_ref, lambda t: send_note, send_ref)
    if not first:
        sending = pltpu.make_async_copy(send_ref, sent_ref, own[1])
        sending.start()
    fill_att(blocks, seg_ref, left, tiles - 1)
    scatter_att(att_ref, left, right)
    if not first:
        sending.wait()


def dots_kernel(
    src0, src1, src2, att0, att1, mine, later, square_ref, scale_ref, side_ref, out_ref, kept_ref
):
    kept_ref[...] = mine[...] + later[...]
    scale = scale_ref[0:1, 0:1]
    upper, weight = side_ref[0:1, 0:1] > 0.5, side_ref[1:2, 0:1]
    half = kept_ref.shape[1]

    def own_half(ref):
        return jnp.where(upper, ref[:, half:], ref[:, :half])

    src = (src0[...], src1[...] * scale, src2[...] * scale)
    att = (own_half(att0), own_half(att1) * scale, kept_ref[...] * scale)
    out = jnp.where(lane_iota(1) == 0, jnp.sum(square_ref[...], keepdims=True), 0.0)
    for at, (one, two) in enumerate(((0, 0), (0, 1), (1, 1), (1, 2), (2, 2))):
        total = jnp.sum(src[one] * src[two], keepdims=True)
        total = total + weight * jnp.sum(att[one] * att[two], keepdims=True)
        out = jnp.where(lane_iota(1) == at + 1, total, out)
    out_ref[...] = jnp.broadcast_to(out, out_ref.shape)


def finish_kernel(
    dots_ref, scale_ref, side_ref, src0, src1, src2, att0, att1, kept, back,
    sol_src, sol_att, dir_src, dir_att, att2,
):
    upper = side_ref[0:1, 0:1] > 0.5
    half = kept.shape[1]
    att2[:, :half] = jnp.where(upper, back[...], kept[...])
    att2[:, half:] = jnp.where(upper, kept[...], back[...])
    sums = jnp.sum(dots_ref[...], axis=0, keepdims=True)
    rhs_square, m0, m1, m2, m3, m4 = [lane_value(sums, at) for at in range(6)]
    scale = scale_ref[0:1, 0:1]
    mean = m1 / m0
    ww = m2 - mean * m1
    wz = m3 - 2.0 * mean * m2 + mean * mean * m1
    zz = m4 - 2.0 * mean * m3 + mean * mean * m2
    root0, root1 = jnp.sqrt(m0), jnp.sqrt(ww)
    beta1 = jnp.sqrt(rhs_square)
    alpha1 = root0 / beta1
    beta2 = jnp.sqrt(mean / scale - alpha1 * alpha1)
    cross = root1 / (scale * root0)
    alpha2 = cross / beta2
    quotient = wz / ww / scale
    beta3 = jnp.sqrt(quotient - alpha2 * alpha2)
    third = zz / ww / (scale * scale) - quotient * quotient - cross * cross
    alpha3 = jnp.sqrt(third) / beta3
    phi_bar, rho_bar = beta1, alpha1
    steps, turns = [], []
    for beta, alpha in ((beta2, alpha2), (beta3, alpha3)):
        rho = jnp.sqrt(rho_bar * rho_bar + beta * beta)
        cosine, sine = rho_bar / rho, beta / rho
        theta = sine * alpha
        rho_bar = -cosine * alpha
        steps.append(cosine * phi_bar / rho)
        turns.append(theta / rho)
        phi_bar = sine * phi_bar
    sides = (
        (src0, src1, src2, sol_src, dir_src),
        (att0, att1, att2, sol_att, dir_att),
    )
    for zero, one, two, sol, direction in sides:
        rows = sol.shape[0]
        base, once, twice = zero[0:rows], one[0:rows] * scale, two[0:rows] * scale
        v1 = base / root0
        v2 = (once - mean * base) / root1
        v3 = ((twice - mean * once) / (scale * root1) - quotient * v2 - cross * v1) / (
            beta3 * alpha3
        )
        turned = v2 - turns[0] * v1
        sol[...] = steps[0] * v1 + steps[1] * turned
        direction[...] = v3 - turns[1] * turned


def sds(shape, dtype=F32):
    return jax.ShapeDtypeStruct(shape, dtype)


def in_hbm(values):
    return pltpu.with_memory_space_constraint(values, pltpu.HBM)


def call(kernel, outs, scratch=(), limit=8, **more):
    return pl.pallas_call(
        kernel,
        out_shape=outs,
        scratch_shapes=list(scratch),
        compiler_params=pltpu.CompilerParams(vmem_limit_bytes=limit * MIB),
        **more,
    )


def on_device(src_design, att_design, right_side, block_source, block_segment, block_count):
    narrow, wide = lax.axis_size("narrow"), lax.axis_size("wide")
    devices = narrow * wide
    blocks = block_source.shape[0]
    tiles = blocks // LANE
    cap = blocks // narrow
    src_rows, att_rows = src_design.shape[0], att_design.shape[0]
    rows = src_rows + att_rows
    columns = right_side.shape[0] // LANE
    groups = columns // LANE
    obs = right_side.shape[0] // blocks

    def across(values, step):
        return lax.ppermute(values, "wide", [(i, i ^ step) for i in range(wide)])

    def exchange(values):
        return lax.all_to_all(values, "narrow", 0, 0)

    def far_sums(total, end):
        later, jump = None, 2
        while jump < end:
            if later is not None:
                total = total + later
            later = across(total, jump)
            jump *= 2
        return total, later

    upper = lax.axis_index("wide") >= wide // 2

    tile_rows = lambda values: values.reshape(tiles, LANE)
    att_view = att_design.reshape(att_rows // 8, 8, columns, LANE).transpose(0, 2, 1, 3)
    src_view = src_design.reshape(src_rows, columns, LANE).transpose(1, 0, 2)

    right_shape = sds((blocks, HIGH), BF16)
    att_left = pltpu.VMEM((3 * 16 * SEG_DEV // HIGH, blocks), BF16)
    src_left = pltpu.VMEM((3 * 8 * SRC_DEV // HIGH, blocks), BF16)
    tile_int = sds((tiles, LANE), I32)
    send_shape = sds((narrow, 8, cap))
    att_shape = sds((16, SEG_DEV + LANE))
    src_shape = sds((8, SRC_DEV))
    table_shape = (tiles, rows, obs, LANE)
    table, square, pos, seg, order, att_right, part, send = call(
        functools.partial(start_kernel, narrow),
        (
            sds(table_shape),
            sds((8, LANE)),
            tile_int,
            tile_int,
            tile_int,
            right_shape,
            att_shape,
            send_shape,
        ),
        [
            pltpu.VMEM((groups, att_rows // 8, LANE, 8, LANE), F32),
            pltpu.VMEM((groups, LANE, 8, LANE), F32),
            pltpu.VMEM((groups, LANE, LANE), F32),
            pltpu.VMEM((tiles, LANE), I32),
            pltpu.VMEM((tiles, LANE), I32),
            pltpu.VMEM((tiles, LANE), I32),
            pltpu.VMEM((tiles, 24, LANE), F32),
            pltpu.VMEM((tiles, LANE), F32),
            pltpu.VMEM((2, 24 * 8, LANE), F32),
            pltpu.VMEM((LANE, 3 * LANE), BF16),
            att_left,
            pltpu.SemaphoreType.DMA((3, groups)),
            pltpu.SemaphoreType.DMA((3,)),
        ],
        in_specs=[pl.BlockSpec(memory_space=pltpu.HBM)] * 6,
        limit=20,
    )(
        *map(
            in_hbm,
            (
                att_view,
                src_view,
                right_side.reshape(columns, LANE),
                tile_rows(block_source),
                tile_rows(block_segment),
                tile_rows(block_count),
            ),
        )
    )

    results = []
    note = jnp.zeros((8, LANE), F32)
    owners = None
    for step in range(3):
        first_time, last_time = step == 0, step == 2
        other = across(part, 1)
        arrived = exchange(send)
        kernel = functools.partial(owner_kernel, narrow, first_time, last_time)
        if last_time:
            total, later = far_sums(part + other, wide // 2)
            if later is not None:
                total = total + later
            low, high = total[:, : SEG_DEV // 2], total[:, SEG_DEV // 2 : SEG_DEV]
            mine, other = jnp.where(upper, high, low), jnp.where(upper, low, high)
            later = across(other, wide // 2)
            src_sum = call(kernel, src_shape, [src_left])(arrived, *owners)
            results.append((src_sum, mine, later))
            break
        outs = (src_shape, send_shape, att_shape)
        if first_time:
            src_sum, back, half, *owners = call(
                kernel, outs + (tile_int, right_shape), [src_left]
            )(arrived, part, other)
        else:
            src_sum, back, half, note = call(kernel, outs + (sds((8, LANE)),), [src_left])(
                arrived, part, other, *owners
            )
        total, later = far_sums(half, wide)
        back = exchange(back)
        own, specs = [], {}
        if not first_time:
            in_vmem = pl.BlockSpec(memory_space=pltpu.VMEM)
            own = [pltpu.VMEM(send_shape.shape, F32), pltpu.SemaphoreType.DMA(())]
            specs = dict(
                out_specs=(in_vmem, in_vmem, pl.BlockSpec(memory_space=pltpu.HBM), in_vmem)
            )
        att_sum, part, send, scale = call(
            functools.partial(product_kernel, narrow, first_time),
            (
                sds((16, SEG_DEV)),
                att_shape,
                send_shape if first_time else pltpu.HBM(send_shape.shape, F32),
                sds((8, LANE)),
            ),
            [
                pltpu.VMEM((tiles, 24, LANE), F32),
                pltpu.VMEM((tiles, 24, LANE), F32),
                att_left,
            ]
            + own,
            **specs,
        )(back, total, later, note, pos, seg, order, att_right, table)
        results.append((src_sum, att_sum))
    counted = lax.axis_index("wide") % (wide // 2) == 0
    side = jnp.where(row_iota(8) == 0, upper, counted).astype(F32)
    (src0, att0), (src1, att1), (src2, mine, later) = results
    dots, kept = call(dots_kernel, (sds((devices, LANE)), sds((16, SEG_DEV // 2))))(
        src0, src1, src2, att0, att1, mine, later, square, scale, side
    )
    dots = lax.all_to_all(dots, ("wide", "narrow"), 0, 0, tiled=True)
    back = across(kept, wide // 2)
    sol_src, sol_att, dir_src, dir_att = call(
        finish_kernel,
        (
            sds((src_rows, SRC_DEV)),
            sds((att_rows, SEG_DEV)),
            sds((src_rows, SRC_DEV)),
            sds((att_rows, SEG_DEV)),
        ),
        [pltpu.VMEM((16, SEG_DEV), F32)],
    )(dots, scale, side, src0, src1, src2, att0, att1, kept, back)
    return (sol_src, sol_att, dir_src, dir_att)


def solution(mesh):
    both = ("wide", "narrow")
    in_specs = (P(None, both), P(None, both), P(both), P(both), P(both), P(both))
    out_specs = (P(None, both), P(None, "narrow"), P(None, both), P(None, "narrow"))

    return jax.shard_map(
        on_device, mesh=mesh, in_specs=in_specs, out_specs=out_specs, check_vma=False
    )
```
